32 devices in a mesh: pts: 8 (over z, x), nbr: 4 (over y, core).
Axes of the slice: x: 2, y: 2, z: 4, core: 2. Of those that a mesh axis runs over, the one named last changes fastest.
Arguments:
- points: bfloat16 [8, 4, 4096, 128], P('pts', 'nbr'), may hold values from -6 to 6
- dest_owner: int32 [8, 4, 4096, 1], P('pts', 'nbr'), may hold values from 0 to 31; in each aligned block of 4096 rows (0 to 4095, 4096 to 8191, ..., all dimensions but the last counted through in order) at most 256 rows name the same one
- dest_cell: int32 [8, 4, 4096], P('pts', 'nbr'), may hold values from 0 to 8191
- level_input: bfloat16 [64, 256, 16, 128], P('nbr', 'pts'), may hold values from -6 to 6
- w_res: bfloat16 [27, 128, 128], replicated, may hold values from -0.109375 to 0.109375
- w_down: bfloat16 [27, 128, 256], replicated, may hold values from -0.109375 to 0.109375
Outputs:
- lowered: bfloat16 [32, 128, 8, 256], P('nbr', 'pts')
The draws below stay inside these ranges and needn't reach their ends.
Inputs may be any that keep to these rules, and one draw needn't show every extreme that they name: `dest_owner`: at most 256 points of one device go to one owner, and some device sends exactly 256 points to some owner.
All inputs are finite; a program needn't handle non-finite values.
Results may differ from the reference program's by a relative error of at most 0.0048.
Values may be sent and summed in bfloat16 or wider, within the bound.
No kernel may reach another device: no remote copies, remote signals or barrier semaphores. Data moves between devices by JAX's collectives and lax.ppermute only.
A program may use at most 64 MiB of HBM per device.

```python
import math
import jax
import jax.numpy as jnp
import numpy as np
from jax import lax

C = 128
C_OUT = 256
BRICK = 16
BX = 1
BY = 2
P_DEV = 4096
CAP = 256
XG = 64
YG = 256
N_PTS = 8
N_NBR = 4
DEVICES = 32


def place_ends(result, rng, low, top_value):
    index_at = [jax.random.randint(jax.random.fold_in(rng, axis), (), 0, length) for axis, length in enumerate(result.shape)]
    longest = result.shape.index(max(result.shape))
    next_to = index_at[:longest] + [(index_at[longest] + 1) % result.shape[longest]] + index_at[longest + 1:]
    return result.at[tuple(index_at)].set(low).at[tuple(next_to)].set(top_value)


def steps_of(key, shape, pieces, smallest, high):
    loudness, own = 1.0, jax.random.fold_in(key, 6)
    for axis_at, parts in pieces:
        heights = jnp.exp(jax.random.uniform(jax.random.fold_in(own, axis_at), (parts,), jnp.float32, smallest / len(pieces), high / len(pieces)))
        loudness = loudness * jnp.repeat(heights, shape[axis_at] // parts).reshape([-1 if axis == axis_at else 1 for axis in range(len(shape))])
    return loudness


def routed_block(key, own, number, rows, number_of, top, reach, slope):
    sequence = jax.random.permutation(key, number_of)
    packed, common = portions_of(number_of, rows * top, reach, slope, True), portions_of(number_of, rows * top, reach, slope, False)
    places = jnp.arange(number_of)

    def named(tallies, rotation):
        used = int((tallies > 0).sum())
        fixed = max(1, used // 4)
        moved = fixed + (places - fixed + rotation * (used - fixed)) % max(1, number_of - fixed)
        return jnp.zeros((number_of,), jnp.int32).at[sequence[jnp.where(places < fixed, places, moved)]].set(jnp.asarray(tallies, jnp.int32))

    tallies = jnp.where(number % 4 == 0, named(packed, number // 4), named(common, number - number // 4 - 1))
    mixed = jax.random.permutation(jax.random.fold_in(own, 3), number_of)
    source_of, taker = mixed[0:number_of // 2 * 2:2], mixed[1:number_of // 2 * 2:2]
    margin = jnp.minimum(tallies[source_of] - 1, reach - tallies[taker]) // 2
    margin = jnp.where((source_of == sequence[0]) | (taker == sequence[0]) | (tallies[taker] == 0), 0, jnp.maximum(margin, 0))
    moved = jax.random.randint(jax.random.fold_in(own, 4), (number_of // 2,), 0, 1 << 20) % (margin + 1)
    tallies = tallies.at[source_of].add(-moved).at[taker].add(moved)
    members = jnp.searchsorted(jnp.cumsum(tallies), jnp.arange(rows * top), side="right").astype(jnp.int32)
    table = members.reshape(top, rows).T
    table = table[jax.random.permutation(jax.random.fold_in(own, 1), rows)]
    rotation = jax.random.randint(jax.random.fold_in(own, 2), (rows, 1), 0, top)
    return jnp.take_along_axis(table, (jnp.arange(top)[None, :] + rotation) % top, axis=1)


def portions_of(number_of, total, reach, lean, full):
    portions = [(1 << 20) // math.isqrt(rank ** lean) + 1 for rank in range(1, number_of + 1)]
    largest = reach if full else min(reach, max(-(-total // number_of), total * portions[0] // sum(portions)))
    least = 1 if total - largest >= number_of - 1 else 0
    holding, spare = [largest] + [least] * (number_of - 1), total - largest - least * (number_of - 1)
    while spare > 0:
        free = [i for i in range(1, number_of) if holding[i] < largest] or [i for i in range(1, number_of) if holding[i] < reach]
        pool, left = sum([portions[i] for i in free]), spare
        for i in free:
            more = min(reach - holding[i], max(1, left * portions[i] // pool), spare)
            holding[i] = holding[i] + more
            spare = spare - more
    return np.array(holding)


def centred(rng, dims, spread, reach, cuts=(), kind=jnp.bfloat16):
    entries = spread * jax.random.normal(rng, dims, jnp.float32)
    if cuts:
        entries = entries * steps_of(rng, dims, cuts, -0.22, 0.18)
    return jnp.clip(entries, -reach, reach).astype(kind)


def setup_inputs(seed: int = 0) -> dict:
    streams_of = jax.random.split(jax.random.key(seed), 7)
    points = centred(streams_of[0], (N_PTS, N_NBR, P_DEV, C), 1.0, 6.0, ((0, 8), (1, 4)))
    dest_owner_keys = jax.random.split(jax.random.fold_in(streams_of[1], 1), N_PTS * N_NBR * P_DEV // P_DEV)
    dest_owner_turns = jax.random.permutation(jax.random.fold_in(streams_of[1], 3), N_PTS * N_NBR * P_DEV // P_DEV)
    dest_owner = jax.vmap(lambda own, number: routed_block(jax.random.fold_in(streams_of[1], 2), own, number, P_DEV, DEVICES, 1, CAP, 2))(dest_owner_keys, dest_owner_turns).reshape((N_PTS, N_NBR, P_DEV, 1))
    dest_cell = place_ends(jax.random.randint(streams_of[2], (N_PTS, N_NBR, P_DEV), 0, BX * BY * BRICK**3), jax.random.fold_in(streams_of[2], 1), 0, (BX * BY * BRICK**3) - 1).astype(jnp.int32)
    level_input = centred(streams_of[3], (XG, YG, BRICK, C), 1.0, 6.0, ((0, 4), (1, 8)))
    w_res = centred(streams_of[4], (27, C, C), (27 * C) ** -0.5, 0.109375)
    w_down = centred(streams_of[5], (27, C, C_OUT), (27 * C) ** -0.5, 0.109375)
    return dict(points=points, dest_owner=dest_owner, dest_cell=dest_cell, level_input=level_input, w_res=w_res, w_down=w_down)


def convolve(source, kernel, stride):
    return lax.conv_general_dilated(source[None], kernel, (stride, stride, stride), ((1, 1), (1, 1), (1, 1)), dimension_numbers=("NDHWC", "DHWIO", "NDHWC"), precision=lax.Precision.HIGHEST)[0]


def reference(points, dest_owner, dest_cell, level_input, w_res, w_down):
    channels = points.shape[-1]
    span_x = BX * BRICK
    span_y = BY * BRICK
    feats = points.reshape(-1, channels).astype(jnp.float32)
    owner = dest_owner.reshape(-1).astype(jnp.int32)
    cell = dest_cell.reshape(-1).astype(jnp.int32)
    cell_x = cell // (span_y * BRICK)
    cell_y = (cell // BRICK) % span_y
    cell_z = cell % BRICK
    glob_x = (owner % N_NBR) * span_x + cell_x
    glob_y = (owner // N_NBR) * span_y + cell_y
    index = ((glob_x * (span_y * N_PTS) + glob_y) * BRICK + cell_z).astype(jnp.int32)
    grid = jnp.zeros((span_x * N_NBR * span_y * N_PTS * BRICK, channels), jnp.float32).at[index].add(feats)
    level = level_input.astype(jnp.float32)
    kernel = w_res.astype(jnp.float32).reshape(3, 3, 3, channels, channels)
    residual = convolve(level, kernel, 1)
    joined = (level + jnp.maximum(residual, 0.0) + grid.reshape(level.shape)).astype(jnp.bfloat16)
    joined = lax.optimization_barrier(joined).astype(jnp.float32)
    down_kernel = w_down.astype(jnp.float32).reshape(3, 3, 3, channels, w_down.shape[-1])
    lowered = convolve(joined, down_kernel, 2)
    return lowered.astype(jnp.bfloat16)
```

```python
import functools
import jax
import jax.numpy as jnp
from jax import lax
from jax.experimental import pallas as pl
from jax.experimental.pallas import tpu as pltpu
from jax.sharding import PartitionSpec as P

LANES = 128
EXTRA = 8


def pack_kernel(devices, cap, owner_ref, cell_ref, rows_ref, out_ref,
                wide, spread, slot_vmem, slot_smem, sem):
    p_local, channels = rows_ref.shape
    blocks = p_local // LANES
    stride = cap + EXTRA
    upper = (lax.broadcasted_iota(jnp.int32, (LANES, LANES), 0)
             <= lax.broadcasted_iota(jnp.int32, (LANES, LANES), 1)).astype(jnp.bfloat16)
    ids = lax.broadcasted_iota(jnp.int32, (devices, LANES), 0)
    spots = lax.broadcasted_iota(jnp.int32, (cap, LANES), 0)
    base = jnp.zeros((devices, 1), jnp.float32)
    table = jnp.zeros((2 * devices, cap), jnp.float32)
    for b in range(blocks):
        own = owner_ref[b:b + 1, :]
        cell = cell_ref[b:b + 1, :]
        hit = ids == own
        hot = hit.astype(jnp.float32)
        run = jnp.dot(hot.astype(jnp.bfloat16), upper, preferred_element_type=jnp.float32)
        place = jnp.sum(hot * (run + base), axis=0, keepdims=True).astype(jnp.int32) - 1
        base = base + run[:, LANES - 1:LANES]
        slot_vmem[b:b + 1, :] = own * stride + place
        high = jnp.where(hit, (cell // LANES + 1).astype(jnp.float32), 0.0)
        low = jnp.where(hit, (cell % LANES).astype(jnp.float32), 0.0)
        left = jnp.concatenate([high, low], axis=0).astype(jnp.bfloat16)
        right = (spots == place).astype(jnp.float32).astype(jnp.bfloat16)
        table = table + lax.dot_general(left, right, (((1,), (1,)), ((), ())),
                                        preferred_element_type=jnp.float32)
    copy = pltpu.make_async_copy(slot_vmem, slot_smem, sem)
    copy.start()
    wide[...] = rows_ref[...].astype(jnp.float32)
    per = -(-cap // LANES)
    for part in range(2):
        for j in range(per):
            width = min(LANES, cap - j * LANES)
            piece = table[part * devices:(part + 1) * devices, j * LANES:j * LANES + width]
            if width < LANES:
                piece = jnp.concatenate(
                    [piece, jnp.zeros((devices, LANES - width), jnp.float32)], axis=1)
            spread[pl.ds(cap + part * per + j, devices, stride=stride), :] = piece
    copy.wait()

    def step(b, carry):
        for u in range(LANES):
            spread[pl.ds(slot_smem[b, u], 1), :] = wide[pl.ds(b * LANES + u, 1), :]
        return carry

    lax.fori_loop(0, blocks, step, 0)
    out_ref[...] = spread[...].astype(jnp.bfloat16)


def pack(owner, cell, rows, devices, cap):
    p_local, channels = rows.shape
    blocks = p_local // LANES
    total = devices * (cap + EXTRA)
    vm = pl.BlockSpec(memory_space=pltpu.VMEM)
    return pl.pallas_call(
        functools.partial(pack_kernel, devices, cap),
        out_shape=jax.ShapeDtypeStruct((total, channels), jnp.bfloat16),
        in_specs=[vm, vm, vm],
        out_specs=vm,
        scratch_shapes=[
            pltpu.VMEM((p_local, channels), jnp.float32),
            pltpu.VMEM((total, channels), jnp.float32),
            pltpu.VMEM((blocks, LANES), jnp.int32),
            pltpu.SMEM((blocks, LANES), jnp.int32),
            pltpu.SemaphoreType.DMA,
        ],
        name="pack",
        cost_estimate=pl.CostEstimate(flops=10**8, bytes_accessed=4 * 10**6, transcendentals=0),
    )(owner.reshape(blocks, LANES), cell.reshape(blocks, LANES), rows)


WAYS = 4


def add_kernel(devices, cap, cells, got_ref, base_hbm, out_ref, wide, slot_vmem, slot_smem,
               sem, sem2, *sums):
    channels = got_ref.shape[-1]
    stride = cap + EXTRA
    per = -(-cap // LANES)
    first = pltpu.make_async_copy(base_hbm, sums[0].at[pl.ds(0, cells)], sem2)
    first.start()
    wide[...] = got_ref[...].astype(jnp.float32)
    for j in range(per):
        width = min(LANES, cap - j * LANES)
        high = wide[pl.ds(cap + j, devices, stride=stride), :].astype(jnp.int32)
        low = wide[pl.ds(cap + per + j, devices, stride=stride), :].astype(jnp.int32)
        spot = jnp.where(high > 0, (high - 1) * LANES + low, cells)
        slot_vmem[:, j * LANES:j * LANES + width] = spot[:, :width]
    copy = pltpu.make_async_copy(slot_vmem, slot_smem, sem)
    copy.start()
    for s in sums[1:]:
        s[...] = jnp.zeros_like(s)
    copy.wait()
    first.wait()

    def step(o, carry):
        def inner(q, carry):
            for u in range(32):
                at = slot_smem[o, q * 32 + u]
                s = sums[u % len(sums)]
                s[pl.ds(at, 1), :] += wide[pl.ds(o * stride + q * 32 + u, 1), :]
            return carry
        return lax.fori_loop(0, cap // 32, inner, carry)

    lax.fori_loop(0, devices, step, 0)
    total = sums[0][pl.ds(0, cells), :]
    for s in sums[1:]:
        total = total + s[pl.ds(0, cells), :]
    out_ref[...] = total.astype(jnp.bfloat16)


def add_rows(got, base, devices, cap):
    cells, channels = base.shape
    vm = pl.BlockSpec(memory_space=pltpu.VMEM)
    total = devices * (cap + EXTRA)
    return pl.pallas_call(
        functools.partial(add_kernel, devices, cap, cells),
        out_shape=jax.ShapeDtypeStruct((cells, channels), jnp.bfloat16),
        in_specs=[vm, pl.BlockSpec(memory_space=pl.ANY)],
        out_specs=vm,
        scratch_shapes=[
            pltpu.VMEM((total, channels), jnp.float32),
            pltpu.VMEM((devices, cap), jnp.int32),
            pltpu.SMEM((devices, cap), jnp.int32),
            pltpu.SemaphoreType.DMA,
            pltpu.SemaphoreType.DMA,
        ] + [pltpu.VMEM((cells + 8, channels), jnp.float32)] * WAYS,
        name="add_rows",
        cost_estimate=pl.CostEstimate(flops=10**8, bytes_accessed=8 * 10**6, transcendentals=0),
    )(got, base)

def extended_2(block, sides, width):
    for axis, dim in sides:
        count = lax.axis_size(axis)
        forward = [(i, i + 1) for i in range(count - 1)]
        backward = [(target, source) for source, target in forward]
        low = lax.ppermute(
            lax.slice_in_dim(block, block.shape[dim] - width, None, axis=dim), axis, forward
        )
        high = lax.ppermute(lax.slice_in_dim(block, 0, width, axis=dim), axis, backward)
        block = jnp.concatenate([low, block, high], axis=dim)
    return block


def passed_along(array, axis, by):
    count = lax.axis_size(axis)
    pairs = [(i, i + by) for i in range(count) if 0 <= i + by < count]
    return lax.ppermute(array, axis, pairs)


def conv_valid(source, kernel, stride):
    return lax.conv_general_dilated(
        source[None],
        kernel,
        (stride, stride, stride),
        "VALID",
        dimension_numbers=("NDHWC", "DHWIO", "NDHWC"),
        preferred_element_type=jnp.float32,
    )[0]


def body(points, dest_owner, dest_cell, level_input, w_res, w_down):
    devices = lax.axis_size("pts") * lax.axis_size("nbr")
    channels = points.shape[-1]
    rows = points.reshape(-1, channels)
    capacity = 2 * rows.shape[0] // devices
    outgoing = pack(dest_owner.reshape(-1), dest_cell.reshape(-1), rows, devices, capacity)
    got = lax.all_to_all(
        outgoing.reshape(devices, capacity + EXTRA, channels),
        ("pts", "nbr"),
        split_axis=0,
        concat_axis=0,
        tiled=True,
    ).reshape(outgoing.shape)
    span_x, span_y, span_z = level_input.shape[:3]
    cells = span_x * span_y * span_z
    padded = extended_2(level_input, (("pts", 1), ("nbr", 0)), 1)
    padded = jnp.pad(padded, ((0, 0), (0, 0), (1, 1), (0, 0)))
    kernel = w_res.reshape(3, 3, 3, channels, channels)
    residual = conv_valid(padded, kernel, 1).reshape(cells, channels)
    base = level_input.reshape(cells, channels).astype(jnp.float32) + jnp.maximum(residual, 0.0)
    joined = add_rows(got, base, devices, capacity)
    joined = joined.reshape(span_x, span_y, span_z, channels)
    front = passed_along(joined[-1:], "nbr", 1)
    extended = jnp.concatenate([front, joined], axis=0)
    side = passed_along(extended[:, -1:], "pts", 1)
    extended = jnp.concatenate([side, extended], axis=1)
    extended = jnp.pad(extended, ((0, 0), (0, 0), (1, 0), (0, 0)))
    down_kernel = w_down.reshape(3, 3, 3, channels, w_down.shape[-1])
    lowered = conv_valid(extended, down_kernel, 2)
    return lowered.astype(jnp.bfloat16)


def solution(mesh):
    return jax.shard_map(
        body,
        mesh=mesh,
        in_specs=(
            P("pts", "nbr", None, None),
            P("pts", "nbr", None, None),
            P("pts", "nbr", None),
            P("nbr", "pts", None, None),
            P(),
            P(),
        ),
        out_specs=P("nbr", "pts", None, None),
        check_vma=False,
    )
```

```python
import functools
import jax
import jax.numpy as jnp
from jax import lax
from jax.experimental import pallas as pl
from jax.experimental.pallas import tpu as pltpu
from jax.sharding import PartitionSpec as P

LANES = 128
EXTRA = 8


def pack_kernel(devices, cap, owner_ref, cell_ref, rows_ref, out_ref,
                wide, spread, slot_vmem, slot_smem, sem):
    p_local, channels = rows_ref.shape
    blocks = p_local // LANES
    stride = cap + EXTRA
    upper = (lax.broadcasted_iota(jnp.int32, (LANES, LANES), 0)
             <= lax.broadcasted_iota(jnp.int32, (LANES, LANES), 1)).astype(jnp.bfloat16)
    ids = lax.broadcasted_iota(jnp.int32, (devices, LANES), 0)
    spots = lax.broadcasted_iota(jnp.int32, (cap, LANES), 0)
    base = jnp.zeros((devices, 1), jnp.float32)
    table = jnp.zeros((2 * devices, cap), jnp.float32)
    for b in range(blocks):
        own = owner_ref[b:b + 1, :]
        cell = cell_ref[b:b + 1, :]
        hit = ids == own
        hot = hit.astype(jnp.float32)
        run = jnp.dot(hot.astype(jnp.bfloat16), upper, preferred_element_type=jnp.float32)
        place = jnp.sum(hot * (run + base), axis=0, keepdims=True).astype(jnp.int32) - 1
        base = base + run[:, LANES - 1:LANES]
        slot_vmem[b:b + 1, :] = own * stride + place
        high = jnp.where(hit, (cell // LANES + 1).astype(jnp.float32), 0.0)
        low = jnp.where(hit, (cell % LANES).astype(jnp.float32), 0.0)
        left = jnp.concatenate([high, low], axis=0).astype(jnp.bfloat16)
        right = (spots == place).astype(jnp.float32).astype(jnp.bfloat16)
        table = table + lax.dot_general(left, right, (((1,), (1,)), ((), ())),
                                        preferred_element_type=jnp.float32)
    copy = pltpu.make_async_copy(slot_vmem, slot_smem, sem)
    copy.start()
    wide[...] = rows_ref[...].astype(jnp.float32)
    per = -(-cap // LANES)
    for part in range(2):
        for j in range(per):
            width = min(LANES, cap - j * LANES)
            piece = table[part * devices:(part + 1) * devices, j * LANES:j * LANES + width]
            if width < LANES:
                piece = jnp.concatenate(
                    [piece, jnp.zeros((devices, LANES - width), jnp.float32)], axis=1)
            spread[pl.ds(cap + part * per + j, devices, stride=stride), :] = piece
    copy.wait()

    def step(b, carry):
        for u in range(LANES):
            spread[pl.ds(slot_smem[b, u], 1), :] = wide[pl.ds(b * LANES + u, 1), :]
        return carry

    lax.fori_loop(0, blocks, step, 0)
    out_ref[...] = spread[...].astype(jnp.bfloat16)


def pack(owner, cell, rows, devices, cap):
    p_local, channels = rows.shape
    blocks = p_local // LANES
    total = devices * (cap + EXTRA)
    vm = pl.BlockSpec(memory_space=pltpu.VMEM)
    return pl.pallas_call(
        functools.partial(pack_kernel, devices, cap),
        out_shape=jax.ShapeDtypeStruct((total, channels), jnp.bfloat16),
        in_specs=[vm, vm, vm],
        out_specs=vm,
        scratch_shapes=[
            pltpu.VMEM((p_local, channels), jnp.float32),
            pltpu.VMEM((total, channels), jnp.float32),
            pltpu.VMEM((blocks, LANES), jnp.int32),
            pltpu.SMEM((blocks, LANES), jnp.int32),
            pltpu.SemaphoreType.DMA,
        ],
        name="pack",
        cost_estimate=pl.CostEstimate(flops=10**8, bytes_accessed=4 * 10**6, transcendentals=0),
    )(owner.reshape(blocks, LANES), cell.reshape(blocks, LANES), rows)


WAYS = 4


def add_kernel(devices, cap, cells, got_ref, base_hbm, out_ref, wide, slot_vmem, slot_smem,
               sem, sem2, *sums):
    channels = got_ref.shape[-1]
    stride = cap + EXTRA
    per = -(-cap // LANES)
    first = pltpu.make_async_copy(base_hbm, sums[0].at[pl.ds(0, cells)], sem2)
    first.start()
    wide[...] = got_ref[...].astype(jnp.float32)
    for j in range(per):
        width = min(LANES, cap - j * LANES)
        high = wide[pl.ds(cap + j, devices, stride=stride), :].astype(jnp.int32)
        low = wide[pl.ds(cap + per + j, devices, stride=stride), :].astype(jnp.int32)
        spot = jnp.where(high > 0, (high - 1) * LANES + low, cells)
        slot_vmem[:, j * LANES:j * LANES + width] = spot[:, :width]
    copy = pltpu.make_async_copy(slot_vmem, slot_smem, sem)
    copy.start()
    for s in sums[1:]:
        s[...] = jnp.zeros_like(s)
    copy.wait()
    first.wait()

    def step(o, carry):
        def inner(q, carry):
            for u in range(32):
                at = slot_smem[o, q * 32 + u]
                s = sums[u % len(sums)]
                s[pl.ds(at, 1), :] += wide[pl.ds(o * stride + q * 32 + u, 1), :]
            return carry
        return lax.fori_loop(0, cap // 32, inner, carry)

    lax.fori_loop(0, devices, step, 0)
    total = sums[0][pl.ds(0, cells), :]
    for s in sums[1:]:
        total = total + s[pl.ds(0, cells), :]
    out_ref[...] = total.astype(jnp.bfloat16)


def add_rows(got, base, devices, cap):
    cells, channels = base.shape
    vm = pl.BlockSpec(memory_space=pltpu.VMEM)
    total = devices * (cap + EXTRA)
    return pl.pallas_call(
        functools.partial(add_kernel, devices, cap, cells),
        out_shape=jax.ShapeDtypeStruct((cells, channels), jnp.bfloat16),
        in_specs=[vm, pl.BlockSpec(memory_space=pl.ANY)],
        out_specs=vm,
        scratch_shapes=[
            pltpu.VMEM((total, channels), jnp.float32),
            pltpu.VMEM((devices, cap), jnp.int32),
            pltpu.SMEM((devices, cap), jnp.int32),
            pltpu.SemaphoreType.DMA,
            pltpu.SemaphoreType.DMA,
        ] + [pltpu.VMEM((cells + 8, channels), jnp.float32)] * WAYS,
        name="add_rows",
        cost_estimate=pl.CostEstimate(flops=10**8, bytes_accessed=8 * 10**6, transcendentals=0),
    )(got, base)


def residual_kernel(group, level_ref, ylow_ref, yhigh_ref, xlow_ref, xhigh_ref, w_ref, out_ref,
                    plane, taps, wide, result):
    span_x, span_y, span_z, channels = level_ref.shape
    half = (span_y + 2) // 2
    lines = half * span_z
    three = 3 * channels
    for a in range(3):
        for d in range(2):
            for par in range(2):
                for c in range(3):
                    at = ((a * 2 + d) * 2 + par) * three + c * channels
                    for s in range(2):
                        b = 2 * d + par - s
                        if 0 <= b <= 2:
                            tile = w_ref[9 * a + 3 * b + c]
                        else:
                            tile = jnp.zeros((channels, channels), jnp.bfloat16)
                        wide[at:at + channels, s * channels:(s + 1) * channels] = tile
    spot = lax.broadcasted_iota(jnp.int32, ((span_y + 2) * span_z, channels), 0) % span_z
    count = (span_y + 2) * span_z
    plane[0:8, :] = jnp.zeros((8, channels), jnp.float32)
    plane[8 + count:16 + count, :] = jnp.zeros((8, channels), jnp.float32)

    def spread(x):
        middle = plane[8:8 + count, :]
        low = jnp.where(spot == 0, 0.0, plane[7:7 + count, :])
        high = jnp.where(spot == span_z - 1, 0.0, plane[9:9 + count, :])
        for c, value in enumerate((low, middle, high)):
            value = value.astype(jnp.bfloat16).reshape(half, 2, span_z, channels)
            for par in range(2):
                taps[pl.ds(pl.multiple_of(x * lines, 16), lines),
                     par * three + c * channels:par * three + (c + 1) * channels] = (
                    value[:, par].reshape(lines, channels))

    for x, ref in ((0, xlow_ref), (span_x + 1, xhigh_ref)):
        plane[8:8 + count, :] = ref[...].reshape(count, channels).astype(jnp.float32)
        spread(x)

    def fill(x, carry):
        plane[8:8 + span_z, :] = ylow_ref[x].reshape(span_z, channels).astype(jnp.float32)
        plane[8 + span_z:8 + count - span_z, :] = level_ref[x].reshape(
            span_y * span_z, channels).astype(jnp.float32)
        plane[8 + count - span_z:8 + count, :] = yhigh_ref[x].reshape(
            span_z, channels).astype(jnp.float32)
        spread(x + 1)
        return carry

    lax.fori_loop(0, span_x, fill, 0)
    height = group * lines - span_z

    def multiply(g, carry):
        total = None
        for a in range(3):
            for d in range(2):
                start = pl.multiple_of((g * group + a) * lines + d * span_z, 16)
                at = (a * 2 + d) * 2 * three
                part = jnp.dot(taps[pl.ds(start, height), :], wide[at:at + 2 * three, :],
                               preferred_element_type=jnp.float32)
                total = part if total is None else total + part
        result[0:height, :] = total
        for i in range(group):
            x = g * group + i
            for s in range(2):
                value = result[i * lines:i * lines + span_y // 2 * span_z,
                               s * channels:(s + 1) * channels]
                value = jnp.maximum(value, 0.0).reshape(span_y // 2, span_z, channels)
                here = level_ref[x].reshape(span_y // 2, 2, span_z, channels)[:, s]
                out_ref[x, :, s] = value + here.astype(jnp.float32)
        return carry

    lax.fori_loop(0, span_x // group, multiply, 0)


def residual_base(level, ylow, yhigh, xlow, xhigh, w_res, group=4):
    span_x, span_y, span_z, channels = level.shape
    lines = (span_y + 2) // 2 * span_z
    vm = pl.BlockSpec(memory_space=pltpu.VMEM)
    flops = 2 * span_x * span_y * span_z * 27 * channels * channels
    out = pl.pallas_call(
        functools.partial(residual_kernel, group),
        out_shape=jax.ShapeDtypeStruct((span_x, span_y // 2, 2, span_z, channels), jnp.float32),
        in_specs=[vm] * 6,
        out_specs=vm,
        scratch_shapes=[
            pltpu.VMEM(((span_y + 2) * span_z + 16, channels), jnp.float32),
            pltpu.VMEM(((span_x + 2) * lines, 6 * channels), jnp.bfloat16),
            pltpu.VMEM((36 * channels, 2 * channels), jnp.bfloat16),
            pltpu.VMEM((group * lines, 2 * channels), jnp.float32),
        ],
        name="residual",
        cost_estimate=pl.CostEstimate(flops=flops, bytes_accessed=8 * 10**6, transcendentals=0),
    )(level, ylow, yhigh, xlow, xhigh, w_res)
    return out.reshape(span_x * span_y * span_z, channels)


def lower_kernel(joined_ref, front_ref, side_ref, corner_ref, w_ref, out_ref, plane, taps):
    span_x, span_y, span_z, channels = joined_ref.shape
    half_y, half_z = span_y // 2, span_z // 2
    lines = half_y * half_z
    count = (span_y + 1) * span_z
    zero = lax.broadcasted_iota(jnp.int32, ((span_y + 1) * half_z, channels), 0) % half_z == 0
    plane[0:8, :] = jnp.zeros((8, channels), jnp.float32)

    def spread(x):
        rows = (span_y + 1) * half_z
        low = jnp.where(zero, 0.0, plane[pl.ds(7, rows, stride=2), :])
        for c, value in enumerate((low, plane[pl.ds(8, rows, stride=2), :],
                                   plane[pl.ds(9, rows, stride=2), :])):
            value = value.reshape(span_y + 1, half_z, channels)
            evens = value[0:span_y].reshape(half_y, 2, half_z, channels)
            odds = value[1:].reshape(half_y, 2, half_z, channels)
            for b, piece in enumerate((evens[:, 0], evens[:, 1], odds[:, 1])):
                at = (b * 3 + c) * channels
                taps[x, :, at:at + channels] = piece.reshape(lines, channels).astype(jnp.bfloat16)

    plane[8:8 + span_z, :] = corner_ref[...].reshape(span_z, channels).astype(jnp.float32)
    plane[8 + span_z:8 + count, :] = front_ref[...].reshape(
        span_y * span_z, channels).astype(jnp.float32)
    spread(0)

    def fill(x, carry):
        plane[8:8 + span_z, :] = side_ref[x].reshape(span_z, channels).astype(jnp.float32)
        plane[8 + span_z:8 + count, :] = joined_ref[x].reshape(
            span_y * span_z, channels).astype(jnp.float32)
        spread(x + 1)
        return carry

    lax.fori_loop(0, span_x, fill, 0)
    depth = 9 * channels

    def multiply(i, carry):
        total = None
        for a in range(3):
            part = jnp.dot(taps[2 * i + a], w_ref[a * depth:(a + 1) * depth, :],
                           preferred_element_type=jnp.float32)
            total = part if total is None else total + part
        out_ref[i] = total.reshape(half_y, half_z, w_ref.shape[-1]).astype(jnp.bfloat16)
        return carry

    lax.fori_loop(0, span_x // 2, multiply, 0)


def lower(joined, front, side, corner, w_down):
    span_x, span_y, span_z, channels = joined.shape
    wide = w_down.shape[-1]
    vm = pl.BlockSpec(memory_space=pltpu.VMEM)
    flops = 2 * span_x * span_y * span_z // 8 * 27 * channels * wide
    return pl.pallas_call(
        lower_kernel,
        out_shape=jax.ShapeDtypeStruct((span_x // 2, span_y // 2, span_z // 2, wide),
                                       jnp.bfloat16),
        in_specs=[vm] * 5,
        out_specs=vm,
        scratch_shapes=[
            pltpu.VMEM(((span_y + 1) * span_z + 16, channels), jnp.float32),
            pltpu.VMEM((span_x + 1, span_y * span_z // 4, 9 * channels), jnp.bfloat16),
        ],
        name="lower",
        cost_estimate=pl.CostEstimate(flops=flops, bytes_accessed=5 * 10**6, transcendentals=0),
    )(joined, front, side, corner, w_down.reshape(-1, wide))


def pairs_of(axis, by):
    count = lax.axis_size(axis)
    return [(i, i + by) for i in range(count) if 0 <= i + by < count]


def passed_along(array, axis, by):
    return lax.ppermute(array, axis, pairs_of(axis, by))


def body(points, dest_owner, dest_cell, level_input, w_res, w_down):
    count_pts = lax.axis_size("pts")
    count_nbr = lax.axis_size("nbr")
    devices = count_pts * count_nbr
    channels = points.shape[-1]
    rows = points.reshape(-1, channels)
    capacity = 2 * rows.shape[0] // devices
    outgoing = pack(dest_owner.reshape(-1), dest_cell.reshape(-1), rows, devices, capacity)
    outgoing, level = lax.optimization_barrier((outgoing, level_input))
    got = lax.all_to_all(
        outgoing.reshape(devices, capacity + EXTRA, channels),
        ("pts", "nbr"),
        split_axis=0,
        concat_axis=0,
        tiled=True,
    ).reshape(outgoing.shape)
    span_x, span_y, span_z = level_input.shape[:3]
    low_y = passed_along(level[:, -1:], "pts", 1)
    high_y = passed_along(level[:, :1], "pts", -1)
    last = jnp.concatenate([low_y[-1:], level[-1:], high_y[-1:]], axis=1)
    first = jnp.concatenate([low_y[:1], level[:1], high_y[:1]], axis=1)
    low_x = passed_along(last, "nbr", 1)
    high_x = passed_along(first, "nbr", -1)
    base = residual_base(level, low_y, high_y, low_x, high_x, w_res)
    joined = add_rows(got, base, devices, capacity)
    joined = joined.reshape(span_x, span_y, span_z, channels)
    front = passed_along(joined[-1:], "nbr", 1)
    side = passed_along(joined[:, -1:], "pts", 1)
    diagonal = [
        (i * count_nbr + j, (i + 1) * count_nbr + j + 1)
        for i in range(count_pts - 1)
        for j in range(count_nbr - 1)
    ]
    corner = lax.ppermute(joined[-1:, -1:], ("pts", "nbr"), diagonal)
    return lower(joined, front, side, corner, w_down)


def solution(mesh):
    return jax.shard_map(
        body,
        mesh=mesh,
        in_specs=(
            P("pts", "nbr", None, None),
            P("pts", "nbr", None, None),
            P("pts", "nbr", None),
            P("nbr", "pts", None, None),
            P(),
            P(),
        ),
        out_specs=P("nbr", "pts", None, None),
        check_vma=False,
    )
```

```python
import functools
import jax
import jax.numpy as jnp
from jax import lax
from jax.experimental import pallas as pl
from jax.experimental.pallas import tpu as pltpu
from jax.sharding import PartitionSpec as P


LANES = 128
EXTRA = 8


def pack_kernel(devices, cap, owner_ref, cell_ref, rows_ref, out_ref,
                wide, spread, slot_vmem, slot_smem, sem):
    p_local, _ = rows_ref.shape
    blocks = p_local // LANES
    stride = cap + EXTRA
    upper = (lax.broadcasted_iota(jnp.int32, (LANES, LANES), 0)
             <= lax.broadcasted_iota(jnp.int32, (LANES, LANES), 1)).astype(jnp.bfloat16)
    ids = lax.broadcasted_iota(jnp.int32, (devices, LANES), 0)
    spots = lax.broadcasted_iota(jnp.int32, (cap, LANES), 0)
    base = jnp.zeros((devices, 1), jnp.float32)
    table = jnp.zeros((2 * devices, cap), jnp.float32)
    for b in range(blocks):
        own = owner_ref[b:b + 1, :]
        cell = cell_ref[b:b + 1, :]
        hit = ids == own
        hot = hit.astype(jnp.float32)
        run = jnp.dot(hot.astype(jnp.bfloat16), upper, preferred_element_type=jnp.float32)
        place = jnp.sum(hot * (run + base), axis=0, keepdims=True).astype(jnp.int32) - 1
        base = base + run[:, LANES - 1:LANES]
        slot_vmem[b:b + 1, :] = own * stride + place
        high = jnp.where(hit, (cell // LANES + 1).astype(jnp.float32), 0.0)
        low = jnp.where(hit, (cell % LANES).astype(jnp.float32), 0.0)
        left = jnp.concatenate([high, low], axis=0).astype(jnp.bfloat16)
        right = (spots == place).astype(jnp.float32).astype(jnp.bfloat16)
        table = table + lax.dot_general(left, right, (((1,), (1,)), ((), ())),
                                        preferred_element_type=jnp.float32)
    copy = pltpu.make_async_copy(slot_vmem, slot_smem, sem)
    copy.start()
    wide[...] = rows_ref[...].astype(jnp.float32)
    per = -(-cap // LANES)
    for part in range(2):
        for j in range(per):
            width = min(LANES, cap - j * LANES)
            piece = table[part * devices:(part + 1) * devices, j * LANES:j * LANES + width]
            if width < LANES:
                piece = jnp.concatenate(
                    [piece, jnp.zeros((devices, LANES - width), jnp.float32)], axis=1)
            spread[pl.ds(cap + part * per + j, devices, stride=stride), :] = piece
    copy.wait()

    def step(b, carry):
        for u in range(LANES):
            spread[pl.ds(slot_smem[b, u], 1), :] = wide[pl.ds(b * LANES + u, 1), :]
        return carry

    lax.fori_loop(0, blocks, step, 0)
    out_ref[...] = spread[...].astype(jnp.bfloat16)


def pack(owner, cell, rows, devices, cap):
    p_local, channels = rows.shape
    blocks = p_local // LANES
    total = devices * (cap + EXTRA)
    vm = pl.BlockSpec(memory_space=pltpu.VMEM)
    return pl.pallas_call(
        functools.partial(pack_kernel, devices, cap),
        out_shape=jax.ShapeDtypeStruct((total, channels), jnp.bfloat16),
        in_specs=[vm, vm, vm],
        out_specs=vm,
        scratch_shapes=[
            pltpu.VMEM((p_local, channels), jnp.float32),
            pltpu.VMEM((total, channels), jnp.float32),
            pltpu.VMEM((blocks, LANES), jnp.int32),
            pltpu.SMEM((blocks, LANES), jnp.int32),
            pltpu.SemaphoreType.DMA,
        ],
        name="pack",
        cost_estimate=pl.CostEstimate(flops=10**8, bytes_accessed=4 * 10**6, transcendentals=0),
    )(owner.reshape(blocks, LANES), cell.reshape(blocks, LANES), rows)


WAYS = 6
PIECES = 4
LIMIT = 48 * 2**20


def add_kernel(capacity, got_hbm, base_hbm, out_ref, front_ref, side_ref, corner_ref,
               landed, wide, slot_vmem, slot_smem, sems, *sums):
    span_x, span_y, span_z, channels = out_ref.shape
    cells = span_x * span_y * span_z
    total, _ = landed.shape
    stride = capacity + EXTRA
    devices = total // stride
    per = -(-capacity // LANES)
    width = min(LANES, capacity)
    piece = total // PIECES
    copies = [
        pltpu.make_async_copy(got_hbm.at[pl.ds(i * piece, piece)],
                              landed.at[pl.ds(i * piece, piece)], sems.at[i])
        for i in range(PIECES)
    ]
    for copy in copies:
        copy.start()
    first = pltpu.make_async_copy(base_hbm, sums[0].at[pl.ds(0, cells)], sems.at[PIECES])
    first.start()
    half = len(sums) // 2
    for s in sums[1:half]:
        s[...] = jnp.zeros_like(s)
    for i, copy in enumerate(copies):
        copy.wait()
        wide[i * piece:(i + 1) * piece, :] = landed[i * piece:(i + 1) * piece, :].astype(
            jnp.float32)
    for j in range(per):
        high = wide[pl.ds(capacity + j, devices, stride=stride), :].astype(jnp.int32)
        low = wide[pl.ds(capacity + per + j, devices, stride=stride), :].astype(jnp.int32)
        slot_vmem[j * devices:(j + 1) * devices, :] = jnp.where(
            high > 0, (high - 1) * LANES + low, cells)
    copy = pltpu.make_async_copy(slot_vmem, slot_smem, sems.at[PIECES + 1])
    copy.start()
    for s in sums[max(half, 1):]:
        s[...] = jnp.zeros_like(s)
    copy.wait()
    first.wait()
    for j in range(per):
        def step(o, carry):
            start = pl.multiple_of(o * stride + j * LANES, 8)
            for u in range(width):
                at = slot_smem[j * devices + o, u]
                s = sums[u % len(sums)]
                s[pl.ds(at, 1), :] += wide[pl.ds(start + u, 1), :]
            return carry

        lax.fori_loop(0, devices, step, 0)

    def finish(x, carry):
        at = pl.ds(pl.multiple_of(x * (span_y * span_z), 8), span_y * span_z)
        value = sums[0][at, :]
        for s in sums[1:]:
            value = value + s[at, :]
        value = value.astype(jnp.bfloat16).reshape(span_y, span_z, channels)
        out_ref[x] = value
        side_ref[x] = value[span_y - 1:]
        return carry

    lax.fori_loop(0, span_x, finish, 0)
    front_ref[...] = out_ref[span_x - 1:]
    corner_ref[...] = out_ref[span_x - 1:, span_y - 1:]


def add_rows(got, base, shape, capacity):
    span_x, span_y, span_z, channels = shape
    cells = span_x * span_y * span_z
    total = got.shape[0]
    devices = total // (capacity + EXTRA)
    per = -(-capacity // LANES)
    vm = pl.BlockSpec(memory_space=pltpu.VMEM)
    hbm = pl.BlockSpec(memory_space=pl.ANY)
    return pl.pallas_call(
        functools.partial(add_kernel, capacity),
        out_shape=[
            jax.ShapeDtypeStruct(shape, jnp.bfloat16),
            jax.ShapeDtypeStruct((1, span_y, span_z, channels), jnp.bfloat16),
            jax.ShapeDtypeStruct((span_x, 1, span_z, channels), jnp.bfloat16),
            jax.ShapeDtypeStruct((1, 1, span_z, channels), jnp.bfloat16),
        ],
        in_specs=[hbm, hbm],
        out_specs=[vm] * 4,
        scratch_shapes=[
            pltpu.VMEM((total, channels), jnp.bfloat16),
            pltpu.VMEM((total, channels), jnp.float32),
            pltpu.VMEM((devices * per, LANES), jnp.int32),
            pltpu.SMEM((devices * per, LANES), jnp.int32),
            pltpu.SemaphoreType.DMA((PIECES + 2,)),
        ] + [pltpu.VMEM((cells + 8, channels), jnp.float32)] * WAYS,
        compiler_params=pltpu.CompilerParams(vmem_limit_bytes=LIMIT),
        name="add_rows",
        cost_estimate=pl.CostEstimate(flops=10**8, bytes_accessed=8 * 10**6, transcendentals=0),
    )(got, base)


def residual_kernel(group, level_ref, ylow_ref, yhigh_ref, xlow_ref, xhigh_ref, w_ref, out_ref,
                    plane, taps, wide, result):
    span_x, span_y, span_z, channels = level_ref.shape
    half = (span_y + 2) // 2
    lines = half * span_z
    three = 3 * channels
    for a in range(3):
        for d in range(2):
            for par in range(2):
                for c in range(3):
                    at = ((a * 2 + d) * 2 + par) * three + c * channels
                    for s in range(2):
                        b = 2 * d + par - s
                        if 0 <= b <= 2:
                            tile = w_ref[9 * a + 3 * b + c]
                        else:
                            tile = jnp.zeros((channels, channels), jnp.bfloat16)
                        wide[at:at + channels, s * channels:(s + 1) * channels] = tile
    spot = lax.broadcasted_iota(jnp.int32, ((span_y + 2) * span_z, channels), 0) % span_z
    count = (span_y + 2) * span_z
    plane[0:8, :] = jnp.zeros((8, channels), jnp.float32)
    plane[8 + count:16 + count, :] = jnp.zeros((8, channels), jnp.float32)

    def spread(x):
        middle = plane[8:8 + count, :]
        low = jnp.where(spot == 0, 0.0, plane[7:7 + count, :])
        high = jnp.where(spot == span_z - 1, 0.0, plane[9:9 + count, :])
        for c, value in enumerate((low, middle, high)):
            value = value.astype(jnp.bfloat16).reshape(half, 2, span_z, channels)
            for par in range(2):
                taps[pl.ds(pl.multiple_of(x * lines, 16), lines),
                     par * three + c * channels:par * three + (c + 1) * channels] = (
                    value[:, par].reshape(lines, channels))

    for x, ref in ((0, xlow_ref), (span_x + 1, xhigh_ref)):
        plane[8:8 + count, :] = ref[...].reshape(count, channels).astype(jnp.float32)
        spread(x)

    def fill(x, carry):
        plane[8:8 + span_z, :] = ylow_ref[x].reshape(span_z, channels).astype(jnp.float32)
        plane[8 + span_z:8 + count - span_z, :] = level_ref[x].reshape(
            span_y * span_z, channels).astype(jnp.float32)
        plane[8 + count - span_z:8 + count, :] = yhigh_ref[x].reshape(
            span_z, channels).astype(jnp.float32)
        spread(x + 1)
        return carry

    lax.fori_loop(0, span_x, fill, 0)
    height = group * lines - span_z

    def multiply(g, carry):
        total = None
        for a in range(3):
            for d in range(2):
                start = pl.multiple_of((g * group + a) * lines + d * span_z, 16)
                at = (a * 2 + d) * 2 * three
                part = jnp.dot(taps[pl.ds(start, height), :], wide[at:at + 2 * three, :],
                               preferred_element_type=jnp.float32)
                total = part if total is None else total + part
        result[0:height, :] = total
        for i in range(group):
            x = g * group + i
            for s in range(2):
                value = result[i * lines:i * lines + span_y // 2 * span_z,
                               s * channels:(s + 1) * channels]
                value = jnp.maximum(value, 0.0).reshape(span_y // 2, span_z, channels)
                here = level_ref[x].reshape(span_y // 2, 2, span_z, channels)[:, s]
                out_ref[x, :, s] = value + here.astype(jnp.float32)
        return carry

    lax.fori_loop(0, span_x // group, multiply, 0)


def residual_base(level, ylow, yhigh, xlow, xhigh, w_res, group=4):
    span_x, span_y, span_z, channels = level.shape
    lines = (span_y + 2) // 2 * span_z
    vm = pl.BlockSpec(memory_space=pltpu.VMEM)
    flops = 2 * span_x * span_y * span_z * 27 * channels * channels
    out = pl.pallas_call(
        functools.partial(residual_kernel, group),
        out_shape=jax.ShapeDtypeStruct((span_x, span_y // 2, 2, span_z, channels), jnp.float32),
        in_specs=[vm] * 6,
        out_specs=vm,
        scratch_shapes=[
            pltpu.VMEM(((span_y + 2) * span_z + 16, channels), jnp.float32),
            pltpu.VMEM(((span_x + 2) * lines, 6 * channels), jnp.bfloat16),
            pltpu.VMEM((36 * channels, 2 * channels), jnp.bfloat16),
            pltpu.VMEM((group * lines, 2 * channels), jnp.float32),
        ],
        compiler_params=pltpu.CompilerParams(vmem_limit_bytes=36 * 2**20),
        name="residual",
        cost_estimate=pl.CostEstimate(flops=flops, bytes_accessed=8 * 10**6, transcendentals=0),
    )(level, ylow, yhigh, xlow, xhigh, w_res)
    return out.reshape(span_x * span_y * span_z, channels)


def lower_kernel(joined_ref, front_ref, side_ref, corner_ref, w_ref, out_ref, plane, taps):
    span_x, span_y, span_z, channels = joined_ref.shape
    half_y, half_z = span_y // 2, span_z // 2
    lines = half_y * half_z
    count = (span_y + 1) * span_z
    zero = lax.broadcasted_iota(jnp.int32, ((span_y + 1) * half_z, channels), 0) % half_z == 0
    plane[0:8, :] = jnp.zeros((8, channels), jnp.float32)

    def spread(x):
        rows = (span_y + 1) * half_z
        low = jnp.where(zero, 0.0, plane[pl.ds(7, rows, stride=2), :])
        for c, value in enumerate((low, plane[pl.ds(8, rows, stride=2), :],
                                   plane[pl.ds(9, rows, stride=2), :])):
            value = value.reshape(span_y + 1, half_z, channels)
            evens = value[0:span_y].reshape(half_y, 2, half_z, channels)
            odds = value[1:].reshape(half_y, 2, half_z, channels)
            for b, piece in enumerate((evens[:, 0], evens[:, 1], odds[:, 1])):
                at = (b * 3 + c) * channels
                taps[x, :, at:at + channels] = piece.reshape(lines, channels).astype(jnp.bfloat16)

    plane[8:8 + span_z, :] = corner_ref[...].reshape(span_z, channels).astype(jnp.float32)
    plane[8 + span_z:8 + count, :] = front_ref[...].reshape(
        span_y * span_z, channels).astype(jnp.float32)
    spread(0)

    def fill(x, carry):
        plane[8:8 + span_z, :] = side_ref[x].reshape(span_z, channels).astype(jnp.float32)
        plane[8 + span_z:8 + count, :] = joined_ref[x].reshape(
            span_y * span_z, channels).astype(jnp.float32)
        spread(x + 1)
        return carry

    lax.fori_loop(0, span_x, fill, 0)
    depth = 9 * channels

    def multiply(i, carry):
        total = None
        for a in range(3):
            part = jnp.dot(taps[2 * i + a], w_ref[a * depth:(a + 1) * depth, :],
                           preferred_element_type=jnp.float32)
            total = part if total is None else total + part
        out_ref[i] = total.reshape(half_y, half_z, w_ref.shape[-1]).astype(jnp.bfloat16)
        return carry

    lax.fori_loop(0, span_x // 2, multiply, 0)


def lower(joined, front, side, corner, w_down):
    span_x, span_y, span_z, channels = joined.shape
    wide = w_down.shape[-1]
    vm = pl.BlockSpec(memory_space=pltpu.VMEM)
    flops = 2 * span_x * span_y * span_z // 8 * 27 * channels * wide
    return pl.pallas_call(
        lower_kernel,
        out_shape=jax.ShapeDtypeStruct((span_x // 2, span_y // 2, span_z // 2, wide),
                                       jnp.bfloat16),
        in_specs=[vm] * 5,
        out_specs=vm,
        scratch_shapes=[
            pltpu.VMEM(((span_y + 1) * span_z + 16, channels), jnp.float32),
            pltpu.VMEM((span_x + 1, span_y * span_z // 4, 9 * channels), jnp.bfloat16),
        ],
        compiler_params=pltpu.CompilerParams(vmem_limit_bytes=28 * 2**20),
        name="lower",
        cost_estimate=pl.CostEstimate(flops=flops, bytes_accessed=5 * 10**6, transcendentals=0),
    )(joined, front, side, corner, w_down.reshape(-1, wide))


def pairs_of(axis, by):
    count = lax.axis_size(axis)
    return [(i, i + by) for i in range(count) if 0 <= i + by < count]


def passed_along(array, axis, by):
    return lax.ppermute(array, axis, pairs_of(axis, by))


def body(points, dest_owner, dest_cell, level_input, w_res, w_down):
    count_pts = lax.axis_size("pts")
    count_nbr = lax.axis_size("nbr")
    devices = count_pts * count_nbr
    channels = points.shape[-1]
    rows = points.reshape(-1, channels)
    capacity = 2 * rows.shape[0] // devices
    level = level_input
    low_y = passed_along(level[:, -1:], "pts", 1)
    high_y = passed_along(level[:, :1], "pts", -1)
    outgoing = pack(dest_owner.reshape(-1), dest_cell.reshape(-1), rows, devices, capacity)
    last = jnp.concatenate([low_y[-1:], level[-1:], high_y[-1:]], axis=1)
    first = jnp.concatenate([low_y[:1], level[:1], high_y[:1]], axis=1)
    outgoing, last, first = lax.optimization_barrier((outgoing, last, first))
    low_x = passed_along(last, "nbr", 1)
    high_x = passed_along(first, "nbr", -1)
    got = lax.all_to_all(
        outgoing.reshape(devices, capacity + EXTRA, channels),
        ("pts", "nbr"),
        split_axis=0,
        concat_axis=0,
        tiled=True,
    ).reshape(outgoing.shape)
    base = residual_base(level, low_y, high_y, low_x, high_x, w_res)
    joined, front, side, corner = add_rows(got, base, level.shape, capacity)
    diagonal = [
        (i * count_nbr + j, (i + 1) * count_nbr + j + 1)
        for i in range(count_pts - 1)
        for j in range(count_nbr - 1)
    ]
    front = passed_along(front, "nbr", 1)
    side = passed_along(side, "pts", 1)
    corner = lax.ppermute(corner, ("pts", "nbr"), diagonal)
    return lower(joined, front, side, corner, w_down)


def solution(mesh):
    return jax.shard_map(
        body,
        mesh=mesh,
        in_specs=(
            P("pts", "nbr", None, None),
            P("pts", "nbr", None, None),
            P("pts", "nbr", None),
            P("nbr", "pts", None, None),
            P(),
            P(),
        ),
        out_specs=P("nbr", "pts", None, None),
        check_vma=False,
    )
```

```python
import functools
import math
import jax
import jax.numpy as jnp
from jax import lax
from jax.experimental import pallas as pl
from jax.experimental.pallas import tpu as pltpu
from jax.sharding import PartitionSpec as P


LANES = 128
EXTRA = 8


def pack_kernel(devices, cap, cut, owner_ref, cell_ref, rows_ref, first_ref, second_ref,
                wide, spread, slot_vmem, slot_smem, sem):
    p_local, _ = rows_ref.shape
    blocks = p_local // LANES
    stride = cut + EXTRA
    rest = cap - cut
    break_at = devices * stride
    upper = (lax.broadcasted_iota(jnp.int32, (LANES, LANES), 0)
             <= lax.broadcasted_iota(jnp.int32, (LANES, LANES), 1)).astype(jnp.bfloat16)
    ids = lax.broadcasted_iota(jnp.int32, (devices, LANES), 0)
    spots = lax.broadcasted_iota(jnp.int32, (cap, LANES), 0)
    base = jnp.zeros((devices, 1), jnp.float32)
    table = jnp.zeros((2 * devices, cap), jnp.float32)
    for b in range(blocks):
        own = owner_ref[b:b + 1, :]
        cell = cell_ref[b:b + 1, :]
        hit = ids == own
        hot = hit.astype(jnp.float32)
        run = jnp.dot(hot.astype(jnp.bfloat16), upper, preferred_element_type=jnp.float32)
        place = jnp.sum(hot * (run + base), axis=0, keepdims=True).astype(jnp.int32) - 1
        base = base + run[:, LANES - 1:LANES]
        slot_vmem[b:b + 1, :] = jnp.where(
            place < cut, own * stride + place, break_at - cut + own * rest + place)
        high = jnp.where(hit, (cell // LANES + 1).astype(jnp.float32), 0.0)
        low = jnp.where(hit, (cell % LANES).astype(jnp.float32), 0.0)
        left = jnp.concatenate([high, low], axis=0).astype(jnp.bfloat16)
        right = (spots == place).astype(jnp.float32).astype(jnp.bfloat16)
        table = table + lax.dot_general(left, right, (((1,), (1,)), ((), ())),
                                        preferred_element_type=jnp.float32)
    copy = pltpu.make_async_copy(slot_vmem, slot_smem, sem)
    copy.start()
    wide[...] = rows_ref[...].astype(jnp.float32)
    per = -(-cap // LANES)
    for part in range(2):
        for j in range(per):
            width = min(LANES, cap - j * LANES)
            piece = table[part * devices:(part + 1) * devices, j * LANES:j * LANES + width]
            if width < LANES:
                piece = jnp.concatenate(
                    [piece, jnp.zeros((devices, LANES - width), jnp.float32)], axis=1)
            spread[pl.ds(cut + part * per + j, devices, stride=stride), :] = piece
    copy.wait()

    def step(b, carry):
        for u in range(LANES):
            spread[pl.ds(slot_smem[b, u], 1), :] = wide[pl.ds(b * LANES + u, 1), :]
        return carry

    lax.fori_loop(0, blocks, step, 0)
    first_ref[...] = spread[0:break_at, :].astype(jnp.bfloat16)
    second_ref[...] = spread[break_at:, :].astype(jnp.bfloat16)


def pack(owner, cell, rows, devices, cap, cut):
    p_local, channels = rows.shape
    blocks = p_local // LANES
    total = devices * (cap + EXTRA)
    vm = pl.BlockSpec(memory_space=pltpu.VMEM)
    return pl.pallas_call(
        functools.partial(pack_kernel, devices, cap, cut),
        out_shape=[
            jax.ShapeDtypeStruct((devices * (cut + EXTRA), channels), jnp.bfloat16),
            jax.ShapeDtypeStruct((devices * (cap - cut), channels), jnp.bfloat16),
        ],
        in_specs=[vm, vm, vm],
        out_specs=[vm, vm],
        scratch_shapes=[
            pltpu.VMEM((p_local, channels), jnp.float32),
            pltpu.VMEM((total, channels), jnp.float32),
            pltpu.VMEM((blocks, LANES), jnp.int32),
            pltpu.SMEM((blocks, LANES), jnp.int32),
            pltpu.SemaphoreType.DMA,
        ],
        name="pack",
        cost_estimate=pl.CostEstimate(flops=10**8, bytes_accessed=4 * 10**6, transcendentals=0),
    )(owner.reshape(blocks, LANES), cell.reshape(blocks, LANES), rows)


WAYS = 4


def add_loop(slots, wide, sums, devices, stride, begin, end):
    for j in range(begin // LANES, -(-end // LANES)):
        low, high = max(begin, j * LANES), min(end, (j + 1) * LANES)

        def step(o, carry):
            start = pl.multiple_of(o * stride + (low - begin), 8)
            for u in range(high - low):
                at = slots[j * devices + o, low - j * LANES + u]
                s = sums[u % len(sums)]
                s[pl.ds(at, 1), :] += wide[pl.ds(start + u, 1), :]
            return carry

        lax.fori_loop(0, devices, step, 0)


def early_kernel(cap, cut, got_ref, out_ref, slot_ref, wide, slot_smem, sem, *sums):
    cells, _ = out_ref.shape
    total, _ = got_ref.shape
    stride = cut + EXTRA
    devices = total // stride
    per = -(-cap // LANES)
    wide[...] = got_ref[...].astype(jnp.float32)
    for j in range(per):
        high = wide[pl.ds(cut + j, devices, stride=stride), :].astype(jnp.int32)
        low = wide[pl.ds(cut + per + j, devices, stride=stride), :].astype(jnp.int32)
        slot_ref[j * devices:(j + 1) * devices, :] = jnp.where(
            high > 0, (high - 1) * LANES + low, cells)
    copy = pltpu.make_async_copy(slot_ref, slot_smem, sem)
    copy.start()
    for s in sums:
        s[...] = jnp.zeros_like(s)
    copy.wait()
    add_loop(slot_smem, wide, sums, devices, stride, 0, cut)
    total = sums[0][pl.ds(0, cells), :]
    for s in sums[1:]:
        total = total + s[pl.ds(0, cells), :]
    out_ref[...] = total


def add_early(got, cells, cap, cut):
    total, channels = got.shape
    devices = total // (cut + EXTRA)
    per = -(-cap // LANES)
    vm = pl.BlockSpec(memory_space=pltpu.VMEM)
    return pl.pallas_call(
        functools.partial(early_kernel, cap, cut),
        out_shape=[
            jax.ShapeDtypeStruct((cells, channels), jnp.float32),
            jax.ShapeDtypeStruct((devices * per, LANES), jnp.int32),
        ],
        in_specs=[vm],
        out_specs=[vm, vm],
        scratch_shapes=[
            pltpu.VMEM((total, channels), jnp.float32),
            pltpu.SMEM((devices * per, LANES), jnp.int32),
            pltpu.SemaphoreType.DMA,
        ] + [pltpu.VMEM((cells + 8, channels), jnp.float32)] * WAYS,
        compiler_params=pltpu.CompilerParams(vmem_limit_bytes=36 * 2**20),
        name="add_early",
        cost_estimate=pl.CostEstimate(flops=10**8, bytes_accessed=8 * 10**6, transcendentals=0),
    )(got)


def late_kernel(cap, cut, slots, got_ref, base_hbm, out_ref, front_ref, side_ref, corner_ref,
                wide, sem, *sums):
    span_x, span_y, span_z, channels = out_ref.shape
    cells = span_x * span_y * span_z
    total, _ = got_ref.shape
    rest = cap - cut
    devices = total // rest
    first = pltpu.make_async_copy(base_hbm, sums[0].at[pl.ds(0, cells)], sem)
    first.start()
    for s in sums[1:]:
        s[...] = jnp.zeros_like(s)
    wide[...] = got_ref[...].astype(jnp.float32)
    first.wait()
    add_loop(slots, wide, sums, devices, rest, cut, cap)

    def finish(x, carry):
        at = pl.ds(pl.multiple_of(x * (span_y * span_z), 8), span_y * span_z)
        value = sums[0][at, :]
        for s in sums[1:]:
            value = value + s[at, :]
        value = value.astype(jnp.bfloat16).reshape(span_y, span_z, channels)
        out_ref[x] = value
        side_ref[x] = value[span_y - 1:]
        return carry

    lax.fori_loop(0, span_x, finish, 0)
    front_ref[...] = out_ref[span_x - 1:]
    corner_ref[...] = out_ref[span_x - 1:, span_y - 1:]


def add_late(slots, got, base, shape, cap, cut):
    span_x, span_y, span_z, channels = shape
    cells = span_x * span_y * span_z
    total = got.shape[0]
    vm = pl.BlockSpec(memory_space=pltpu.VMEM)
    return pl.pallas_call(
        functools.partial(late_kernel, cap, cut),
        out_shape=[
            jax.ShapeDtypeStruct(shape, jnp.bfloat16),
            jax.ShapeDtypeStruct((1, span_y, span_z, channels), jnp.bfloat16),
            jax.ShapeDtypeStruct((span_x, 1, span_z, channels), jnp.bfloat16),
            jax.ShapeDtypeStruct((1, 1, span_z, channels), jnp.bfloat16),
        ],
        in_specs=[pl.BlockSpec(memory_space=pltpu.SMEM), vm, pl.BlockSpec(memory_space=pl.ANY)],
        out_specs=[vm] * 4,
        scratch_shapes=[
            pltpu.VMEM((total, channels), jnp.float32),
            pltpu.SemaphoreType.DMA,
        ] + [pltpu.VMEM((cells + 8, channels), jnp.float32)] * WAYS,
        compiler_params=pltpu.CompilerParams(vmem_limit_bytes=LIMIT),
        name="add_late",
        cost_estimate=pl.CostEstimate(flops=10**8, bytes_accessed=8 * 10**6, transcendentals=0),
    )(slots, got, base)


LIMIT = 48 * 2**20


def residual_kernel(group, level_ref, ylow_ref, yhigh_ref, xlow_ref, xhigh_ref,
                    ll_ref, lh_ref, hl_ref, hh_ref, partial_ref, w_ref, out_ref,
                    plane, taps, wide, result):
    span_x, span_y, span_z, channels = level_ref.shape
    half = (span_y + 2) // 2
    lines = half * span_z
    three = 3 * channels
    for a in range(3):
        for d in range(2):
            for par in range(2):
                for c in range(3):
                    at = ((a * 2 + d) * 2 + par) * three + c * channels
                    for s in range(2):
                        b = 2 * d + par - s
                        if 0 <= b <= 2:
                            tile = w_ref[9 * a + 3 * b + c]
                        else:
                            tile = jnp.zeros((channels, channels), jnp.bfloat16)
                        wide[at:at + channels, s * channels:(s + 1) * channels] = tile
    spot = lax.broadcasted_iota(jnp.int32, ((span_y + 2) * span_z, channels), 0) % span_z
    count = (span_y + 2) * span_z
    plane[0:8, :] = jnp.zeros((8, channels), jnp.float32)
    plane[8 + count:16 + count, :] = jnp.zeros((8, channels), jnp.float32)

    def spread(x):
        middle = plane[8:8 + count, :]
        low = jnp.where(spot == 0, 0.0, plane[7:7 + count, :])
        high = jnp.where(spot == span_z - 1, 0.0, plane[9:9 + count, :])
        for c, value in enumerate((low, middle, high)):
            value = value.astype(jnp.bfloat16).reshape(half, 2, span_z, channels)
            for par in range(2):
                taps[pl.ds(pl.multiple_of(x * lines, 16), lines),
                     par * three + c * channels:par * three + (c + 1) * channels] = (
                    value[:, par].reshape(lines, channels))

    def stage(x, low, middle, high):
        plane[8:8 + span_z, :] = low.reshape(span_z, channels).astype(jnp.float32)
        plane[8 + span_z:8 + count - span_z, :] = middle.reshape(
            span_y * span_z, channels).astype(jnp.float32)
        plane[8 + count - span_z:8 + count, :] = high.reshape(
            span_z, channels).astype(jnp.float32)
        spread(x)

    stage(0, ll_ref[...], xlow_ref[...], lh_ref[...])
    stage(span_x + 1, hl_ref[...], xhigh_ref[...], hh_ref[...])

    def fill(x, carry):
        stage(x + 1, ylow_ref[x], level_ref[x], yhigh_ref[x])
        return carry

    lax.fori_loop(0, span_x, fill, 0)
    height = group * lines - span_z

    def multiply(g, carry):
        total = None
        for a in range(3):
            for d in range(2):
                start = pl.multiple_of((g * group + a) * lines + d * span_z, 16)
                at = (a * 2 + d) * 2 * three
                part = jnp.dot(taps[pl.ds(start, height), :], wide[at:at + 2 * three, :],
                               preferred_element_type=jnp.float32)
                total = part if total is None else total + part
        result[0:height, :] = total
        for i in range(group):
            x = g * group + i
            for s in range(2):
                value = result[i * lines:i * lines + span_y // 2 * span_z,
                               s * channels:(s + 1) * channels]
                value = jnp.maximum(value, 0.0).reshape(span_y // 2, span_z, channels)
                here = level_ref[x].reshape(span_y // 2, 2, span_z, channels)[:, s]
                out_ref[x, :, s] = value + here.astype(jnp.float32) + partial_ref[x, :, s]
        return carry

    lax.fori_loop(0, span_x // group, multiply, 0)


def residual_base(level, faces, partial, w_res, group=4):
    span_x, span_y, span_z, channels = level.shape
    lines = (span_y + 2) // 2 * span_z
    vm = pl.BlockSpec(memory_space=pltpu.VMEM)
    flops = 2 * span_x * span_y * span_z * 27 * channels * channels
    out = pl.pallas_call(
        functools.partial(residual_kernel, group),
        out_shape=jax.ShapeDtypeStruct((span_x, span_y // 2, 2, span_z, channels), jnp.float32),
        in_specs=[vm] * 11,
        out_specs=vm,
        scratch_shapes=[
            pltpu.VMEM(((span_y + 2) * span_z + 16, channels), jnp.float32),
            pltpu.VMEM(((span_x + 2) * lines, 6 * channels), jnp.bfloat16),
            pltpu.VMEM((36 * channels, 2 * channels), jnp.bfloat16),
            pltpu.VMEM((group * lines, 2 * channels), jnp.float32),
        ],
        compiler_params=pltpu.CompilerParams(vmem_limit_bytes=36 * 2**20),
        name="residual",
        cost_estimate=pl.CostEstimate(flops=flops, bytes_accessed=8 * 10**6, transcendentals=0),
    )(level, *faces, partial.reshape(span_x, span_y // 2, 2, span_z, channels), w_res)
    return out.reshape(span_x * span_y * span_z, channels)


def lower_kernel(joined_ref, front_ref, side_ref, corner_ref, w_ref, out_ref, plane, taps):
    span_x, span_y, span_z, channels = joined_ref.shape
    half_y, half_z = span_y // 2, span_z // 2
    lines = half_y * half_z
    count = (span_y + 1) * span_z
    zero = lax.broadcasted_iota(jnp.int32, ((span_y + 1) * half_z, channels), 0) % half_z == 0
    plane[0:8, :] = jnp.zeros((8, channels), jnp.float32)

    def spread(x):
        rows = (span_y + 1) * half_z
        low = jnp.where(zero, 0.0, plane[pl.ds(7, rows, stride=2), :])
        for c, value in enumerate((low, plane[pl.ds(8, rows, stride=2), :],
                                   plane[pl.ds(9, rows, stride=2), :])):
            value = value.reshape(span_y + 1, half_z, channels)
            evens = value[0:span_y].reshape(half_y, 2, half_z, channels)
            odds = value[1:].reshape(half_y, 2, half_z, channels)
            for b, piece in enumerate((evens[:, 0], evens[:, 1], odds[:, 1])):
                at = (b * 3 + c) * channels
                taps[x, :, at:at + channels] = piece.reshape(lines, channels).astype(jnp.bfloat16)

    plane[8:8 + span_z, :] = corner_ref[...].reshape(span_z, channels).astype(jnp.float32)
    plane[8 + span_z:8 + count, :] = front_ref[...].reshape(
        span_y * span_z, channels).astype(jnp.float32)
    spread(0)

    def fill(x, carry):
        plane[8:8 + span_z, :] = side_ref[x].reshape(span_z, channels).astype(jnp.float32)
        plane[8 + span_z:8 + count, :] = joined_ref[x].reshape(
            span_y * span_z, channels).astype(jnp.float32)
        spread(x + 1)
        return carry

    lax.fori_loop(0, span_x, fill, 0)
    depth = 9 * channels

    def multiply(i, carry):
        total = None
        for a in range(3):
            part = jnp.dot(taps[2 * i + a], w_ref[a * depth:(a + 1) * depth, :],
                           preferred_element_type=jnp.float32)
            total = part if total is None else total + part
        out_ref[i] = total.reshape(half_y, half_z, w_ref.shape[-1]).astype(jnp.bfloat16)
        return carry

    lax.fori_loop(0, span_x // 2, multiply, 0)


def lower(joined, front, side, corner, w_down):
    span_x, span_y, span_z, channels = joined.shape
    wide = w_down.shape[-1]
    vm = pl.BlockSpec(memory_space=pltpu.VMEM)
    flops = 2 * span_x * span_y * span_z // 8 * 27 * channels * wide
    return pl.pallas_call(
        lower_kernel,
        out_shape=jax.ShapeDtypeStruct((span_x // 2, span_y // 2, span_z // 2, wide),
                                       jnp.bfloat16),
        in_specs=[vm] * 5,
        out_specs=vm,
        scratch_shapes=[
            pltpu.VMEM(((span_y + 1) * span_z + 16, channels), jnp.float32),
            pltpu.VMEM((span_x + 1, span_y * span_z // 4, 9 * channels), jnp.bfloat16),
        ],
        compiler_params=pltpu.CompilerParams(vmem_limit_bytes=28 * 2**20),
        name="lower",
        cost_estimate=pl.CostEstimate(flops=flops, bytes_accessed=5 * 10**6, transcendentals=0),
    )(joined, front, side, corner, w_down.reshape(-1, wide))


def shifted(array, by_pts, by_nbr):
    count_pts = lax.axis_size("pts")
    count_nbr = lax.axis_size("nbr")
    pairs = [
        (i * count_nbr + j, (i + by_pts) * count_nbr + j + by_nbr)
        for i in range(count_pts)
        for j in range(count_nbr)
        if 0 <= i + by_pts < count_pts and 0 <= j + by_nbr < count_nbr
    ]
    return lax.ppermute(array, ("pts", "nbr"), pairs)


def exchanged(array, devices):
    got = lax.all_to_all(
        array.reshape(devices, -1, array.shape[-1]),
        ("pts", "nbr"),
        split_axis=0,
        concat_axis=0,
        tiled=True,
    )
    return got.reshape(array.shape)


def body(points, dest_owner, dest_cell, level_input, w_res, w_down):
    devices = lax.axis_size("pts") * lax.axis_size("nbr")
    channels = points.shape[-1]
    rows = points.reshape(-1, channels)
    capacity = 2 * rows.shape[0] // devices
    cut = capacity // 2
    cells = math.prod(level_input.shape[:3])
    early, late = pack(
        dest_owner.reshape(-1), dest_cell.reshape(-1), rows, devices, capacity, cut)
    early, late, level = lax.optimization_barrier((early, late, level_input))
    early = exchanged(early, devices)
    faces = [
        shifted(level[:, -1:], 1, 0),
        shifted(level[:, :1], -1, 0),
        shifted(level[-1:], 0, 1),
        shifted(level[:1], 0, -1),
        shifted(level[-1:, -1:], 1, 1),
        shifted(level[-1:, :1], -1, 1),
        shifted(level[:1, -1:], 1, -1),
        shifted(level[:1, :1], -1, -1),
    ]
    late = exchanged(late, devices)
    partial, slots = add_early(early, cells, capacity, cut)
    base = residual_base(level, faces, partial, w_res)
    joined, front, side, corner = add_late(slots, late, base, level.shape, capacity, cut)
    front = shifted(front, 0, 1)
    side = shifted(side, 1, 0)
    corner = shifted(corner, 1, 1)
    return lower(joined, front, side, corner, w_down)


def solution(mesh):
    return jax.shard_map(
        body,
        mesh=mesh,
        in_specs=(
            P("pts", "nbr", None, None),
            P("pts", "nbr", None, None),
            P("pts", "nbr", None),
            P("nbr", "pts", None, None),
            P(),
            P(),
        ),
        out_specs=P("nbr", "pts", None, None),
        check_vma=False,
    )
```

```python
import functools
import jax
import jax.numpy as jnp
from jax import lax
from jax.experimental import pallas as pl
from jax.experimental.pallas import tpu as pltpu
from jax.sharding import PartitionSpec as P


LANES = 128
EXTRA = 8


def pack_kernel(devices, cap, owner_ref, cell_ref, rows_ref, out_ref,
                wide, spread, slot_vmem, slot_smem, sem):
    p_local, _ = rows_ref.shape
    blocks = p_local // LANES
    stride = cap + EXTRA
    upper = (lax.broadcasted_iota(jnp.int32, (LANES, LANES), 0)
             <= lax.broadcasted_iota(jnp.int32, (LANES, LANES), 1)).astype(jnp.bfloat16)
    ids = lax.broadcasted_iota(jnp.int32, (devices, LANES), 0)
    spots = lax.broadcasted_iota(jnp.int32, (cap, LANES), 0)
    base = jnp.zeros((devices, 1), jnp.float32)
    table = jnp.zeros((2 * devices, cap), jnp.float32)
    for b in range(blocks):
        own = owner_ref[b:b + 1, :]
        cell = cell_ref[b:b + 1, :]
        hit = ids == own
        hot = hit.astype(jnp.float32)
        run = jnp.dot(hot.astype(jnp.bfloat16), upper, preferred_element_type=jnp.float32)
        place = jnp.sum(hot * (run + base), axis=0, keepdims=True).astype(jnp.int32) - 1
        base = base + run[:, LANES - 1:LANES]
        slot_vmem[b:b + 1, :] = own * stride + place
        high = jnp.where(hit, (cell // LANES + 1).astype(jnp.float32), 0.0)
        low = jnp.where(hit, (cell % LANES).astype(jnp.float32), 0.0)
        left = jnp.concatenate([high, low], axis=0).astype(jnp.bfloat16)
        right = (spots == place).astype(jnp.float32).astype(jnp.bfloat16)
        table = table + lax.dot_general(left, right, (((1,), (1,)), ((), ())),
                                        preferred_element_type=jnp.float32)
    copy = pltpu.make_async_copy(slot_vmem, slot_smem, sem)
    copy.start()
    wide[...] = rows_ref[...].astype(jnp.float32)
    per = -(-cap // LANES)
    for part in range(2):
        for j in range(per):
            width = min(LANES, cap - j * LANES)
            piece = table[part * devices:(part + 1) * devices, j * LANES:j * LANES + width]
            if width < LANES:
                piece = jnp.concatenate(
                    [piece, jnp.zeros((devices, LANES - width), jnp.float32)], axis=1)
            spread[pl.ds(cap + part * per + j, devices, stride=stride), :] = piece
    copy.wait()

    def step(b, carry):
        for u in range(LANES):
            spread[pl.ds(slot_smem[b, u], 1), :] = wide[pl.ds(b * LANES + u, 1), :]
        return carry

    lax.fori_loop(0, blocks, step, 0)
    out_ref[...] = spread[...].astype(jnp.bfloat16)


def pack(owner, cell, rows, devices, cap):
    p_local, channels = rows.shape
    blocks = p_local // LANES
    total = devices * (cap + EXTRA)
    vm = pl.BlockSpec(memory_space=pltpu.VMEM)
    return pl.pallas_call(
        functools.partial(pack_kernel, devices, cap),
        out_shape=jax.ShapeDtypeStruct((total, channels), jnp.bfloat16),
        in_specs=[vm, vm, vm],
        out_specs=vm,
        scratch_shapes=[
            pltpu.VMEM((p_local, channels), jnp.float32),
            pltpu.VMEM((total, channels), jnp.float32),
            pltpu.VMEM((blocks, LANES), jnp.int32),
            pltpu.SMEM((blocks, LANES), jnp.int32),
            pltpu.SemaphoreType.DMA,
        ],
        name="pack",
        cost_estimate=pl.CostEstimate(flops=10**8, bytes_accessed=4 * 10**6, transcendentals=0),
    )(owner.reshape(blocks, LANES), cell.reshape(blocks, LANES), rows)


WAYS = 6
PIECES = 4
LIMIT = 48 * 2**20


def add_kernel(capacity, got_hbm, base_hbm, ends_ref, edges_ref, out_ref, front_ref, side_ref, corner_ref,
               landed, wide, slot_vmem, slot_smem, sems, *sums):
    span_x, span_y, span_z, channels = out_ref.shape
    cells = span_x * span_y * span_z
    total, _ = landed.shape
    stride = capacity + EXTRA
    devices = total // stride
    per = -(-capacity // LANES)
    width = min(LANES, capacity)
    piece = total // PIECES
    copies = [
        pltpu.make_async_copy(got_hbm.at[pl.ds(i * piece, piece)],
                              landed.at[pl.ds(i * piece, piece)], sems.at[i])
        for i in range(PIECES)
    ]
    for copy in copies:
        copy.start()
    first = pltpu.make_async_copy(base_hbm, sums[0].at[pl.ds(0, cells)], sems.at[PIECES])
    first.start()
    half = len(sums) // 2
    for s in sums[1:half]:
        s[...] = jnp.zeros_like(s)
    for i, copy in enumerate(copies):
        copy.wait()
        wide[i * piece:(i + 1) * piece, :] = landed[i * piece:(i + 1) * piece, :].astype(
            jnp.float32)
    for j in range(per):
        high = wide[pl.ds(capacity + j, devices, stride=stride), :].astype(jnp.int32)
        low = wide[pl.ds(capacity + per + j, devices, stride=stride), :].astype(jnp.int32)
        slot_vmem[j * devices:(j + 1) * devices, :] = jnp.where(
            high > 0, (high - 1) * LANES + low, cells)
    copy = pltpu.make_async_copy(slot_vmem, slot_smem, sems.at[PIECES + 1])
    copy.start()
    for s in sums[max(half, 1):]:
        s[...] = jnp.zeros_like(s)
    copy.wait()
    first.wait()
    for i in range(span_x):
        for k, y in ((0, 0), (1, span_y - 1)):
            start = (i * span_y + y) * span_z
            sums[0][start:start + span_z, :] = edges_ref[k, i]
    for k, x in ((0, 0), (1, span_x - 1)):
        start = x * span_y * span_z
        sums[0][start:start + span_y * span_z, :] = ends_ref[k].reshape(
            span_y * span_z, channels)
    for j in range(per):
        def step(o, carry):
            start = pl.multiple_of(o * stride + j * LANES, 8)
            for u in range(width):
                at = slot_smem[j * devices + o, u]
                s = sums[u % len(sums)]
                s[pl.ds(at, 1), :] += wide[pl.ds(start + u, 1), :]
            return carry

        lax.fori_loop(0, devices, step, 0)

    def finish(x, carry):
        at = pl.ds(pl.multiple_of(x * (span_y * span_z), 8), span_y * span_z)
        value = sums[0][at, :]
        for s in sums[1:]:
            value = value + s[at, :]
        value = value.astype(jnp.bfloat16).reshape(span_y, span_z, channels)
        out_ref[x] = value
        side_ref[x] = value[span_y - 1:]
        return carry

    lax.fori_loop(0, span_x, finish, 0)
    front_ref[...] = out_ref[span_x - 1:]
    corner_ref[...] = out_ref[span_x - 1:, span_y - 1:]


def add_rows(got, base, ends, edges, shape, capacity):
    span_x, span_y, span_z, channels = shape
    cells = span_x * span_y * span_z
    total = got.shape[0]
    devices = total // (capacity + EXTRA)
    per = -(-capacity // LANES)
    vm = pl.BlockSpec(memory_space=pltpu.VMEM)
    hbm = pl.BlockSpec(memory_space=pl.ANY)
    return pl.pallas_call(
        functools.partial(add_kernel, capacity),
        out_shape=[
            jax.ShapeDtypeStruct(shape, jnp.bfloat16),
            jax.ShapeDtypeStruct((1, span_y, span_z, channels), jnp.bfloat16),
            jax.ShapeDtypeStruct((span_x, 1, span_z, channels), jnp.bfloat16),
            jax.ShapeDtypeStruct((1, 1, span_z, channels), jnp.bfloat16),
        ],
        in_specs=[hbm, hbm, vm, vm],
        out_specs=[vm] * 4,
        scratch_shapes=[
            pltpu.VMEM((total, channels), jnp.bfloat16),
            pltpu.VMEM((total, channels), jnp.float32),
            pltpu.VMEM((devices * per, LANES), jnp.int32),
            pltpu.SMEM((devices * per, LANES), jnp.int32),
            pltpu.SemaphoreType.DMA((PIECES + 2,)),
        ] + [pltpu.VMEM((cells + 8, channels), jnp.float32)] * WAYS,
        compiler_params=pltpu.CompilerParams(vmem_limit_bytes=LIMIT),
        name="add_rows",
        cost_estimate=pl.CostEstimate(flops=10**8, bytes_accessed=8 * 10**6, transcendentals=0),
    )(got, base, ends, edges)


def join_taps(w_ref, wide, rows):
    channels = w_ref.shape[-1]
    for r, a in enumerate(rows):
        for d in range(2):
            for par in range(2):
                for c in range(3):
                    at = (((r * 2 + d) * 2 + par) * 3 + c) * channels
                    for s in range(2):
                        b = 2 * d + par - s
                        if 0 <= b <= 2:
                            tile = w_ref[9 * a + 3 * b + c]
                        else:
                            tile = jnp.zeros((channels, channels), jnp.bfloat16)
                        wide[at:at + channels, s * channels:(s + 1) * channels] = tile


def shifts(plane, count, span_z):
    spot = lax.broadcasted_iota(jnp.int32, (count, plane.shape[-1]), 0) % span_z
    middle = plane[8:8 + count, :]
    low = jnp.where(spot == 0, 0.0, plane[7:7 + count, :])
    high = jnp.where(spot == span_z - 1, 0.0, plane[9:9 + count, :])
    return [value.astype(jnp.bfloat16) for value in (low, middle, high)]


def spread_plane(plane, taps, start, half, span_z):
    channels = plane.shape[-1]
    lines = half * span_z
    for c, value in enumerate(shifts(plane, 2 * lines, span_z)):
        value = value.reshape(half, 2, span_z, channels)
        for par in range(2):
            at = (par * 3 + c) * channels
            taps[pl.ds(start, lines), at:at + channels] = value[:, par].reshape(lines, channels)


def residual_kernel(group, level_ref, w_ref, out_ref, ends_ref, edges_ref,
                    plane, taps, wide, result):
    span_x, span_y, span_z, channels = level_ref.shape
    half = (span_y + 2) // 2
    lines = half * span_z
    depth = 6 * channels
    count = (span_y + 2) * span_z
    join_taps(w_ref, wide, (0, 1, 2))
    plane[0:8 + span_z, :] = jnp.zeros((8 + span_z, channels), jnp.float32)
    plane[8 + count - span_z:16 + count, :] = jnp.zeros((8 + span_z, channels), jnp.float32)
    for x in (0, span_x + 1):
        taps[x * lines:(x + 1) * lines, :] = jnp.zeros((lines, depth), jnp.bfloat16)

    def fill(x, carry):
        plane[8 + span_z:8 + count - span_z, :] = level_ref[x].reshape(
            span_y * span_z, channels).astype(jnp.float32)
        spread_plane(plane, taps, pl.multiple_of((x + 1) * lines, 16), half, span_z)
        return carry

    lax.fori_loop(0, span_x, fill, 0)
    height = group * lines - span_z

    def multiply(g, carry):
        total = None
        for a in range(3):
            for d in range(2):
                start = pl.multiple_of((g * group + a) * lines + d * span_z, 16)
                at = (a * 2 + d) * depth
                part = jnp.dot(taps[pl.ds(start, height), :], wide[at:at + depth, :],
                               preferred_element_type=jnp.float32)
                total = part if total is None else total + part
        result[0:height, :] = total
        for i in range(group):
            x = g * group + i
            for s in range(2):
                value = result[i * lines:i * lines + span_y // 2 * span_z,
                               s * channels:(s + 1) * channels]
                value = value.reshape(span_y // 2, span_z, channels)
                edges_ref[s, x] = value[s * (span_y // 2 - 1)]
                if i == 0:
                    @pl.when(g == 0)
                    def _():
                        ends_ref[0, :, s] = value

                if i == group - 1:
                    @pl.when(x == span_x - 1)
                    def _():
                        ends_ref[1, :, s] = value

                here = level_ref[x].reshape(span_y // 2, 2, span_z, channels)[:, s]
                out_ref[x, :, s] = jnp.maximum(value, 0.0) + here.astype(jnp.float32)
        return carry

    lax.fori_loop(0, span_x // group, multiply, 0)


def residual_base(level, w_res, group=4):
    span_x, span_y, span_z, channels = level.shape
    lines = (span_y + 2) // 2 * span_z
    vm = pl.BlockSpec(memory_space=pltpu.VMEM)
    flops = 2 * span_x * span_y * span_z * 27 * channels * channels
    pairs = (span_y // 2, 2, span_z, channels)
    return pl.pallas_call(
        functools.partial(residual_kernel, group),
        out_shape=[
            jax.ShapeDtypeStruct((span_x,) + pairs, jnp.float32),
            jax.ShapeDtypeStruct((2,) + pairs, jnp.float32),
            jax.ShapeDtypeStruct((2, span_x, span_z, channels), jnp.float32),
        ],
        in_specs=[vm] * 2,
        out_specs=[vm] * 3,
        scratch_shapes=[
            pltpu.VMEM(((span_y + 2) * span_z + 16, channels), jnp.float32),
            pltpu.VMEM(((span_x + 2) * lines, 6 * channels), jnp.bfloat16),
            pltpu.VMEM((36 * channels, 2 * channels), jnp.bfloat16),
            pltpu.VMEM((group * lines, 2 * channels), jnp.float32),
        ],
        compiler_params=pltpu.CompilerParams(vmem_limit_bytes=36 * 2**20),
        name="residual",
        cost_estimate=pl.CostEstimate(flops=flops, bytes_accessed=8 * 10**6, transcendentals=0),
    )(level, w_res)


def border_kernel(ends_ref, edges_ref, xfirst_ref, xlast_ref, yfirst_ref, ylast_ref,
                  xlow_ref, xhigh_ref, ylow_ref, yhigh_ref, ll_ref, lh_ref, hl_ref, hh_ref,
                  w_ref, new_ends_ref, new_edges_ref, plane, taps, wide):
    _, half_y, _, span_z, channels = ends_ref.shape
    span_x = edges_ref.shape[1]
    span_y = 2 * half_y
    count = (span_y + 2) * span_z
    depth = 6 * channels
    join_taps(w_ref, wide, (0, 2))
    plane[0:8, :] = jnp.zeros((8, channels), jnp.float32)
    plane[8 + count:16 + count, :] = jnp.zeros((8, channels), jnp.float32)
    for k, (low, middle, high) in enumerate(
            ((ll_ref, xlow_ref, lh_ref), (hl_ref, xhigh_ref, hh_ref))):
        plane[8:8 + span_z, :] = low[...].reshape(span_z, channels).astype(jnp.float32)
        plane[8 + span_z:8 + count - span_z, :] = middle[...].reshape(
            span_y * span_z, channels).astype(jnp.float32)
        plane[8 + count - span_z:8 + count, :] = high[...].reshape(
            span_z, channels).astype(jnp.float32)
        spread_plane(plane, taps, 0, half_y + 1, span_z)
        change = None
        for d in range(2):
            at = (k * 2 + d) * depth
            part = jnp.dot(taps[d * span_z:(d + half_y) * span_z, :], wide[at:at + depth, :],
                           preferred_element_type=jnp.float32)
            change = part if change is None else change + part
        for s in range(2):
            value = change[:, s * channels:(s + 1) * channels].reshape(
                half_y, span_z, channels)
            new_ends_ref[k, :, s] = ends_ref[k, :, s] + value
    rows = (span_x + 2) * span_z
    for k, (source, here) in enumerate(((ylow_ref, yfirst_ref), (yhigh_ref, ylast_ref))):
        plane[8:8 + span_z, :] = jnp.zeros((span_z, channels), jnp.float32)
        plane[8 + span_z:8 + rows - span_z, :] = source[...].reshape(
            span_x * span_z, channels).astype(jnp.float32)
        plane[8 + rows - span_z:16 + rows, :] = jnp.zeros((span_z + 8, channels), jnp.float32)
        for c, value in enumerate(shifts(plane, rows, span_z)):
            taps[0:rows, c * channels:(c + 1) * channels] = value
        change = None
        for a in range(3):
            first = 9 * a + 3 * (2 * k)
            part = jnp.dot(taps[a * span_z:(a + span_x) * span_z, 0:3 * channels],
                           w_ref[first:first + 3].reshape(3 * channels, channels),
                           preferred_element_type=jnp.float32)
            change = part if change is None else change + part
        change = change.reshape(span_x, span_z, channels)
        new_edges_ref[k] = jnp.maximum(edges_ref[k] + change, 0.0) + here[...].reshape(
            span_x, span_z, channels).astype(jnp.float32)
        for e, x in ((0, 0), (1, span_x - 1)):
            new_ends_ref[e, k * (half_y - 1), k] = new_ends_ref[e, k * (half_y - 1), k] + change[x]
    for e, here in enumerate((xfirst_ref, xlast_ref)):
        new_ends_ref[e] = jnp.maximum(new_ends_ref[e], 0.0) + here[...].reshape(
            half_y, 2, span_z, channels).astype(jnp.float32)


def border(ends, edges, own, faces, w_res):
    _, half_y, _, span_z, channels = ends.shape
    span_x = edges.shape[1]
    rows = max((half_y + 1), (span_x + 2)) * span_z
    vm = pl.BlockSpec(memory_space=pltpu.VMEM)
    return pl.pallas_call(
        border_kernel,
        out_shape=[jax.ShapeDtypeStruct(ends.shape, jnp.float32),
                   jax.ShapeDtypeStruct(edges.shape, jnp.float32)],
        in_specs=[vm] * 15,
        out_specs=[vm] * 2,
        scratch_shapes=[
            pltpu.VMEM((2 * rows + 16, channels), jnp.float32),
            pltpu.VMEM((rows, 6 * channels), jnp.bfloat16),
            pltpu.VMEM((24 * channels, 2 * channels), jnp.bfloat16),
        ],
        compiler_params=pltpu.CompilerParams(vmem_limit_bytes=24 * 2**20),
        name="border",
        cost_estimate=pl.CostEstimate(flops=10**9, bytes_accessed=3 * 10**6, transcendentals=0),
    )(ends, edges, *own, *faces, w_res)


def lower_kernel(joined_ref, front_ref, side_ref, corner_ref, w_ref, out_ref, plane, taps):
    span_x, span_y, span_z, channels = joined_ref.shape
    half_y, half_z = span_y // 2, span_z // 2
    lines = half_y * half_z
    count = (span_y + 1) * span_z
    zero = lax.broadcasted_iota(jnp.int32, ((span_y + 1) * half_z, channels), 0) % half_z == 0
    plane[0:8, :] = jnp.zeros((8, channels), jnp.float32)

    def spread(x):
        rows = (span_y + 1) * half_z
        low = jnp.where(zero, 0.0, plane[pl.ds(7, rows, stride=2), :])
        for c, value in enumerate((low, plane[pl.ds(8, rows, stride=2), :],
                                   plane[pl.ds(9, rows, stride=2), :])):
            value = value.reshape(span_y + 1, half_z, channels)
            evens = value[0:span_y].reshape(half_y, 2, half_z, channels)
            odds = value[1:].reshape(half_y, 2, half_z, channels)
            for b, piece in enumerate((evens[:, 0], evens[:, 1], odds[:, 1])):
                at = (b * 3 + c) * channels
                taps[x, :, at:at + channels] = piece.reshape(lines, channels).astype(jnp.bfloat16)

    plane[8:8 + span_z, :] = corner_ref[...].reshape(span_z, channels).astype(jnp.float32)
    plane[8 + span_z:8 + count, :] = front_ref[...].reshape(
        span_y * span_z, channels).astype(jnp.float32)
    spread(0)

    def fill(x, carry):
        plane[8:8 + span_z, :] = side_ref[x].reshape(span_z, channels).astype(jnp.float32)
        plane[8 + span_z:8 + count, :] = joined_ref[x].reshape(
            span_y * span_z, channels).astype(jnp.float32)
        spread(x + 1)
        return carry

    lax.fori_loop(0, span_x, fill, 0)
    depth = 9 * channels

    def multiply(i, carry):
        total = None
        for a in range(3):
            part = jnp.dot(taps[2 * i + a], w_ref[a * depth:(a + 1) * depth, :],
                           preferred_element_type=jnp.float32)
            total = part if total is None else total + part
        out_ref[i] = total.reshape(half_y, half_z, w_ref.shape[-1]).astype(jnp.bfloat16)
        return carry

    lax.fori_loop(0, span_x // 2, multiply, 0)


def lower(joined, front, side, corner, w_down):
    span_x, span_y, span_z, channels = joined.shape
    wide = w_down.shape[-1]
    vm = pl.BlockSpec(memory_space=pltpu.VMEM)
    flops = 2 * span_x * span_y * span_z // 8 * 27 * channels * wide
    return pl.pallas_call(
        lower_kernel,
        out_shape=jax.ShapeDtypeStruct((span_x // 2, span_y // 2, span_z // 2, wide),
                                       jnp.bfloat16),
        in_specs=[vm] * 5,
        out_specs=vm,
        scratch_shapes=[
            pltpu.VMEM(((span_y + 1) * span_z + 16, channels), jnp.float32),
            pltpu.VMEM((span_x + 1, span_y * span_z // 4, 9 * channels), jnp.bfloat16),
        ],
        compiler_params=pltpu.CompilerParams(vmem_limit_bytes=28 * 2**20),
        name="lower",
        cost_estimate=pl.CostEstimate(flops=flops, bytes_accessed=5 * 10**6, transcendentals=0),
    )(joined, front, side, corner, w_down.reshape(-1, wide))


def shifted(array, by_pts, by_nbr):
    count_pts = lax.axis_size("pts")
    count_nbr = lax.axis_size("nbr")
    pairs = [
        (i * count_nbr + j, (i + by_pts) * count_nbr + j + by_nbr)
        for i in range(count_pts)
        for j in range(count_nbr)
        if 0 <= i + by_pts < count_pts and 0 <= j + by_nbr < count_nbr
    ]
    return lax.ppermute(array, ("pts", "nbr"), pairs)


def exchanged(array, devices):
    got = lax.all_to_all(
        array.reshape(devices, -1, array.shape[-1]),
        ("pts", "nbr"),
        split_axis=0,
        concat_axis=0,
        tiled=True,
    )
    return got.reshape(array.shape)


def body(points, dest_owner, dest_cell, level_input, w_res, w_down):
    devices = lax.axis_size("pts") * lax.axis_size("nbr")
    channels = points.shape[-1]
    rows = points.reshape(-1, channels)
    capacity = 2 * rows.shape[0] // devices
    outgoing = pack(dest_owner.reshape(-1), dest_cell.reshape(-1), rows, devices, capacity)
    outgoing, level = lax.optimization_barrier((outgoing, level_input))
    got = exchanged(outgoing, devices)
    x_first, x_last = level[:1], level[-1:]
    y_first, y_last = level[:, :1], level[:, -1:]
    faces = [
        shifted(x_last, 0, 1),
        shifted(x_first, 0, -1),
        shifted(y_last, 1, 0),
        shifted(y_first, -1, 0),
        shifted(level[-1:, -1:], 1, 1),
        shifted(level[-1:, :1], -1, 1),
        shifted(level[:1, -1:], 1, -1),
        shifted(level[:1, :1], -1, -1),
    ]
    base, ends, edges = residual_base(level, w_res)
    ends, edges = border(ends, edges, (x_first, x_last, y_first, y_last), faces, w_res)
    joined, front, side, corner = add_rows(
        got, base.reshape(-1, channels), ends, edges, level.shape, capacity)
    front = shifted(front, 0, 1)
    side = shifted(side, 1, 0)
    corner = shifted(corner, 1, 1)
    return lower(joined, front, side, corner, w_down)


def solution(mesh):
    return jax.shard_map(
        body,
        mesh=mesh,
        in_specs=(
            P("pts", "nbr", None, None),
            P("pts", "nbr", None, None),
            P("pts", "nbr", None),
            P("nbr", "pts", None, None),
            P(),
            P(),
        ),
        out_specs=P("nbr", "pts", None, None),
        check_vma=False,
    )
```

```python
import functools
import jax
import jax.numpy as jnp
from jax import lax
from jax.experimental import pallas as pl
from jax.experimental.pallas import tpu as pltpu
from jax.sharding import PartitionSpec as P


LANES = 128
EXTRA = 8
PIECES = 4


def pack_kernel(devices, cap, owner_ref, cell_ref, rows_hbm, out_hbm,
                rows_ref, wide, spread, staged, slot_vmem, slot_smem, sems):
    p_local, _ = rows_ref.shape
    fetch = pltpu.make_async_copy(rows_hbm, rows_ref, sems.at[PIECES + 1])
    fetch.start()
    blocks = p_local // LANES
    stride = cap + EXTRA
    upper = (lax.broadcasted_iota(jnp.int32, (LANES, LANES), 0)
             <= lax.broadcasted_iota(jnp.int32, (LANES, LANES), 1)).astype(jnp.bfloat16)
    ids = lax.broadcasted_iota(jnp.int32, (devices, LANES), 0)
    spots = lax.broadcasted_iota(jnp.int32, (cap, LANES), 0)
    base = jnp.zeros((devices, 1), jnp.float32)
    table = jnp.zeros((2 * devices, cap), jnp.float32)
    for b in range(blocks):
        own = owner_ref[b:b + 1, :]
        cell = cell_ref[b:b + 1, :]
        hit = ids == own
        hot = hit.astype(jnp.float32)
        run = jnp.dot(hot.astype(jnp.bfloat16), upper, preferred_element_type=jnp.float32)
        place = jnp.sum(hot * (run + base), axis=0, keepdims=True).astype(jnp.int32) - 1
        base = base + run[:, LANES - 1:LANES]
        slot_vmem[b:b + 1, :] = own * stride + place
        high = jnp.where(hit, (cell // LANES + 1).astype(jnp.float32), 0.0)
        low = jnp.where(hit, (cell % LANES).astype(jnp.float32), 0.0)
        left = jnp.concatenate([high, low], axis=0).astype(jnp.bfloat16)
        right = (spots == place).astype(jnp.float32).astype(jnp.bfloat16)
        table = table + lax.dot_general(left, right, (((1,), (1,)), ((), ())),
                                        preferred_element_type=jnp.float32)
    copy = pltpu.make_async_copy(slot_vmem, slot_smem, sems.at[PIECES])
    copy.start()
    fetch.wait()
    wide[...] = rows_ref[...].astype(jnp.float32)
    per = -(-cap // LANES)
    for part in range(2):
        for j in range(per):
            width = min(LANES, cap - j * LANES)
            piece = table[part * devices:(part + 1) * devices, j * LANES:j * LANES + width]
            if width < LANES:
                piece = jnp.concatenate(
                    [piece, jnp.zeros((devices, LANES - width), jnp.float32)], axis=1)
            spread[pl.ds(cap + part * per + j, devices, stride=stride), :] = piece
    copy.wait()

    def step(b, carry):
        for u in range(LANES):
            spread[pl.ds(slot_smem[b, u], 1), :] = wide[pl.ds(b * LANES + u, 1), :]
        return carry

    lax.fori_loop(0, blocks, step, 0)
    piece = staged.shape[0] // PIECES
    sends = []
    for i in range(PIECES):
        part = pl.ds(i * piece, piece)
        staged[part, :] = spread[part, :].astype(jnp.bfloat16)
        sends.append(pltpu.make_async_copy(staged.at[part], out_hbm.at[part], sems.at[i]))
        sends[-1].start()
    for send in sends:
        send.wait()


def pack(owner, cell, rows, devices, cap):
    p_local, channels = rows.shape
    blocks = p_local // LANES
    total = devices * (cap + EXTRA)
    vm = pl.BlockSpec(memory_space=pltpu.VMEM)
    hbm = pl.BlockSpec(memory_space=pl.ANY)
    return pl.pallas_call(
        functools.partial(pack_kernel, devices, cap),
        out_shape=jax.ShapeDtypeStruct((total, channels), jnp.bfloat16),
        in_specs=[vm, vm, hbm],
        out_specs=hbm,
        scratch_shapes=[
            pltpu.VMEM((p_local, channels), jnp.bfloat16),
            pltpu.VMEM((p_local, channels), jnp.float32),
            pltpu.VMEM((total, channels), jnp.float32),
            pltpu.VMEM((total, channels), jnp.bfloat16),
            pltpu.VMEM((blocks, LANES), jnp.int32),
            pltpu.SMEM((blocks, LANES), jnp.int32),
            pltpu.SemaphoreType.DMA((PIECES + 2,)),
        ],
        name="pack",
        cost_estimate=pl.CostEstimate(flops=10**8, bytes_accessed=4 * 10**6, transcendentals=0),
    )(owner.reshape(blocks, LANES), cell.reshape(blocks, LANES), rows)


WAYS = 6


def add_kernel(capacity, got_ref, base_hbm, ends_ref, edges_ref, out_ref, front_ref, side_ref,
               corner_ref, wide, slot_vmem, slot_smem, sems, *sums):
    span_x, span_y, span_z, channels = out_ref.shape
    cells = span_x * span_y * span_z
    total, _ = got_ref.shape
    stride = capacity + EXTRA
    devices = total // stride
    per = -(-capacity // LANES)
    width = min(LANES, capacity)
    area = span_y * span_z
    first = pltpu.make_async_copy(base_hbm, sums[0].at[pl.ds(0, cells)], sems.at[0])
    first.start()
    wide[...] = got_ref[...].astype(jnp.float32)
    for j in range(per):
        high = wide[pl.ds(capacity + j, devices, stride=stride), :].astype(jnp.int32)
        low = wide[pl.ds(capacity + per + j, devices, stride=stride), :].astype(jnp.int32)
        slot_vmem[j * devices:(j + 1) * devices, :] = jnp.where(
            high > 0, (high - 1) * LANES + low, cells)
    copy = pltpu.make_async_copy(slot_vmem, slot_smem, sems.at[1])
    copy.start()
    for s in sums[1:]:
        s[...] = jnp.zeros_like(s)
    first.wait()
    for x in range(span_x):
        sums[0][x * area:x * area + span_z, :] = edges_ref[0, x]
        sums[0][(x + 1) * area - span_z:(x + 1) * area, :] = edges_ref[1, x]
    for k, x in ((0, 0), (1, span_x - 1)):
        sums[0][x * area:(x + 1) * area, :] = ends_ref[k].reshape(area, channels)
    copy.wait()
    for j in range(per):
        def step(o, carry):
            start = pl.multiple_of(o * stride + j * LANES, 8)
            for u in range(width):
                at = slot_smem[j * devices + o, u]
                s = sums[u % len(sums)]
                s[pl.ds(at, 1), :] += wide[pl.ds(start + u, 1), :]
            return carry

        lax.fori_loop(0, devices, step, 0)

    def finish(x, carry):
        at = pl.ds(pl.multiple_of(x * area, 8), area)
        value = sums[0][at, :]
        for s in sums[1:]:
            value = value + s[at, :]
        value = value.astype(jnp.bfloat16).reshape(span_y, span_z, channels)
        out_ref[x] = value
        side_ref[x] = value[span_y - 1:]
        return carry

    lax.fori_loop(0, span_x, finish, 0)
    front_ref[...] = out_ref[span_x - 1:]
    corner_ref[...] = out_ref[span_x - 1:, span_y - 1:]


def add_rows(got, base, ends, edges, shape, capacity):
    span_x, span_y, span_z, channels = shape
    cells = span_x * span_y * span_z
    total = got.shape[0]
    devices = total // (capacity + EXTRA)
    per = -(-capacity // LANES)
    vm = pl.BlockSpec(memory_space=pltpu.VMEM)
    return pl.pallas_call(
        functools.partial(add_kernel, capacity),
        out_shape=[
            jax.ShapeDtypeStruct(shape, jnp.bfloat16),
            jax.ShapeDtypeStruct((1, span_y, span_z, channels), jnp.bfloat16),
            jax.ShapeDtypeStruct((span_x, 1, span_z, channels), jnp.bfloat16),
            jax.ShapeDtypeStruct((1, 1, span_z, channels), jnp.bfloat16),
        ],
        in_specs=[vm, pl.BlockSpec(memory_space=pl.ANY), vm, vm],
        out_specs=[vm] * 4,
        scratch_shapes=[
            pltpu.VMEM((total, channels), jnp.float32),
            pltpu.VMEM((devices * per, LANES), jnp.int32),
            pltpu.SMEM((devices * per, LANES), jnp.int32),
            pltpu.SemaphoreType.DMA((2,)),
        ] + [pltpu.VMEM((cells + 8, channels), jnp.float32)] * WAYS,
        compiler_params=pltpu.CompilerParams(vmem_limit_bytes=LIMIT),
        name="add_rows",
        cost_estimate=pl.CostEstimate(flops=10**8, bytes_accessed=8 * 10**6, transcendentals=0),
    )(got, base, ends, edges)


LIMIT = 48 * 2**20


def join_taps(w_ref, wide, rows):
    channels = w_ref.shape[-1]
    for r, a in enumerate(rows):
        for d in range(2):
            for par in range(2):
                for c in range(3):
                    at = (((r * 2 + d) * 2 + par) * 3 + c) * channels
                    for s in range(2):
                        b = 2 * d + par - s
                        if 0 <= b <= 2:
                            tile = w_ref[9 * a + 3 * b + c]
                        else:
                            tile = jnp.zeros((channels, channels), jnp.bfloat16)
                        wide[at:at + channels, s * channels:(s + 1) * channels] = tile


def shifts(plane, count, span_z):
    spot = lax.broadcasted_iota(jnp.int32, (count, plane.shape[-1]), 0) % span_z
    middle = plane[8:8 + count, :]
    low = jnp.where(spot == 0, 0.0, plane[7:7 + count, :])
    high = jnp.where(spot == span_z - 1, 0.0, plane[9:9 + count, :])
    return [value.astype(jnp.bfloat16) for value in (low, middle, high)]


def spread_plane(plane, taps, start, half, span_z):
    channels = plane.shape[-1]
    lines = half * span_z
    for c, value in enumerate(shifts(plane, 2 * lines, span_z)):
        value = value.reshape(half, 2, span_z, channels)
        for par in range(2):
            at = (par * 3 + c) * channels
            taps[pl.ds(start, lines), at:at + channels] = value[:, par].reshape(lines, channels)


def residual_kernel(group, level_ref, w_ref, out_ref, ends_ref, edges_ref,
                    plane, taps, wide, result):
    span_x, span_y, span_z, channels = level_ref.shape
    half = (span_y + 2) // 2
    lines = half * span_z
    depth = 6 * channels
    count = (span_y + 2) * span_z
    join_taps(w_ref, wide, (0, 1, 2))
    plane[0:8 + span_z, :] = jnp.zeros((8 + span_z, channels), jnp.float32)
    plane[8 + count - span_z:16 + count, :] = jnp.zeros((8 + span_z, channels), jnp.float32)
    for x in (0, span_x + 1):
        taps[x * lines:(x + 1) * lines, :] = jnp.zeros((lines, depth), jnp.bfloat16)

    def fill(x, carry):
        plane[8 + span_z:8 + count - span_z, :] = level_ref[x].reshape(
            span_y * span_z, channels).astype(jnp.float32)
        spread_plane(plane, taps, pl.multiple_of((x + 1) * lines, 16), half, span_z)
        return carry

    lax.fori_loop(0, span_x, fill, 0)
    height = group * lines - span_z

    def multiply(g, carry):
        total = None
        for a in range(3):
            for d in range(2):
                start = pl.multiple_of((g * group + a) * lines + d * span_z, 16)
                at = (a * 2 + d) * depth
                part = jnp.dot(taps[pl.ds(start, height), :], wide[at:at + depth, :],
                               preferred_element_type=jnp.float32)
                total = part if total is None else total + part
        result[0:height, :] = total
        for i in range(group):
            x = g * group + i
            for s in range(2):
                value = result[i * lines:i * lines + span_y // 2 * span_z,
                               s * channels:(s + 1) * channels]
                value = value.reshape(span_y // 2, span_z, channels)
                edges_ref[s, x] = value[s * (span_y // 2 - 1)]
                if i == 0:
                    @pl.when(g == 0)
                    def _():
                        ends_ref[0, :, s] = value

                if i == group - 1:
                    @pl.when(x == span_x - 1)
                    def _():
                        ends_ref[1, :, s] = value

                here = level_ref[x].reshape(span_y // 2, 2, span_z, channels)[:, s]
                out_ref[x, :, s] = jnp.maximum(value, 0.0) + here.astype(jnp.float32)
        return carry

    lax.fori_loop(0, span_x // group, multiply, 0)


def residual_base(level, w_res, group=4):
    span_x, span_y, span_z, channels = level.shape
    lines = (span_y + 2) // 2 * span_z
    vm = pl.BlockSpec(memory_space=pltpu.VMEM)
    flops = 2 * span_x * span_y * span_z * 27 * channels * channels
    pairs = (span_y // 2, 2, span_z, channels)
    return pl.pallas_call(
        functools.partial(residual_kernel, group),
        out_shape=[
            jax.ShapeDtypeStruct((span_x,) + pairs, jnp.float32),
            jax.ShapeDtypeStruct((2,) + pairs, jnp.float32),
            jax.ShapeDtypeStruct((2, span_x, span_z, channels), jnp.float32),
        ],
        in_specs=[vm] * 2,
        out_specs=[vm] * 3,
        scratch_shapes=[
            pltpu.VMEM(((span_y + 2) * span_z + 16, channels), jnp.float32),
            pltpu.VMEM(((span_x + 2) * lines, 6 * channels), jnp.bfloat16),
            pltpu.VMEM((36 * channels, 2 * channels), jnp.bfloat16),
            pltpu.VMEM((group * lines, 2 * channels), jnp.float32),
        ],
        compiler_params=pltpu.CompilerParams(vmem_limit_bytes=26 * 2**20),
        name="residual",
        cost_estimate=pl.CostEstimate(flops=flops, bytes_accessed=8 * 10**6, transcendentals=0),
    )(level, w_res)


def border_kernel(ends_ref, edges_ref, xfirst_ref, xlast_ref, yfirst_ref, ylast_ref,
                  xlow_ref, xhigh_ref, ylow_ref, yhigh_ref, ll_ref, lh_ref, hl_ref, hh_ref,
                  w_ref, new_ends_ref, new_edges_ref, plane, taps, wide):
    _, half_y, _, span_z, channels = ends_ref.shape
    span_x = edges_ref.shape[1]
    span_y = 2 * half_y
    count = (span_y + 2) * span_z
    depth = 6 * channels
    join_taps(w_ref, wide, (0, 2))
    plane[0:8, :] = jnp.zeros((8, channels), jnp.float32)
    plane[8 + count:16 + count, :] = jnp.zeros((8, channels), jnp.float32)
    for k, (low, middle, high) in enumerate(
            ((ll_ref, xlow_ref, lh_ref), (hl_ref, xhigh_ref, hh_ref))):
        plane[8:8 + span_z, :] = low[...].reshape(span_z, channels).astype(jnp.float32)
        plane[8 + span_z:8 + count - span_z, :] = middle[...].reshape(
            span_y * span_z, channels).astype(jnp.float32)
        plane[8 + count - span_z:8 + count, :] = high[...].reshape(
            span_z, channels).astype(jnp.float32)
        spread_plane(plane, taps, 0, half_y + 1, span_z)
        change = None
        for d in range(2):
            at = (k * 2 + d) * depth
            part = jnp.dot(taps[d * span_z:(d + half_y) * span_z, :], wide[at:at + depth, :],
                           preferred_element_type=jnp.float32)
            change = part if change is None else change + part
        for s in range(2):
            value = change[:, s * channels:(s + 1) * channels].reshape(
                half_y, span_z, channels)
            new_ends_ref[k, :, s] = ends_ref[k, :, s] + value
    rows = (span_x + 2) * span_z
    for k, (source, here) in enumerate(((ylow_ref, yfirst_ref), (yhigh_ref, ylast_ref))):
        plane[8:8 + span_z, :] = jnp.zeros((span_z, channels), jnp.float32)
        plane[8 + span_z:8 + rows - span_z, :] = source[...].reshape(
            span_x * span_z, channels).astype(jnp.float32)
        plane[8 + rows - span_z:16 + rows, :] = jnp.zeros((span_z + 8, channels), jnp.float32)
        for c, value in enumerate(shifts(plane, rows, span_z)):
            taps[0:rows, c * channels:(c + 1) * channels] = value
        change = None
        for a in range(3):
            first = 9 * a + 3 * (2 * k)
            part = jnp.dot(taps[a * span_z:(a + span_x) * span_z, 0:3 * channels],
                           w_ref[first:first + 3].reshape(3 * channels, channels),
                           preferred_element_type=jnp.float32)
            change = part if change is None else change + part
        change = change.reshape(span_x, span_z, channels)
        new_edges_ref[k] = jnp.maximum(edges_ref[k] + change, 0.0) + here[...].reshape(
            span_x, span_z, channels).astype(jnp.float32)
        for e, x in ((0, 0), (1, span_x - 1)):
            new_ends_ref[e, k * (half_y - 1), k] = new_ends_ref[e, k * (half_y - 1), k] + change[x]
    for e, here in enumerate((xfirst_ref, xlast_ref)):
        new_ends_ref[e] = jnp.maximum(new_ends_ref[e], 0.0) + here[...].reshape(
            half_y, 2, span_z, channels).astype(jnp.float32)


def border(ends, edges, own, faces, w_res):
    _, half_y, _, span_z, channels = ends.shape
    span_x = edges.shape[1]
    rows = max((half_y + 1), (span_x + 2)) * span_z
    vm = pl.BlockSpec(memory_space=pltpu.VMEM)
    return pl.pallas_call(
        border_kernel,
        out_shape=[jax.ShapeDtypeStruct(ends.shape, jnp.float32),
                   jax.ShapeDtypeStruct(edges.shape, jnp.float32)],
        in_specs=[vm] * 15,
        out_specs=[vm] * 2,
        scratch_shapes=[
            pltpu.VMEM((2 * rows + 16, channels), jnp.float32),
            pltpu.VMEM((rows, 6 * channels), jnp.bfloat16),
            pltpu.VMEM((24 * channels, 2 * channels), jnp.bfloat16),
        ],
        compiler_params=pltpu.CompilerParams(vmem_limit_bytes=8 * 2**20),
        name="border",
        cost_estimate=pl.CostEstimate(flops=10**9, bytes_accessed=3 * 10**6, transcendentals=0),
    )(ends, edges, *own, *faces, w_res)


def lower_kernel(joined_ref, front_ref, side_ref, corner_ref, w_ref, out_ref, planes, taps):
    span_x, span_y, span_z, channels = joined_ref.shape
    half_y, half_z = span_y // 2, span_z // 2
    lines = half_y * half_z
    count = (span_y + 1) * span_z
    rows = (span_y + 1) * half_z
    depth = 9 * channels
    zero = lax.broadcasted_iota(jnp.int32, (rows, channels), 0) % half_z == 0
    for k in range(2):
        planes[k, 0:8, :] = jnp.zeros((8, channels), jnp.float32)

    def fill(x, first, rest):
        plane = planes.at[x % 2]
        plane[8:8 + span_z, :] = first.reshape(span_z, channels).astype(jnp.float32)
        plane[8 + span_z:8 + count, :] = rest.reshape(
            span_y * span_z, channels).astype(jnp.float32)
        low = jnp.where(zero, 0.0, plane[pl.ds(7, rows, stride=2), :])
        for c, value in enumerate((low, plane[pl.ds(8, rows, stride=2), :],
                                   plane[pl.ds(9, rows, stride=2), :])):
            value = value.reshape(span_y + 1, half_z, channels)
            evens = value[0:span_y].reshape(half_y, 2, half_z, channels)
            odds = value[1:].reshape(half_y, 2, half_z, channels)
            for b, piece in enumerate((evens[:, 0], evens[:, 1], odds[:, 1])):
                at = (b * 3 + c) * channels
                taps[x, :, at:at + channels] = piece.reshape(lines, channels).astype(jnp.bfloat16)

    def multiply(i):
        total = None
        for a in range(3):
            part = jnp.dot(taps[2 * i + a], w_ref[a * depth:(a + 1) * depth, :],
                           preferred_element_type=jnp.float32)
            total = part if total is None else total + part
        out_ref[i] = total.reshape(half_y, half_z, w_ref.shape[-1]).astype(jnp.bfloat16)

    fill(0, corner_ref[...], front_ref[...])
    for x in range(1, span_x + 1):
        fill(x, side_ref[x - 1], joined_ref[x - 1])
        if x % 2 == 0:
            multiply(x // 2 - 1)


def lower(joined, front, side, corner, w_down):
    span_x, span_y, span_z, channels = joined.shape
    wide = w_down.shape[-1]
    vm = pl.BlockSpec(memory_space=pltpu.VMEM)
    flops = 2 * span_x * span_y * span_z // 8 * 27 * channels * wide
    return pl.pallas_call(
        lower_kernel,
        out_shape=jax.ShapeDtypeStruct((span_x // 2, span_y // 2, span_z // 2, wide),
                                       jnp.bfloat16),
        in_specs=[vm] * 5,
        out_specs=vm,
        scratch_shapes=[
            pltpu.VMEM((2, (span_y + 1) * span_z + 16, channels), jnp.float32),
            pltpu.VMEM((span_x + 1, span_y * span_z // 4, 9 * channels), jnp.bfloat16),
        ],
        compiler_params=pltpu.CompilerParams(vmem_limit_bytes=28 * 2**20),
        name="lower",
        cost_estimate=pl.CostEstimate(flops=flops, bytes_accessed=5 * 10**6, transcendentals=0),
    )(joined, front, side, corner, w_down.reshape(-1, wide))


def shifted(array, by_pts, by_nbr):
    count_pts = lax.axis_size("pts")
    count_nbr = lax.axis_size("nbr")
    pairs = [
        (i * count_nbr + j, (i + by_pts) * count_nbr + j + by_nbr)
        for i in range(count_pts)
        for j in range(count_nbr)
        if 0 <= i + by_pts < count_pts and 0 <= j + by_nbr < count_nbr
    ]
    return lax.ppermute(array, ("pts", "nbr"), pairs)


def exchanged(array, devices):
    got = lax.all_to_all(
        array.reshape(devices, -1, array.shape[-1]),
        ("pts", "nbr"),
        split_axis=0,
        concat_axis=0,
        tiled=True,
    )
    return got.reshape(array.shape)


def body(points, dest_owner, dest_cell, level_input, w_res, w_down):
    devices = lax.axis_size("pts") * lax.axis_size("nbr")
    channels = points.shape[-1]
    rows = points.reshape(-1, channels)
    capacity = 2 * rows.shape[0] // devices
    outgoing = pack(dest_owner.reshape(-1), dest_cell.reshape(-1), rows, devices, capacity)
    outgoing, level = lax.optimization_barrier((outgoing, level_input))
    got = exchanged(outgoing, devices)
    x_first, x_last = level[:1], level[-1:]
    y_first, y_last = level[:, :1], level[:, -1:]
    faces = [
        shifted(x_last, 0, 1),
        shifted(x_first, 0, -1),
        shifted(y_last, 1, 0),
        shifted(y_first, -1, 0),
        shifted(level[-1:, -1:], 1, 1),
        shifted(level[-1:, :1], -1, 1),
        shifted(level[:1, -1:], 1, -1),
        shifted(level[:1, :1], -1, -1),
    ]
    base, ends, edges = residual_base(level, w_res)
    ends, edges = border(ends, edges, (x_first, x_last, y_first, y_last), faces, w_res)
    joined, front, side, corner = add_rows(
        got, base.reshape(-1, channels), ends, edges, level.shape, capacity)
    front = shifted(front, 0, 1)
    side = shifted(side, 1, 0)
    corner = shifted(corner, 1, 1)
    return lower(joined, front, side, corner, w_down)


def solution(mesh):
    return jax.shard_map(
        body,
        mesh=mesh,
        in_specs=(
            P("pts", "nbr", None, None),
            P("pts", "nbr", None, None),
            P("pts", "nbr", None),
            P("nbr", "pts", None, None),
            P(),
            P(),
        ),
        out_specs=P("nbr", "pts", None, None),
        check_vma=False,
    )
```

```python
import functools
import jax
import jax.numpy as jnp
from jax import lax
from jax.experimental import pallas as pl
from jax.experimental.pallas import tpu as pltpu
from jax.sharding import PartitionSpec as P


LANES = 128
EXTRA = 8
PIECES = 4
LINES = 4


def pack_kernel(devices, cap, owner_ref, cell_ref, rows_hbm, out_hbm,
                rows_ref, wide, spread, staged, slot_vmem, slot_smem, sems):
    p_local, _ = rows_ref.shape
    fetch = pltpu.make_async_copy(rows_hbm, rows_ref, sems.at[PIECES + 1])
    fetch.start()
    blocks = p_local // LANES
    stride = cap + EXTRA
    upper = (lax.broadcasted_iota(jnp.int32, (LANES, LANES), 0)
             <= lax.broadcasted_iota(jnp.int32, (LANES, LANES), 1)).astype(jnp.bfloat16)
    ids = lax.broadcasted_iota(jnp.int32, (devices, LANES), 0)
    spots = lax.broadcasted_iota(jnp.int32, (cap, LANES), 0)
    base = jnp.zeros((devices, 1), jnp.float32)
    table = jnp.zeros((2 * devices, cap), jnp.float32)
    for b in range(blocks):
        own = owner_ref[b:b + 1, :]
        cell = cell_ref[b:b + 1, :]
        hit = ids == own
        hot = hit.astype(jnp.float32)
        run = jnp.dot(hot.astype(jnp.bfloat16), upper, preferred_element_type=jnp.float32)
        place = jnp.sum(hot * (run + base), axis=0, keepdims=True).astype(jnp.int32) - 1
        base = base + run[:, LANES - 1:LANES]
        slot_vmem[b:b + 1, :] = own * stride + place
        high = jnp.where(hit, (cell // LANES + 1).astype(jnp.float32), 0.0)
        low = jnp.where(hit, (cell % LANES).astype(jnp.float32), 0.0)
        left = jnp.concatenate([high, low], axis=0).astype(jnp.bfloat16)
        right = (spots == place).astype(jnp.float32).astype(jnp.bfloat16)
        table = table + lax.dot_general(left, right, (((1,), (1,)), ((), ())),
                                        preferred_element_type=jnp.float32)
    copy = pltpu.make_async_copy(slot_vmem, slot_smem, sems.at[PIECES])
    copy.start()
    fetch.wait()
    wide[...] = rows_ref[...].astype(jnp.float32)
    per = -(-cap // LANES)
    for part in range(2):
        for j in range(per):
            width = min(LANES, cap - j * LANES)
            piece = table[part * devices:(part + 1) * devices, j * LANES:j * LANES + width]
            if width < LANES:
                piece = jnp.concatenate(
                    [piece, jnp.zeros((devices, LANES - width), jnp.float32)], axis=1)
            spread[pl.ds(cap + part * per + j, devices, stride=stride), :] = piece
    copy.wait()

    def step(b, carry):
        lines = [slot_smem.at[b * LINES + i] for i in range(LINES)]
        for u in range(LANES):
            for i in range(LINES):
                spread[pl.ds(lines[i][u], 1), :] = wide[
                    pl.ds((b * LINES + i) * LANES + u, 1), :]
        return carry

    lax.fori_loop(0, blocks // LINES, step, 0)
    piece = staged.shape[0] // PIECES
    sends = []
    for i in range(PIECES):
        part = pl.ds(i * piece, piece)
        staged[part, :] = spread[part, :].astype(jnp.bfloat16)
        sends.append(pltpu.make_async_copy(staged.at[part], out_hbm.at[part], sems.at[i]))
        sends[-1].start()
    for send in sends:
        send.wait()


def pack(owner, cell, rows, devices, cap):
    p_local, channels = rows.shape
    blocks = p_local // LANES
    total = devices * (cap + EXTRA)
    vm = pl.BlockSpec(memory_space=pltpu.VMEM)
    hbm = pl.BlockSpec(memory_space=pl.ANY)
    return pl.pallas_call(
        functools.partial(pack_kernel, devices, cap),
        out_shape=jax.ShapeDtypeStruct((total, channels), jnp.bfloat16),
        in_specs=[vm, vm, hbm],
        out_specs=hbm,
        scratch_shapes=[
            pltpu.VMEM((p_local, channels), jnp.bfloat16),
            pltpu.VMEM((p_local, channels), jnp.float32),
            pltpu.VMEM((total, channels), jnp.float32),
            pltpu.VMEM((total, channels), jnp.bfloat16),
            pltpu.VMEM((blocks, LANES), jnp.int32),
            pltpu.SMEM((blocks, LANES), jnp.int32),
            pltpu.SemaphoreType.DMA((PIECES + 2,)),
        ],
        name="pack",
        cost_estimate=pl.CostEstimate(flops=10**8, bytes_accessed=4 * 10**6, transcendentals=0),
    )(owner.reshape(blocks, LANES), cell.reshape(blocks, LANES), rows)


WAYS = 6


def add_kernel(capacity, got_ref, base_hbm, ends_ref, edges_ref, out_ref, front_ref, side_ref,
               corner_ref, wide, slot_vmem, slot_smem, sems, *sums):
    span_x, span_y, span_z, channels = out_ref.shape
    cells = span_x * span_y * span_z
    total, _ = got_ref.shape
    stride = capacity + EXTRA
    devices = total // stride
    per = -(-capacity // LANES)
    width = min(LANES, capacity)
    area = span_y * span_z
    first = pltpu.make_async_copy(base_hbm, sums[0].at[pl.ds(0, cells)], sems.at[0])
    first.start()
    wide[...] = got_ref[...].astype(jnp.float32)
    for j in range(per):
        high = wide[pl.ds(capacity + j, devices, stride=stride), :].astype(jnp.int32)
        low = wide[pl.ds(capacity + per + j, devices, stride=stride), :].astype(jnp.int32)
        slot_vmem[j * devices:(j + 1) * devices, :] = jnp.where(
            high > 0, (high - 1) * LANES + low, cells)
    copy = pltpu.make_async_copy(slot_vmem, slot_smem, sems.at[1])
    copy.start()
    for s in sums[1:]:
        s[...] = jnp.zeros_like(s)
    first.wait()
    for x in range(span_x):
        sums[0][x * area:x * area + span_z, :] = edges_ref[0, x]
        sums[0][(x + 1) * area - span_z:(x + 1) * area, :] = edges_ref[1, x]
    for k, x in ((0, 0), (1, span_x - 1)):
        sums[0][x * area:(x + 1) * area, :] = ends_ref[k].reshape(area, channels)
    copy.wait()
    for j in range(per):
        def step(o, carry):
            start = pl.multiple_of(o * stride + j * LANES, 8)
            line = slot_smem.at[j * devices + o]
            for u in range(width):
                s = sums[u % len(sums)]
                s[pl.ds(line[u], 1), :] += wide[pl.ds(start + u, 1), :]
            return carry

        lax.fori_loop(0, devices, step, 0)

    def finish(x, carry):
        at = pl.ds(pl.multiple_of(x * area, 8), area)
        value = sums[0][at, :]
        for s in sums[1:]:
            value = value + s[at, :]
        value = value.astype(jnp.bfloat16).reshape(span_y, span_z, channels)
        out_ref[x] = value
        side_ref[x] = value[span_y - 1:]
        return carry

    lax.fori_loop(0, span_x, finish, 0)
    front_ref[...] = out_ref[span_x - 1:]
    corner_ref[...] = out_ref[span_x - 1:, span_y - 1:]


def add_rows(got, base, ends, edges, shape, capacity):
    span_x, span_y, span_z, channels = shape
    cells = span_x * span_y * span_z
    total = got.shape[0]
    devices = total // (capacity + EXTRA)
    per = -(-capacity // LANES)
    vm = pl.BlockSpec(memory_space=pltpu.VMEM)
    return pl.pallas_call(
        functools.partial(add_kernel, capacity),
        out_shape=[
            jax.ShapeDtypeStruct(shape, jnp.bfloat16),
            jax.ShapeDtypeStruct((1, span_y, span_z, channels), jnp.bfloat16),
            jax.ShapeDtypeStruct((span_x, 1, span_z, channels), jnp.bfloat16),
            jax.ShapeDtypeStruct((1, 1, span_z, channels), jnp.bfloat16),
        ],
        in_specs=[vm, pl.BlockSpec(memory_space=pl.ANY), vm, vm],
        out_specs=[vm] * 4,
        scratch_shapes=[
            pltpu.VMEM((total, channels), jnp.float32),
            pltpu.VMEM((devices * per, LANES), jnp.int32),
            pltpu.SMEM((devices * per, LANES), jnp.int32),
            pltpu.SemaphoreType.DMA((2,)),
        ] + [pltpu.VMEM((cells + 8, channels), jnp.float32)] * WAYS,
        compiler_params=pltpu.CompilerParams(vmem_limit_bytes=LIMIT),
        name="add_rows",
        cost_estimate=pl.CostEstimate(flops=10**8, bytes_accessed=8 * 10**6, transcendentals=0),
    )(got, base, ends, edges)


LIMIT = 48 * 2**20


def join_taps(w_ref, wide, rows):
    channels = w_ref.shape[-1]
    for r, a in enumerate(rows):
        for d in range(2):
            for par in range(2):
                for c in range(3):
                    at = (((r * 2 + d) * 2 + par) * 3 + c) * channels
                    for s in range(2):
                        b = 2 * d + par - s
                        if 0 <= b <= 2:
                            tile = w_ref[9 * a + 3 * b + c]
                        else:
                            tile = jnp.zeros((channels, channels), jnp.bfloat16)
                        wide[at:at + channels, s * channels:(s + 1) * channels] = tile


def shifts(plane, count, span_z):
    spot = lax.broadcasted_iota(jnp.int32, (count, plane.shape[-1]), 0) % span_z
    middle = plane[8:8 + count, :]
    low = jnp.where(spot == 0, 0.0, plane[7:7 + count, :])
    high = jnp.where(spot == span_z - 1, 0.0, plane[9:9 + count, :])
    return [value.astype(jnp.bfloat16) for value in (low, middle, high)]


def spread_plane(plane, taps, start, half, span_z):
    channels = plane.shape[-1]
    lines = half * span_z
    for c, value in enumerate(shifts(plane, 2 * lines, span_z)):
        value = value.reshape(half, 2, span_z, channels)
        for par in range(2):
            at = (par * 3 + c) * channels
            taps[pl.ds(start, lines), at:at + channels] = value[:, par].reshape(lines, channels)


def residual_kernel(group, level_ref, w_ref, out_ref, ends_ref, edges_ref,
                    plane, taps, wide, result):
    span_x, span_y, span_z, channels = level_ref.shape
    half = (span_y + 2) // 2
    lines = half * span_z
    depth = 6 * channels
    count = (span_y + 2) * span_z
    join_taps(w_ref, wide, (0, 1, 2))
    plane[0:8 + span_z, :] = jnp.zeros((8 + span_z, channels), jnp.float32)
    plane[8 + count - span_z:16 + count, :] = jnp.zeros((8 + span_z, channels), jnp.float32)
    for x in (0, span_x + 1):
        taps[x * lines:(x + 1) * lines, :] = jnp.zeros((lines, depth), jnp.bfloat16)

    def fill(x, carry):
        plane[8 + span_z:8 + count - span_z, :] = level_ref[x].reshape(
            span_y * span_z, channels).astype(jnp.float32)
        spread_plane(plane, taps, pl.multiple_of((x + 1) * lines, 16), half, span_z)
        return carry

    lax.fori_loop(0, span_x, fill, 0)
    height = group * lines - span_z

    def multiply(g, carry):
        total = None
        for a in range(3):
            for d in range(2):
                start = pl.multiple_of((g * group + a) * lines + d * span_z, 16)
                at = (a * 2 + d) * depth
                part = jnp.dot(taps[pl.ds(start, height), :], wide[at:at + depth, :],
                               preferred_element_type=jnp.float32)
                total = part if total is None else total + part
        result[0:height, :] = total
        for i in range(group):
            x = g * group + i
            for s in range(2):
                value = result[i * lines:i * lines + span_y // 2 * span_z,
                               s * channels:(s + 1) * channels]
                value = value.reshape(span_y // 2, span_z, channels)
                edges_ref[s, x] = value[s * (span_y // 2 - 1)]
                if i == 0:
                    @pl.when(g == 0)
                    def _():
                        ends_ref[0, :, s] = value

                if i == group - 1:
                    @pl.when(x == span_x - 1)
                    def _():
                        ends_ref[1, :, s] = value

                here = level_ref[x].reshape(span_y // 2, 2, span_z, channels)[:, s]
                out_ref[x, :, s] = jnp.maximum(value, 0.0) + here.astype(jnp.float32)
        return carry

    lax.fori_loop(0, span_x // group, multiply, 0)


def residual_base(level, w_res, group=4):
    span_x, span_y, span_z, channels = level.shape
    lines = (span_y + 2) // 2 * span_z
    vm = pl.BlockSpec(memory_space=pltpu.VMEM)
    flops = 2 * span_x * span_y * span_z * 27 * channels * channels
    pairs = (span_y // 2, 2, span_z, channels)
    return pl.pallas_call(
        functools.partial(residual_kernel, group),
        out_shape=[
            jax.ShapeDtypeStruct((span_x,) + pairs, jnp.float32),
            jax.ShapeDtypeStruct((2,) + pairs, jnp.float32),
            jax.ShapeDtypeStruct((2, span_x, span_z, channels), jnp.float32),
        ],
        in_specs=[vm] * 2,
        out_specs=[vm] * 3,
        scratch_shapes=[
            pltpu.VMEM(((span_y + 2) * span_z + 16, channels), jnp.float32),
            pltpu.VMEM(((span_x + 2) * lines, 6 * channels), jnp.bfloat16),
            pltpu.VMEM((36 * channels, 2 * channels), jnp.bfloat16),
            pltpu.VMEM((group * lines, 2 * channels), jnp.float32),
        ],
        compiler_params=pltpu.CompilerParams(vmem_limit_bytes=26 * 2**20),
        name="residual",
        cost_estimate=pl.CostEstimate(flops=flops, bytes_accessed=8 * 10**6, transcendentals=0),
    )(level, w_res)


def border_kernel(ends_ref, edges_ref, xfirst_ref, xlast_ref, yfirst_ref, ylast_ref,
                  xlow_ref, xhigh_ref, ylow_ref, yhigh_ref, ll_ref, lh_ref, hl_ref, hh_ref,
                  w_ref, new_ends_ref, new_edges_ref, plane, taps, wide):
    _, half_y, _, span_z, channels = ends_ref.shape
    span_x = edges_ref.shape[1]
    span_y = 2 * half_y
    count = (span_y + 2) * span_z
    depth = 6 * channels
    join_taps(w_ref, wide, (0, 2))
    plane[0:8, :] = jnp.zeros((8, channels), jnp.float32)
    plane[8 + count:16 + count, :] = jnp.zeros((8, channels), jnp.float32)
    for k, (low, middle, high) in enumerate(
            ((ll_ref, xlow_ref, lh_ref), (hl_ref, xhigh_ref, hh_ref))):
        plane[8:8 + span_z, :] = low[...].reshape(span_z, channels).astype(jnp.float32)
        plane[8 + span_z:8 + count - span_z, :] = middle[...].reshape(
            span_y * span_z, channels).astype(jnp.float32)
        plane[8 + count - span_z:8 + count, :] = high[...].reshape(
            span_z, channels).astype(jnp.float32)
        spread_plane(plane, taps, 0, half_y + 1, span_z)
        change = None
        for d in range(2):
            at = (k * 2 + d) * depth
            part = jnp.dot(taps[d * span_z:(d + half_y) * span_z, :], wide[at:at + depth, :],
                           preferred_element_type=jnp.float32)
            change = part if change is None else change + part
        for s in range(2):
            value = change[:, s * channels:(s + 1) * channels].reshape(
                half_y, span_z, channels)
            new_ends_ref[k, :, s] = ends_ref[k, :, s] + value
    rows = (span_x + 2) * span_z
    for k, (source, here) in enumerate(((ylow_ref, yfirst_ref), (yhigh_ref, ylast_ref))):
        plane[8:8 + span_z, :] = jnp.zeros((span_z, channels), jnp.float32)
        plane[8 + span_z:8 + rows - span_z, :] = source[...].reshape(
            span_x * span_z, channels).astype(jnp.float32)
        plane[8 + rows - span_z:16 + rows, :] = jnp.zeros((span_z + 8, channels), jnp.float32)
        for c, value in enumerate(shifts(plane, rows, span_z)):
            taps[0:rows, c * channels:(c + 1) * channels] = value
        change = None
        for a in range(3):
            first = 9 * a + 3 * (2 * k)
            part = jnp.dot(taps[a * span_z:(a + span_x) * span_z, 0:3 * channels],
                           w_ref[first:first + 3].reshape(3 * channels, channels),
                           preferred_element_type=jnp.float32)
            change = part if change is None else change + part
        change = change.reshape(span_x, span_z, channels)
        new_edges_ref[k] = jnp.maximum(edges_ref[k] + change, 0.0) + here[...].reshape(
            span_x, span_z, channels).astype(jnp.float32)
        for e, x in ((0, 0), (1, span_x - 1)):
            new_ends_ref[e, k * (half_y - 1), k] = new_ends_ref[e, k * (half_y - 1), k] + change[x]
    for e, here in enumerate((xfirst_ref, xlast_ref)):
        new_ends_ref[e] = jnp.maximum(new_ends_ref[e], 0.0) + here[...].reshape(
            half_y, 2, span_z, channels).astype(jnp.float32)


def border(ends, edges, own, faces, w_res):
    _, half_y, _, span_z, channels = ends.shape
    span_x = edges.shape[1]
    rows = max((half_y + 1), (span_x + 2)) * span_z
    vm = pl.BlockSpec(memory_space=pltpu.VMEM)
    return pl.pallas_call(
        border_kernel,
        out_shape=[jax.ShapeDtypeStruct(ends.shape, jnp.float32),
                   jax.ShapeDtypeStruct(edges.shape, jnp.float32)],
        in_specs=[vm] * 15,
        out_specs=[vm] * 2,
        scratch_shapes=[
            pltpu.VMEM((2 * rows + 16, channels), jnp.float32),
            pltpu.VMEM((rows, 6 * channels), jnp.bfloat16),
            pltpu.VMEM((24 * channels, 2 * channels), jnp.bfloat16),
        ],
        compiler_params=pltpu.CompilerParams(vmem_limit_bytes=8 * 2**20),
        name="border",
        cost_estimate=pl.CostEstimate(flops=10**9, bytes_accessed=3 * 10**6, transcendentals=0),
    )(ends, edges, *own, *faces, w_res)


def lower_kernel(joined_ref, front_ref, side_ref, corner_ref, w_ref, out_ref, planes, taps):
    span_x, span_y, span_z, channels = joined_ref.shape
    half_y, half_z = span_y // 2, span_z // 2
    lines = half_y * half_z
    count = (span_y + 1) * span_z
    rows = (span_y + 1) * half_z
    depth = 9 * channels
    zero = lax.broadcasted_iota(jnp.int32, (rows, channels), 0) % half_z == 0
    for k in range(2):
        planes[k, 0:8, :] = jnp.zeros((8, channels), jnp.float32)

    def fill(x, first, rest):
        plane = planes.at[x % 2]
        plane[8:8 + span_z, :] = first.reshape(span_z, channels).astype(jnp.float32)
        plane[8 + span_z:8 + count, :] = rest.reshape(
            span_y * span_z, channels).astype(jnp.float32)
        low = jnp.where(zero, 0.0, plane[pl.ds(7, rows, stride=2), :])
        for c, value in enumerate((low, plane[pl.ds(8, rows, stride=2), :],
                                   plane[pl.ds(9, rows, stride=2), :])):
            value = value.reshape(span_y + 1, half_z, channels)
            evens = value[0:span_y].reshape(half_y, 2, half_z, channels)
            odds = value[1:].reshape(half_y, 2, half_z, channels)
            for b, piece in enumerate((evens[:, 0], evens[:, 1], odds[:, 1])):
                at = (b * 3 + c) * channels
                taps[x, :, at:at + channels] = piece.reshape(lines, channels).astype(jnp.bfloat16)

    def multiply(i):
        total = None
        for a in range(3):
            part = jnp.dot(taps[2 * i + a], w_ref[a * depth:(a + 1) * depth, :],
                           preferred_element_type=jnp.float32)
            total = part if total is None else total + part
        out_ref[i] = total.reshape(half_y, half_z, w_ref.shape[-1]).astype(jnp.bfloat16)

    fill(0, corner_ref[...], front_ref[...])
    for x in range(1, span_x + 1):
        fill(x, side_ref[x - 1], joined_ref[x - 1])
        if x % 2 == 0:
            multiply(x // 2 - 1)


def lower(joined, front, side, corner, w_down):
    span_x, span_y, span_z, channels = joined.shape
    wide = w_down.shape[-1]
    vm = pl.BlockSpec(memory_space=pltpu.VMEM)
    flops = 2 * span_x * span_y * span_z // 8 * 27 * channels * wide
    return pl.pallas_call(
        lower_kernel,
        out_shape=jax.ShapeDtypeStruct((span_x // 2, span_y // 2, span_z // 2, wide),
                                       jnp.bfloat16),
        in_specs=[vm] * 5,
        out_specs=vm,
        scratch_shapes=[
            pltpu.VMEM((2, (span_y + 1) * span_z + 16, channels), jnp.float32),
            pltpu.VMEM((span_x + 1, span_y * span_z // 4, 9 * channels), jnp.bfloat16),
        ],
        compiler_params=pltpu.CompilerParams(vmem_limit_bytes=28 * 2**20),
        name="lower",
        cost_estimate=pl.CostEstimate(flops=flops, bytes_accessed=5 * 10**6, transcendentals=0),
    )(joined, front, side, corner, w_down.reshape(-1, wide))


def shifted(array, by_pts, by_nbr):
    count_pts = lax.axis_size("pts")
    count_nbr = lax.axis_size("nbr")
    pairs = [
        (i * count_nbr + j, (i + by_pts) * count_nbr + j + by_nbr)
        for i in range(count_pts)
        for j in range(count_nbr)
        if 0 <= i + by_pts < count_pts and 0 <= j + by_nbr < count_nbr
    ]
    return lax.ppermute(array, ("pts", "nbr"), pairs)


def exchanged(array, devices):
    got = lax.all_to_all(
        array.reshape(devices, -1, array.shape[-1]),
        ("pts", "nbr"),
        split_axis=0,
        concat_axis=0,
        tiled=True,
    )
    return got.reshape(array.shape)


def body(points, dest_owner, dest_cell, level_input, w_res, w_down):
    devices = lax.axis_size("pts") * lax.axis_size("nbr")
    channels = points.shape[-1]
    rows = points.reshape(-1, channels)
    capacity = 2 * rows.shape[0] // devices
    outgoing = pack(dest_owner.reshape(-1), dest_cell.reshape(-1), rows, devices, capacity)
    outgoing, level = lax.optimization_barrier((outgoing, level_input))
    got = exchanged(outgoing, devices)
    x_first, x_last = level[:1], level[-1:]
    y_first, y_last = level[:, :1], level[:, -1:]
    faces = [
        shifted(x_last, 0, 1),
        shifted(x_first, 0, -1),
        shifted(y_last, 1, 0),
        shifted(y_first, -1, 0),
        shifted(level[-1:, -1:], 1, 1),
        shifted(level[-1:, :1], -1, 1),
        shifted(level[:1, -1:], 1, -1),
        shifted(level[:1, :1], -1, -1),
    ]
    base, ends, edges = residual_base(level, w_res)
    ends, edges = border(ends, edges, (x_first, x_last, y_first, y_last), faces, w_res)
    joined, front, side, corner = add_rows(
        got, base.reshape(-1, channels), ends, edges, level.shape, capacity)
    front = shifted(front, 0, 1)
    side = shifted(side, 1, 0)
    corner = shifted(corner, 1, 1)
    return lower(joined, front, side, corner, w_down)


def solution(mesh):
    return jax.shard_map(
        body,
        mesh=mesh,
        in_specs=(
            P("pts", "nbr", None, None),
            P("pts", "nbr", None, None),
            P("pts", "nbr", None),
            P("nbr", "pts", None, None),
            P(),
            P(),
        ),
        out_specs=P("nbr", "pts", None, None),
        check_vma=False,
    )
```

```python
import functools
import jax
import jax.numpy as jnp
from jax import lax
from jax.experimental import pallas as pl
from jax.experimental.pallas import tpu as pltpu
from jax.sharding import PartitionSpec as P


LANES = 128
EXTRA = 8
PIECES = 4
LINES = 4


def pack_kernel(devices, cap, owner_ref, cell_ref, rows_hbm, out_hbm,
                rows_ref, wide, spread, staged, slot_vmem, slot_smem, sems):
    p_local, _ = rows_ref.shape
    fetch = pltpu.make_async_copy(rows_hbm, rows_ref, sems.at[PIECES + 1])
    fetch.start()
    blocks = p_local // LANES
    stride = cap + EXTRA
    upper = (lax.broadcasted_iota(jnp.int32, (LANES, LANES), 0)
             <= lax.broadcasted_iota(jnp.int32, (LANES, LANES), 1)).astype(jnp.bfloat16)
    ids = lax.broadcasted_iota(jnp.int32, (devices, LANES), 0)
    spots = lax.broadcasted_iota(jnp.int32, (cap, LANES), 0)
    base = jnp.zeros((devices, 1), jnp.float32)
    table = jnp.zeros((2 * devices, cap), jnp.float32)
    for b in range(blocks):
        own = owner_ref[b:b + 1, :]
        cell = cell_ref[b:b + 1, :]
        hit = ids == own
        hot = hit.astype(jnp.float32)
        run = jnp.dot(hot.astype(jnp.bfloat16), upper, preferred_element_type=jnp.float32)
        place = jnp.sum(hot * (run + base), axis=0, keepdims=True).astype(jnp.int32) - 1
        base = base + run[:, LANES - 1:LANES]
        slot_vmem[b:b + 1, :] = own * stride + place
        high = jnp.where(hit, (cell // LANES + 1).astype(jnp.float32), 0.0)
        low = jnp.where(hit, (cell % LANES).astype(jnp.float32), 0.0)
        left = jnp.concatenate([high, low], axis=0).astype(jnp.bfloat16)
        right = (spots == place).astype(jnp.float32).astype(jnp.bfloat16)
        table = table + lax.dot_general(left, right, (((1,), (1,)), ((), ())),
                                        preferred_element_type=jnp.float32)
    copy = pltpu.make_async_copy(slot_vmem, slot_smem, sems.at[PIECES])
    copy.start()
    fetch.wait()

    def widen(i, carry):
        at = pl.ds(pl.multiple_of(i * 2 * LANES, 16), 2 * LANES)
        wide[at, :] = rows_ref[at, :].astype(jnp.float32)
        return carry

    lax.fori_loop(0, p_local // (2 * LANES), widen, 0)
    per = -(-cap // LANES)
    for part in range(2):
        for j in range(per):
            width = min(LANES, cap - j * LANES)
            piece = table[part * devices:(part + 1) * devices, j * LANES:j * LANES + width]
            if width < LANES:
                piece = jnp.concatenate(
                    [piece, jnp.zeros((devices, LANES - width), jnp.float32)], axis=1)
            spread[pl.ds(cap + part * per + j, devices, stride=stride), :] = piece
    copy.wait()

    def step(b, carry):
        lines = [slot_smem.at[b * LINES + i] for i in range(LINES)]
        for u in range(LANES):
            for i in range(LINES):
                spread[pl.ds(lines[i][u], 1), :] = wide[
                    pl.ds((b * LINES + i) * LANES + u, 1), :]
        return carry

    lax.fori_loop(0, blocks // LINES, step, 0)
    piece = staged.shape[0] // PIECES
    sends = []
    for i in range(PIECES):
        part = pl.ds(i * piece, piece)
        staged[part, :] = spread[part, :].astype(jnp.bfloat16)
        sends.append(pltpu.make_async_copy(staged.at[part], out_hbm.at[part], sems.at[i]))
        sends[-1].start()
    for send in sends:
        send.wait()


def pack(owner, cell, rows, devices, cap):
    p_local, channels = rows.shape
    blocks = p_local // LANES
    total = devices * (cap + EXTRA)
    vm = pl.BlockSpec(memory_space=pltpu.VMEM)
    hbm = pl.BlockSpec(memory_space=pl.ANY)
    return pl.pallas_call(
        functools.partial(pack_kernel, devices, cap),
        out_shape=jax.ShapeDtypeStruct((total, channels), jnp.bfloat16),
        in_specs=[vm, vm, hbm],
        out_specs=hbm,
        scratch_shapes=[
            pltpu.VMEM((p_local, channels), jnp.bfloat16),
            pltpu.VMEM((p_local, channels), jnp.float32),
            pltpu.VMEM((total, channels), jnp.float32),
            pltpu.VMEM((total, channels), jnp.bfloat16),
            pltpu.VMEM((blocks, LANES), jnp.int32),
            pltpu.SMEM((blocks, LANES), jnp.int32),
            pltpu.SemaphoreType.DMA((PIECES + 2,)),
        ],
        name="pack",
        cost_estimate=pl.CostEstimate(flops=10**8, bytes_accessed=4 * 10**6, transcendentals=0),
    )(owner.reshape(blocks, LANES), cell.reshape(blocks, LANES), rows)


WAYS = 8


def add_kernel(capacity, got_ref, base_hbm, ends_ref, edges_ref, out_ref, front_ref, side_ref,
               corner_ref, wide, slot_vmem, slot_smem, sems, *sums):
    span_x, span_y, span_z, channels = out_ref.shape
    cells = span_x * span_y * span_z
    total, _ = got_ref.shape
    stride = capacity + EXTRA
    devices = total // stride
    per = -(-capacity // LANES)
    width = min(LANES, capacity)
    area = span_y * span_z
    first = pltpu.make_async_copy(base_hbm, sums[0].at[pl.ds(0, cells)], sems.at[0])
    first.start()
    wide[...] = got_ref[...].astype(jnp.float32)
    for j in range(per):
        high = wide[pl.ds(capacity + j, devices, stride=stride), :].astype(jnp.int32)
        low = wide[pl.ds(capacity + per + j, devices, stride=stride), :].astype(jnp.int32)
        slot_vmem[j * devices:(j + 1) * devices, :] = jnp.where(
            high > 0, (high - 1) * LANES + low, cells)
    copy = pltpu.make_async_copy(slot_vmem, slot_smem, sems.at[1])
    copy.start()

    def clear(x, carry):
        at = pl.ds(pl.multiple_of(x * area, 8), area)
        for s in sums[1:]:
            s[at, :] = jnp.zeros((area, channels), jnp.float32)
        return carry

    lax.fori_loop(0, span_x, clear, 0)
    for s in sums[1:]:
        s[cells:cells + 8, :] = jnp.zeros((8, channels), jnp.float32)
    first.wait()
    for x in range(span_x):
        sums[0][x * area:x * area + span_z, :] = edges_ref[0, x]
        sums[0][(x + 1) * area - span_z:(x + 1) * area, :] = edges_ref[1, x]
    for k, x in ((0, 0), (1, span_x - 1)):
        sums[0][x * area:(x + 1) * area, :] = ends_ref[k].reshape(area, channels)
    copy.wait()
    for j in range(per):
        def step(o, carry):
            lines = [slot_smem.at[j * devices + o * LINES + i] for i in range(LINES)]
            starts = [pl.multiple_of((o * LINES + i) * stride + j * LANES, 8)
                      for i in range(LINES)]
            for u in range(width):
                for i in range(LINES):
                    s = sums[(u * LINES + i) % len(sums)]
                    s[pl.ds(lines[i][u], 1), :] += wide[pl.ds(starts[i] + u, 1), :]
            return carry

        lax.fori_loop(0, devices // LINES, step, 0)

    def finish(x, carry):
        at = pl.ds(pl.multiple_of(x * area, 8), area)
        value = sums[0][at, :]
        for s in sums[1:]:
            value = value + s[at, :]
        value = value.astype(jnp.bfloat16).reshape(span_y, span_z, channels)
        out_ref[x] = value
        side_ref[x] = value[span_y - 1:]
        return carry

    lax.fori_loop(0, span_x, finish, 0)
    front_ref[...] = out_ref[span_x - 1:]
    corner_ref[...] = out_ref[span_x - 1:, span_y - 1:]


def add_rows(got, base, ends, edges, shape, capacity):
    span_x, span_y, span_z, channels = shape
    cells = span_x * span_y * span_z
    total = got.shape[0]
    devices = total // (capacity + EXTRA)
    per = -(-capacity // LANES)
    vm = pl.BlockSpec(memory_space=pltpu.VMEM)
    return pl.pallas_call(
        functools.partial(add_kernel, capacity),
        out_shape=[
            jax.ShapeDtypeStruct(shape, jnp.bfloat16),
            jax.ShapeDtypeStruct((1, span_y, span_z, channels), jnp.bfloat16),
            jax.ShapeDtypeStruct((span_x, 1, span_z, channels), jnp.bfloat16),
            jax.ShapeDtypeStruct((1, 1, span_z, channels), jnp.bfloat16),
        ],
        in_specs=[vm, pl.BlockSpec(memory_space=pl.ANY), vm, vm],
        out_specs=[vm] * 4,
        scratch_shapes=[
            pltpu.VMEM((total, channels), jnp.float32),
            pltpu.VMEM((devices * per, LANES), jnp.int32),
            pltpu.SMEM((devices * per, LANES), jnp.int32),
            pltpu.SemaphoreType.DMA((2,)),
        ] + [pltpu.VMEM((cells + 8, channels), jnp.float32)] * WAYS,
        compiler_params=pltpu.CompilerParams(vmem_limit_bytes=LIMIT),
        name="add_rows",
        cost_estimate=pl.CostEstimate(flops=10**8, bytes_accessed=8 * 10**6, transcendentals=0),
    )(got, base, ends, edges)


LIMIT = 48 * 2**20


def join_taps(w_ref, wide, rows):
    channels = w_ref.shape[-1]
    for r, a in enumerate(rows):
        for d in range(2):
            for par in range(2):
                for c in range(3):
                    at = (((r * 2 + d) * 2 + par) * 3 + c) * channels
                    for s in range(2):
                        b = 2 * d + par - s
                        if 0 <= b <= 2:
                            tile = w_ref[9 * a + 3 * b + c]
                        else:
                            tile = jnp.zeros((channels, channels), jnp.bfloat16)
                        wide[at:at + channels, s * channels:(s + 1) * channels] = tile


def shifts(plane, count, span_z):
    spot = lax.broadcasted_iota(jnp.int32, (count, plane.shape[-1]), 0) % span_z
    middle = plane[8:8 + count, :]
    low = jnp.where(spot == 0, 0.0, plane[7:7 + count, :])
    high = jnp.where(spot == span_z - 1, 0.0, plane[9:9 + count, :])
    return [value.astype(jnp.bfloat16) for value in (low, middle, high)]


def spread_plane(plane, taps, start, half, span_z):
    channels = plane.shape[-1]
    lines = half * span_z
    for c, value in enumerate(shifts(plane, 2 * lines, span_z)):
        value = value.reshape(half, 2, span_z, channels)
        for par in range(2):
            at = (par * 3 + c) * channels
            taps[pl.ds(start, lines), at:at + channels] = value[:, par].reshape(lines, channels)


def residual_kernel(group, level_ref, w_ref, out_ref, ends_ref, edges_ref,
                    plane, taps, wide, result):
    span_x, span_y, span_z, channels = level_ref.shape
    half = (span_y + 2) // 2
    lines = half * span_z
    depth = 6 * channels
    count = (span_y + 2) * span_z
    join_taps(w_ref, wide, (0, 1, 2))
    plane[0:8 + span_z, :] = jnp.zeros((8 + span_z, channels), jnp.float32)
    plane[8 + count - span_z:16 + count, :] = jnp.zeros((8 + span_z, channels), jnp.float32)
    for x in (0, span_x + 1):
        taps[x * lines:(x + 1) * lines, :] = jnp.zeros((lines, depth), jnp.bfloat16)

    def fill(x, carry):
        plane[8 + span_z:8 + count - span_z, :] = level_ref[x].reshape(
            span_y * span_z, channels).astype(jnp.float32)
        spread_plane(plane, taps, pl.multiple_of((x + 1) * lines, 16), half, span_z)
        return carry

    lax.fori_loop(0, span_x, fill, 0)
    height = group * lines - span_z

    def multiply(g, carry):
        total = None
        for a in range(3):
            for d in range(2):
                start = pl.multiple_of((g * group + a) * lines + d * span_z, 16)
                at = (a * 2 + d) * depth
                part = jnp.dot(taps[pl.ds(start, height), :], wide[at:at + depth, :],
                               preferred_element_type=jnp.float32)
                total = part if total is None else total + part
        result[0:height, :] = total
        for i in range(group):
            x = g * group + i
            for s in range(2):
                value = result[i * lines:i * lines + span_y // 2 * span_z,
                               s * channels:(s + 1) * channels]
                value = value.reshape(span_y // 2, span_z, channels)
                edges_ref[s, x] = value[s * (span_y // 2 - 1)]
                if i == 0:
                    @pl.when(g == 0)
                    def _():
                        ends_ref[0, :, s] = value

                if i == group - 1:
                    @pl.when(x == span_x - 1)
                    def _():
                        ends_ref[1, :, s] = value

                here = level_ref[x].reshape(span_y // 2, 2, span_z, channels)[:, s]
                out_ref[x, :, s] = jnp.maximum(value, 0.0) + here.astype(jnp.float32)
        return carry

    lax.fori_loop(0, span_x // group, multiply, 0)


def residual_base(level, w_res, group=4):
    span_x, span_y, span_z, channels = level.shape
    lines = (span_y + 2) // 2 * span_z
    vm = pl.BlockSpec(memory_space=pltpu.VMEM)
    flops = 2 * span_x * span_y * span_z * 27 * channels * channels
    pairs = (span_y // 2, 2, span_z, channels)
    return pl.pallas_call(
        functools.partial(residual_kernel, group),
        out_shape=[
            jax.ShapeDtypeStruct((span_x,) + pairs, jnp.float32),
            jax.ShapeDtypeStruct((2,) + pairs, jnp.float32),
            jax.ShapeDtypeStruct((2, span_x, span_z, channels), jnp.float32),
        ],
        in_specs=[vm] * 2,
        out_specs=[vm] * 3,
        scratch_shapes=[
            pltpu.VMEM(((span_y + 2) * span_z + 16, channels), jnp.float32),
            pltpu.VMEM(((span_x + 2) * lines, 6 * channels), jnp.bfloat16),
            pltpu.VMEM((36 * channels, 2 * channels), jnp.bfloat16),
            pltpu.VMEM((group * lines, 2 * channels), jnp.float32),
        ],
        compiler_params=pltpu.CompilerParams(vmem_limit_bytes=26 * 2**20),
        name="residual",
        cost_estimate=pl.CostEstimate(flops=flops, bytes_accessed=8 * 10**6, transcendentals=0),
    )(level, w_res)


def border_kernel(ends_ref, edges_ref, xfirst_ref, xlast_ref, yfirst_ref, ylast_ref,
                  xlow_ref, xhigh_ref, ylow_ref, yhigh_ref, ll_ref, lh_ref, hl_ref, hh_ref,
                  w_ref, new_ends_ref, new_edges_ref, plane, taps, wide):
    _, half_y, _, span_z, channels = ends_ref.shape
    span_x = edges_ref.shape[1]
    span_y = 2 * half_y
    count = (span_y + 2) * span_z
    depth = 6 * channels
    join_taps(w_ref, wide, (0, 2))
    plane[0:8, :] = jnp.zeros((8, channels), jnp.float32)
    plane[8 + count:16 + count, :] = jnp.zeros((8, channels), jnp.float32)
    for k, (low, middle, high) in enumerate(
            ((ll_ref, xlow_ref, lh_ref), (hl_ref, xhigh_ref, hh_ref))):
        plane[8:8 + span_z, :] = low[...].reshape(span_z, channels).astype(jnp.float32)
        plane[8 + span_z:8 + count - span_z, :] = middle[...].reshape(
            span_y * span_z, channels).astype(jnp.float32)
        plane[8 + count - span_z:8 + count, :] = high[...].reshape(
            span_z, channels).astype(jnp.float32)
        spread_plane(plane, taps, 0, half_y + 1, span_z)
        change = None
        for d in range(2):
            at = (k * 2 + d) * depth
            part = jnp.dot(taps[d * span_z:(d + half_y) * span_z, :], wide[at:at + depth, :],
                           preferred_element_type=jnp.float32)
            change = part if change is None else change + part
        for s in range(2):
            value = change[:, s * channels:(s + 1) * channels].reshape(
                half_y, span_z, channels)
            new_ends_ref[k, :, s] = ends_ref[k, :, s] + value
    rows = (span_x + 2) * span_z
    for k, (source, here) in enumerate(((ylow_ref, yfirst_ref), (yhigh_ref, ylast_ref))):
        plane[8:8 + span_z, :] = jnp.zeros((span_z, channels), jnp.float32)
        plane[8 + span_z:8 + rows - span_z, :] = source[...].reshape(
            span_x * span_z, channels).astype(jnp.float32)
        plane[8 + rows - span_z:16 + rows, :] = jnp.zeros((span_z + 8, channels), jnp.float32)
        for c, value in enumerate(shifts(plane, rows, span_z)):
            taps[0:rows, c * channels:(c + 1) * channels] = value
        change = None
        for a in range(3):
            first = 9 * a + 3 * (2 * k)
            part = jnp.dot(taps[a * span_z:(a + span_x) * span_z, 0:3 * channels],
                           w_ref[first:first + 3].reshape(3 * channels, channels),
                           preferred_element_type=jnp.float32)
            change = part if change is None else change + part
        change = change.reshape(span_x, span_z, channels)
        new_edges_ref[k] = jnp.maximum(edges_ref[k] + change, 0.0) + here[...].reshape(
            span_x, span_z, channels).astype(jnp.float32)
        for e, x in ((0, 0), (1, span_x - 1)):
            new_ends_ref[e, k * (half_y - 1), k] = new_ends_ref[e, k * (half_y - 1), k] + change[x]
    for e, here in enumerate((xfirst_ref, xlast_ref)):
        new_ends_ref[e] = jnp.maximum(new_ends_ref[e], 0.0) + here[...].reshape(
            half_y, 2, span_z, channels).astype(jnp.float32)


def border(ends, edges, own, faces, w_res):
    _, half_y, _, span_z, channels = ends.shape
    span_x = edges.shape[1]
    rows = max((half_y + 1), (span_x + 2)) * span_z
    vm = pl.BlockSpec(memory_space=pltpu.VMEM)
    return pl.pallas_call(
        border_kernel,
        out_shape=[jax.ShapeDtypeStruct(ends.shape, jnp.float32),
                   jax.ShapeDtypeStruct(edges.shape, jnp.float32)],
        in_specs=[vm] * 15,
        out_specs=[vm] * 2,
        scratch_shapes=[
            pltpu.VMEM((2 * rows + 16, channels), jnp.float32),
            pltpu.VMEM((rows, 6 * channels), jnp.bfloat16),
            pltpu.VMEM((24 * channels, 2 * channels), jnp.bfloat16),
        ],
        compiler_params=pltpu.CompilerParams(vmem_limit_bytes=8 * 2**20),
        name="border",
        cost_estimate=pl.CostEstimate(flops=10**9, bytes_accessed=3 * 10**6, transcendentals=0),
    )(ends, edges, *own, *faces, w_res)


def lower_kernel(joined_ref, front_ref, side_ref, corner_ref, w_ref, out_ref, planes, taps):
    span_x, span_y, span_z, channels = joined_ref.shape
    half_y, half_z = span_y // 2, span_z // 2
    lines = half_y * half_z
    count = (span_y + 1) * span_z
    rows = (span_y + 1) * half_z
    depth = 9 * channels
    zero = lax.broadcasted_iota(jnp.int32, (rows, channels), 0) % half_z == 0
    for k in range(2):
        planes[k, 0:8, :] = jnp.zeros((8, channels), jnp.float32)

    def fill(x, first, rest):
        plane = planes.at[x % 2]
        plane[8:8 + span_z, :] = first.reshape(span_z, channels).astype(jnp.float32)
        plane[8 + span_z:8 + count, :] = rest.reshape(
            span_y * span_z, channels).astype(jnp.float32)
        low = jnp.where(zero, 0.0, plane[pl.ds(7, rows, stride=2), :])
        for c, value in enumerate((low, plane[pl.ds(8, rows, stride=2), :],
                                   plane[pl.ds(9, rows, stride=2), :])):
            value = value.reshape(span_y + 1, half_z, channels)
            evens = value[0:span_y].reshape(half_y, 2, half_z, channels)
            odds = value[1:].reshape(half_y, 2, half_z, channels)
            for b, piece in enumerate((evens[:, 0], evens[:, 1], odds[:, 1])):
                at = (b * 3 + c) * channels
                taps[x, :, at:at + channels] = piece.reshape(lines, channels).astype(jnp.bfloat16)

    def multiply(i):
        total = None
        for a in range(3):
            part = jnp.dot(taps[2 * i + a], w_ref[a * depth:(a + 1) * depth, :],
                           preferred_element_type=jnp.float32)
            total = part if total is None else total + part
        out_ref[i] = total.reshape(half_y, half_z, w_ref.shape[-1]).astype(jnp.bfloat16)

    fill(0, corner_ref[...], front_ref[...])
    for x in range(1, span_x + 1):
        fill(x, side_ref[x - 1], joined_ref[x - 1])
        if x % 2 == 0:
            multiply(x // 2 - 1)


def lower(joined, front, side, corner, w_down):
    span_x, span_y, span_z, channels = joined.shape
    wide = w_down.shape[-1]
    vm = pl.BlockSpec(memory_space=pltpu.VMEM)
    flops = 2 * span_x * span_y * span_z // 8 * 27 * channels * wide
    return pl.pallas_call(
        lower_kernel,
        out_shape=jax.ShapeDtypeStruct((span_x // 2, span_y // 2, span_z // 2, wide),
                                       jnp.bfloat16),
        in_specs=[vm] * 5,
        out_specs=vm,
        scratch_shapes=[
            pltpu.VMEM((2, (span_y + 1) * span_z + 16, channels), jnp.float32),
            pltpu.VMEM((span_x + 1, span_y * span_z // 4, 9 * channels), jnp.bfloat16),
        ],
        compiler_params=pltpu.CompilerParams(vmem_limit_bytes=28 * 2**20),
        name="lower",
        cost_estimate=pl.CostEstimate(flops=flops, bytes_accessed=5 * 10**6, transcendentals=0),
    )(joined, front, side, corner, w_down.reshape(-1, wide))


def shifted(array, by_pts, by_nbr):
    count_pts = lax.axis_size("pts")
    count_nbr = lax.axis_size("nbr")
    pairs = [
        (i * count_nbr + j, (i + by_pts) * count_nbr + j + by_nbr)
        for i in range(count_pts)
        for j in range(count_nbr)
        if 0 <= i + by_pts < count_pts and 0 <= j + by_nbr < count_nbr
    ]
    return lax.ppermute(array, ("pts", "nbr"), pairs)


def exchanged(array, devices):
    got = lax.all_to_all(
        array.reshape(devices, -1, array.shape[-1]),
        ("pts", "nbr"),
        split_axis=0,
        concat_axis=0,
        tiled=True,
    )
    return got.reshape(array.shape)


def body(points, dest_owner, dest_cell, level_input, w_res, w_down):
    devices = lax.axis_size("pts") * lax.axis_size("nbr")
    channels = points.shape[-1]
    rows = points.reshape(-1, channels)
    capacity = 2 * rows.shape[0] // devices
    outgoing = pack(dest_owner.reshape(-1), dest_cell.reshape(-1), rows, devices, capacity)
    outgoing, level = lax.optimization_barrier((outgoing, level_input))
    got = exchanged(outgoing, devices)
    x_first, x_last = level[:1], level[-1:]
    y_first, y_last = level[:, :1], level[:, -1:]
    faces = [
        shifted(x_last, 0, 1),
        shifted(x_first, 0, -1),
        shifted(y_last, 1, 0),
        shifted(y_first, -1, 0),
        shifted(level[-1:, -1:], 1, 1),
        shifted(level[-1:, :1], -1, 1),
        shifted(level[:1, -1:], 1, -1),
        shifted(level[:1, :1], -1, -1),
    ]
    base, ends, edges = residual_base(level, w_res)
    ends, edges = border(ends, edges, (x_first, x_last, y_first, y_last), faces, w_res)
    joined, front, side, corner = add_rows(
        got, base.reshape(-1, channels), ends, edges, level.shape, capacity)
    front = shifted(front, 0, 1)
    side = shifted(side, 1, 0)
    corner = shifted(corner, 1, 1)
    return lower(joined, front, side, corner, w_down)


def solution(mesh):
    return jax.shard_map(
        body,
        mesh=mesh,
        in_specs=(
            P("pts", "nbr", None, None),
            P("pts", "nbr", None, None),
            P("pts", "nbr", None),
            P("nbr", "pts", None, None),
            P(),
            P(),
        ),
        out_specs=P("nbr", "pts", None, None),
        check_vma=False,
    )
```

```python
import functools
import jax
import jax.numpy as jnp
from jax import lax
from jax.experimental import pallas as pl
from jax.experimental.pallas import tpu as pltpu
from jax.sharding import PartitionSpec as P


LANES = 128
EXTRA = 8
PIECES = 4
LINES = 4


def pack_kernel(devices, cap, owner_ref, cell_ref, rows_hbm, out_hbm,
                rows_ref, wide, spread, staged, slot_vmem, slot_smem, sems):
    p_local, _ = rows_ref.shape
    fetch = pltpu.make_async_copy(rows_hbm, rows_ref, sems.at[PIECES + 1])
    fetch.start()
    blocks = p_local // LANES
    stride = cap + EXTRA
    upper = (lax.broadcasted_iota(jnp.int32, (LANES, LANES), 0)
             <= lax.broadcasted_iota(jnp.int32, (LANES, LANES), 1)).astype(jnp.bfloat16)
    ids = lax.broadcasted_iota(jnp.int32, (devices, LANES), 0)
    spots = lax.broadcasted_iota(jnp.int32, (cap, LANES), 0)
    base = jnp.zeros((devices, 1), jnp.float32)
    table = jnp.zeros((2 * devices, cap), jnp.float32)
    for b in range(blocks):
        own = owner_ref[b:b + 1, :]
        cell = cell_ref[b:b + 1, :]
        hit = ids == own
        hot = hit.astype(jnp.float32)
        run = jnp.dot(hot.astype(jnp.bfloat16), upper, preferred_element_type=jnp.float32)
        place = jnp.sum(hot * (run + base), axis=0, keepdims=True).astype(jnp.int32) - 1
        base = base + run[:, LANES - 1:LANES]
        slot_vmem[b:b + 1, :] = own * stride + place
        high = jnp.where(hit, (cell // LANES + 1).astype(jnp.float32), 0.0)
        low = jnp.where(hit, (cell % LANES).astype(jnp.float32), 0.0)
        left = jnp.concatenate([high, low], axis=0).astype(jnp.bfloat16)
        right = (spots == place).astype(jnp.float32).astype(jnp.bfloat16)
        table = table + lax.dot_general(left, right, (((1,), (1,)), ((), ())),
                                        preferred_element_type=jnp.float32)
    copy = pltpu.make_async_copy(slot_vmem, slot_smem, sems.at[PIECES])
    copy.start()
    fetch.wait()

    def widen(i, carry):
        at = pl.ds(pl.multiple_of(i * 2 * LANES, 16), 2 * LANES)
        wide[at, :] = rows_ref[at, :].astype(jnp.float32)
        return carry

    lax.fori_loop(0, p_local // (2 * LANES), widen, 0)
    per = -(-cap // LANES)
    for part in range(2):
        for j in range(per):
            width = min(LANES, cap - j * LANES)
            piece = table[part * devices:(part + 1) * devices, j * LANES:j * LANES + width]
            if width < LANES:
                piece = jnp.concatenate(
                    [piece, jnp.zeros((devices, LANES - width), jnp.float32)], axis=1)
            spread[pl.ds(cap + part * per + j, devices, stride=stride), :] = piece
    copy.wait()

    def step(b, carry):
        lines = [slot_smem.at[b * LINES + i] for i in range(LINES)]
        for u in range(LANES):
            for i in range(LINES):
                spread[pl.ds(lines[i][u], 1), :] = wide[
                    pl.ds((b * LINES + i) * LANES + u, 1), :]
        return carry

    lax.fori_loop(0, blocks // LINES, step, 0)
    piece = staged.shape[0] // PIECES
    sends = []
    for i in range(PIECES):
        part = pl.ds(i * piece, piece)
        staged[part, :] = spread[part, :].astype(jnp.bfloat16)
        sends.append(pltpu.make_async_copy(staged.at[part], out_hbm.at[part], sems.at[i]))
        sends[-1].start()
    for send in sends:
        send.wait()


def pack(owner, cell, rows, devices, cap):
    p_local, channels = rows.shape
    blocks = p_local // LANES
    total = devices * (cap + EXTRA)
    vm = pl.BlockSpec(memory_space=pltpu.VMEM)
    hbm = pl.BlockSpec(memory_space=pl.ANY)
    return pl.pallas_call(
        functools.partial(pack_kernel, devices, cap),
        out_shape=jax.ShapeDtypeStruct((total, channels), jnp.bfloat16),
        in_specs=[vm, vm, hbm],
        out_specs=hbm,
        scratch_shapes=[
            pltpu.VMEM((p_local, channels), jnp.bfloat16),
            pltpu.VMEM((p_local, channels), jnp.float32),
            pltpu.VMEM((total, channels), jnp.float32),
            pltpu.VMEM((total, channels), jnp.bfloat16),
            pltpu.VMEM((blocks, LANES), jnp.int32),
            pltpu.SMEM((blocks, LANES), jnp.int32),
            pltpu.SemaphoreType.DMA((PIECES + 2,)),
        ],
        name="pack",
        cost_estimate=pl.CostEstimate(flops=10**8, bytes_accessed=4 * 10**6, transcendentals=0),
    )(owner.reshape(blocks, LANES), cell.reshape(blocks, LANES), rows)


WAYS = 8


def add_kernel(capacity, got_ref, base_hbm, ends_ref, edges_ref, out_ref, front_ref, side_ref,
               corner_ref, wide, slot_vmem, slot_smem, sems, *sums):
    span_x, span_y, span_z, channels = out_ref.shape
    cells = span_x * span_y * span_z
    total, _ = got_ref.shape
    stride = capacity + EXTRA
    devices = total // stride
    per = -(-capacity // LANES)
    width = min(LANES, capacity)
    area = span_y * span_z
    first = pltpu.make_async_copy(base_hbm, sums[0].at[pl.ds(0, cells)], sems.at[0])
    first.start()
    wide[...] = got_ref[...].astype(jnp.float32)
    for j in range(per):
        high = wide[pl.ds(capacity + j, devices, stride=stride), :].astype(jnp.int32)
        low = wide[pl.ds(capacity + per + j, devices, stride=stride), :].astype(jnp.int32)
        slot_vmem[j * devices:(j + 1) * devices, :] = jnp.where(
            high > 0, (high - 1) * LANES + low, cells)
    copy = pltpu.make_async_copy(slot_vmem, slot_smem, sems.at[1])
    copy.start()

    def clear(x, carry):
        at = pl.ds(pl.multiple_of(x * area, 8), area)
        for s in sums[1:]:
            s[at, :] = jnp.zeros((area, channels), jnp.float32)
        return carry

    lax.fori_loop(0, span_x, clear, 0)
    for s in sums[1:]:
        s[cells:cells + 8, :] = jnp.zeros((8, channels), jnp.float32)
    first.wait()
    for x in range(span_x):
        sums[0][x * area:x * area + span_z, :] = edges_ref[0, x]
        sums[0][(x + 1) * area - span_z:(x + 1) * area, :] = edges_ref[1, x]
    for k, x in ((0, 0), (1, span_x - 1)):
        sums[0][x * area:(x + 1) * area, :] = ends_ref[k].reshape(area, channels)
    copy.wait()
    for j in range(per):
        def step(o, carry):
            lines = [slot_smem.at[j * devices + o * LINES + i] for i in range(LINES)]
            starts = [pl.multiple_of((o * LINES + i) * stride + j * LANES, 8)
                      for i in range(LINES)]
            for u in range(width):
                for i in range(LINES):
                    s = sums[(u * LINES + i) % len(sums)]
                    s[pl.ds(lines[i][u], 1), :] += wide[pl.ds(starts[i] + u, 1), :]
            return carry

        lax.fori_loop(0, devices // LINES, step, 0)

    def finish(x, carry):
        at = pl.ds(pl.multiple_of(x * area, 8), area)
        value = sums[0][at, :]
        for s in sums[1:]:
            value = value + s[at, :]
        value = value.astype(jnp.bfloat16).reshape(span_y, span_z, channels)
        out_ref[x] = value
        side_ref[x] = value[span_y - 1:]
        return carry

    lax.fori_loop(0, span_x, finish, 0)
    front_ref[...] = out_ref[span_x - 1:]
    corner_ref[...] = out_ref[span_x - 1:, span_y - 1:]


def add_rows(got, base, ends, edges, shape, capacity):
    span_x, span_y, span_z, channels = shape
    cells = span_x * span_y * span_z
    total = got.shape[0]
    devices = total // (capacity + EXTRA)
    per = -(-capacity // LANES)
    vm = pl.BlockSpec(memory_space=pltpu.VMEM)
    return pl.pallas_call(
        functools.partial(add_kernel, capacity),
        out_shape=[
            jax.ShapeDtypeStruct(shape, jnp.bfloat16),
            jax.ShapeDtypeStruct((1, span_y, span_z, channels), jnp.bfloat16),
            jax.ShapeDtypeStruct((span_x, 1, span_z, channels), jnp.bfloat16),
            jax.ShapeDtypeStruct((1, 1, span_z, channels), jnp.bfloat16),
        ],
        in_specs=[vm, pl.BlockSpec(memory_space=pl.ANY), vm, vm],
        out_specs=[vm] * 4,
        scratch_shapes=[
            pltpu.VMEM((total, channels), jnp.float32),
            pltpu.VMEM((devices * per, LANES), jnp.int32),
            pltpu.SMEM((devices * per, LANES), jnp.int32),
            pltpu.SemaphoreType.DMA((2,)),
        ] + [pltpu.VMEM((cells + 8, channels), jnp.float32)] * WAYS,
        compiler_params=pltpu.CompilerParams(vmem_limit_bytes=LIMIT),
        name="add_rows",
        cost_estimate=pl.CostEstimate(flops=10**8, bytes_accessed=8 * 10**6, transcendentals=0),
    )(got, base, ends, edges)


LIMIT = 48 * 2**20


def join_taps(w_ref, wide, rows):
    channels = w_ref.shape[-1]
    for r, a in enumerate(rows):
        for d in range(2):
            for par in range(2):
                for c in range(3):
                    at = (((r * 2 + d) * 2 + par) * 3 + c) * channels
                    for s in range(2):
                        b = 2 * d + par - s
                        if 0 <= b <= 2:
                            tile = w_ref[9 * a + 3 * b + c]
                        else:
                            tile = jnp.zeros((channels, channels), jnp.bfloat16)
                        wide[at:at + channels, s * channels:(s + 1) * channels] = tile


def shifts(plane, count, span_z):
    spot = lax.broadcasted_iota(jnp.int32, (count, plane.shape[-1]), 0) % span_z
    middle = plane[8:8 + count, :]
    low = jnp.where(spot == 0, 0.0, plane[7:7 + count, :])
    high = jnp.where(spot == span_z - 1, 0.0, plane[9:9 + count, :])
    return [value.astype(jnp.bfloat16) for value in (low, middle, high)]


def spread_plane(plane, taps, start, half, span_z):
    channels = plane.shape[-1]
    lines = half * span_z
    for c, value in enumerate(shifts(plane, 2 * lines, span_z)):
        value = value.reshape(half, 2, span_z, channels)
        for par in range(2):
            at = (par * 3 + c) * channels
            taps[pl.ds(start, lines), at:at + channels] = value[:, par].reshape(lines, channels)


def residual_kernel(group, level_ref, w_ref, out_ref, ends_ref, edges_ref,
                    plane, taps, wide, result):
    span_x, span_y, span_z, channels = level_ref.shape
    half = (span_y + 2) // 2
    lines = half * span_z
    depth = 6 * channels
    count = (span_y + 2) * span_z
    join_taps(w_ref, wide, (0, 1, 2))
    plane[0:8 + span_z, :] = jnp.zeros((8 + span_z, channels), jnp.float32)
    plane[8 + count - span_z:16 + count, :] = jnp.zeros((8 + span_z, channels), jnp.float32)
    for x in (0, span_x + 1):
        taps[x * lines:(x + 1) * lines, :] = jnp.zeros((lines, depth), jnp.bfloat16)

    def fill(x, carry):
        plane[8 + span_z:8 + count - span_z, :] = level_ref[x].reshape(
            span_y * span_z, channels).astype(jnp.float32)
        spread_plane(plane, taps, pl.multiple_of((x + 1) * lines, 16), half, span_z)
        return carry

    lax.fori_loop(0, span_x, fill, 0)
    height = group * lines - span_z

    def multiply(g, carry):
        total = None
        for a in range(3):
            for d in range(2):
                start = pl.multiple_of((g * group + a) * lines + d * span_z, 16)
                at = (a * 2 + d) * depth
                part = jnp.dot(taps[pl.ds(start, height), :], wide[at:at + depth, :],
                               preferred_element_type=jnp.float32)
                total = part if total is None else total + part
        result[0:height, :] = total
        for i in range(group):
            x = g * group + i
            for s in range(2):
                value = result[i * lines:i * lines + span_y // 2 * span_z,
                               s * channels:(s + 1) * channels]
                value = value.reshape(span_y // 2, span_z, channels)
                edges_ref[s, x] = value[s * (span_y // 2 - 1)]
                if i == 0:
                    @pl.when(g == 0)
                    def _():
                        ends_ref[0, :, s] = value

                if i == group - 1:
                    @pl.when(x == span_x - 1)
                    def _():
                        ends_ref[1, :, s] = value

                here = level_ref[x].reshape(span_y // 2, 2, span_z, channels)[:, s]
                out_ref[x, :, s] = jnp.maximum(value, 0.0) + here.astype(jnp.float32)
        return carry

    lax.fori_loop(0, span_x // group, multiply, 0)


def residual_base(level, w_res, group=4):
    span_x, span_y, span_z, channels = level.shape
    lines = (span_y + 2) // 2 * span_z
    vm = pl.BlockSpec(memory_space=pltpu.VMEM)
    flops = 2 * span_x * span_y * span_z * 27 * channels * channels
    pairs = (span_y // 2, 2, span_z, channels)
    return pl.pallas_call(
        functools.partial(residual_kernel, group),
        out_shape=[
            jax.ShapeDtypeStruct((span_x,) + pairs, jnp.float32),
            jax.ShapeDtypeStruct((2,) + pairs, jnp.float32),
            jax.ShapeDtypeStruct((2, span_x, span_z, channels), jnp.float32),
        ],
        in_specs=[vm] * 2,
        out_specs=[vm] * 3,
        scratch_shapes=[
            pltpu.VMEM(((span_y + 2) * span_z + 16, channels), jnp.float32),
            pltpu.VMEM(((span_x + 2) * lines, 6 * channels), jnp.bfloat16),
            pltpu.VMEM((36 * channels, 2 * channels), jnp.bfloat16),
            pltpu.VMEM((group * lines, 2 * channels), jnp.float32),
        ],
        compiler_params=pltpu.CompilerParams(vmem_limit_bytes=26 * 2**20),
        name="residual",
        cost_estimate=pl.CostEstimate(flops=flops, bytes_accessed=8 * 10**6, transcendentals=0),
    )(level, w_res)


def border_kernel(ends_ref, edges_ref, xfirst_ref, xlast_ref, yfirst_ref, ylast_ref,
                  xlow_ref, xhigh_ref, ylow_ref, yhigh_ref, ll_ref, lh_ref, hl_ref, hh_ref,
                  w_ref, new_ends_ref, new_edges_ref, plane, taps, wide):
    _, half_y, _, span_z, channels = ends_ref.shape
    span_x = edges_ref.shape[1]
    span_y = 2 * half_y
    count = (span_y + 2) * span_z
    depth = 6 * channels
    join_taps(w_ref, wide, (0, 2))
    plane[0:8, :] = jnp.zeros((8, channels), jnp.float32)
    plane[8 + count:16 + count, :] = jnp.zeros((8, channels), jnp.float32)
    for k, (low, middle, high) in enumerate(
            ((ll_ref, xlow_ref, lh_ref), (hl_ref, xhigh_ref, hh_ref))):
        plane[8:8 + span_z, :] = low[...].reshape(span_z, channels).astype(jnp.float32)
        plane[8 + span_z:8 + count - span_z, :] = middle[...].reshape(
            span_y * span_z, channels).astype(jnp.float32)
        plane[8 + count - span_z:8 + count, :] = high[...].reshape(
            span_z, channels).astype(jnp.float32)
        spread_plane(plane, taps, 0, half_y + 1, span_z)
        change = None
        for d in range(2):
            at = (k * 2 + d) * depth
            part = jnp.dot(taps[d * span_z:(d + half_y) * span_z, :], wide[at:at + depth, :],
                           preferred_element_type=jnp.float32)
            change = part if change is None else change + part
        for s in range(2):
            value = change[:, s * channels:(s + 1) * channels].reshape(
                half_y, span_z, channels)
            new_ends_ref[k, :, s] = ends_ref[k, :, s] + value
    rows = (span_x + 2) * span_z
    for k, (source, here) in enumerate(((ylow_ref, yfirst_ref), (yhigh_ref, ylast_ref))):
        plane[8:8 + span_z, :] = jnp.zeros((span_z, channels), jnp.float32)
        plane[8 + span_z:8 + rows - span_z, :] = source[...].reshape(
            span_x * span_z, channels).astype(jnp.float32)
        plane[8 + rows - span_z:16 + rows, :] = jnp.zeros((span_z + 8, channels), jnp.float32)
        for c, value in enumerate(shifts(plane, rows, span_z)):
            taps[0:rows, c * channels:(c + 1) * channels] = value
        change = None
        for a in range(3):
            first = 9 * a + 3 * (2 * k)
            part = jnp.dot(taps[a * span_z:(a + span_x) * span_z, 0:3 * channels],
                           w_ref[first:first + 3].reshape(3 * channels, channels),
                           preferred_element_type=jnp.float32)
            change = part if change is None else change + part
        change = change.reshape(span_x, span_z, channels)
        new_edges_ref[k] = jnp.maximum(edges_ref[k] + change, 0.0) + here[...].reshape(
            span_x, span_z, channels).astype(jnp.float32)
        for e, x in ((0, 0), (1, span_x - 1)):
            new_ends_ref[e, k * (half_y - 1), k] = new_ends_ref[e, k * (half_y - 1), k] + change[x]
    for e, here in enumerate((xfirst_ref, xlast_ref)):
        new_ends_ref[e] = jnp.maximum(new_ends_ref[e], 0.0) + here[...].reshape(
            half_y, 2, span_z, channels).astype(jnp.float32)


def border(ends, edges, own, faces, w_res):
    _, half_y, _, span_z, channels = ends.shape
    span_x = edges.shape[1]
    rows = max((half_y + 1), (span_x + 2)) * span_z
    vm = pl.BlockSpec(memory_space=pltpu.VMEM)
    return pl.pallas_call(
        border_kernel,
        out_shape=[jax.ShapeDtypeStruct(ends.shape, jnp.float32),
                   jax.ShapeDtypeStruct(edges.shape, jnp.float32)],
        in_specs=[vm] * 15,
        out_specs=[vm] * 2,
        scratch_shapes=[
            pltpu.VMEM((2 * rows + 16, channels), jnp.float32),
            pltpu.VMEM((rows, 6 * channels), jnp.bfloat16),
            pltpu.VMEM((24 * channels, 2 * channels), jnp.bfloat16),
        ],
        compiler_params=pltpu.CompilerParams(vmem_limit_bytes=8 * 2**20),
        name="border",
        cost_estimate=pl.CostEstimate(flops=10**9, bytes_accessed=3 * 10**6, transcendentals=0),
    )(ends, edges, *own, *faces, w_res)


def fill_taps(plane, store, zero, half_y, half_z):
    channels = plane.shape[-1]
    span_y = 2 * half_y
    rows = (span_y + 1) * half_z
    low = jnp.where(zero, 0.0, plane[pl.ds(7, rows, stride=2), :])
    for c, value in enumerate((low, plane[pl.ds(8, rows, stride=2), :],
                               plane[pl.ds(9, rows, stride=2), :])):
        value = value.reshape(span_y + 1, half_z, channels)
        evens = value[0:span_y].reshape(half_y, 2, half_z, channels)
        odds = value[1:].reshape(half_y, 2, half_z, channels)
        for b, piece in enumerate((evens[:, 0], evens[:, 1], odds[:, 1])):
            at = (b * 3 + c) * channels
            store(at, piece.reshape(half_y * half_z, channels).astype(jnp.bfloat16))


def taps_kernel(joined_ref, taps_ref, planes):
    span_x, span_y, span_z, channels = joined_ref.shape
    half_y, half_z = span_y // 2, span_z // 2
    count = (span_y + 1) * span_z
    rows = (span_y + 1) * half_z
    zero = lax.broadcasted_iota(jnp.int32, (rows, channels), 0) % half_z == 0
    for k in range(2):
        planes[k, 0:8 + span_z, :] = jnp.zeros((8 + span_z, channels), jnp.float32)
    for x in range(span_x):
        plane = planes.at[x % 2]
        plane[8 + span_z:8 + count, :] = joined_ref[x].reshape(
            span_y * span_z, channels).astype(jnp.float32)

        def store(at, value):
            taps_ref[x % 2, x // 2, :, at:at + channels] = value

        fill_taps(plane, store, zero, half_y, half_z)


def local_taps(joined):
    span_x, span_y, span_z, channels = joined.shape
    vm = pl.BlockSpec(memory_space=pltpu.VMEM)
    return pl.pallas_call(
        taps_kernel,
        out_shape=jax.ShapeDtypeStruct(
            (2, span_x // 2, span_y * span_z // 4, 9 * channels), jnp.bfloat16),
        in_specs=[vm],
        out_specs=vm,
        scratch_shapes=[pltpu.VMEM((2, (span_y + 1) * span_z + 16, channels), jnp.float32)],
        compiler_params=pltpu.CompilerParams(vmem_limit_bytes=8 * 2**20),
        name="local_taps",
        cost_estimate=pl.CostEstimate(flops=10**7, bytes_accessed=7 * 10**6, transcendentals=0),
    )(joined)


GROUPS = 2


def lower_kernel(taps_ref, front_ref, side_ref, corner_ref, w_ref, out_ref, plane, front_taps,
                 side_taps):
    _, span_y, span_z, channels = front_ref.shape
    span_x = side_ref.shape[0]
    half_x, half_y, half_z = span_x // 2, span_y // 2, span_z // 2
    count = (span_y + 1) * span_z
    rows = (span_y + 1) * half_z
    depth = 9 * channels
    wide = w_ref.shape[-1]
    zero = lax.broadcasted_iota(jnp.int32, (rows, channels), 0) % half_z == 0
    plane[0:8, :] = jnp.zeros((8, channels), jnp.float32)
    plane[8:8 + span_x * span_z, :] = side_ref[...].reshape(
        span_x * span_z, channels).astype(jnp.float32)
    lines = span_x * half_z
    low = jnp.where(zero[0:lines], 0.0, plane[pl.ds(7, lines, stride=2), :])
    for c, value in enumerate((low, plane[pl.ds(8, lines, stride=2), :],
                               plane[pl.ds(9, lines, stride=2), :])):
        value = value.reshape(half_x, 2, half_z, channels)
        even = value[:, 0].reshape(half_x * half_z, channels)
        odd = value[:, 1].reshape(half_x * half_z, channels)
        before = jnp.concatenate(
            [jnp.zeros((half_z, channels), jnp.float32), odd[:(half_x - 1) * half_z]], axis=0)
        for a, piece in enumerate((before, even, odd)):
            side_taps[a, :, c * channels:(c + 1) * channels] = piece.astype(jnp.bfloat16)
    change = None
    for a in range(3):
        part = jnp.dot(side_taps[a], w_ref[a * depth:a * depth + 3 * channels, :],
                       preferred_element_type=jnp.float32)
        change = part if change is None else change + part
    change = change.reshape(half_x, half_z, wide)
    plane[8:8 + span_z, :] = corner_ref[...].reshape(span_z, channels).astype(jnp.float32)
    plane[8 + span_z:8 + count, :] = front_ref[...].reshape(
        span_y * span_z, channels).astype(jnp.float32)

    def store(at, value):
        front_taps[:, at:at + channels] = value

    fill_taps(plane, store, zero, half_y, half_z)
    lines = half_y * half_z
    group = half_x // GROUPS

    def product(piece, a):
        return jnp.dot(piece.reshape(-1, depth), w_ref[a * depth:(a + 1) * depth, :],
                       preferred_element_type=jnp.float32)

    for g in range(GROUPS):
        first = g * group
        total = (product(taps_ref[0, first:first + group], 1)
                 + product(taps_ref[1, first:first + group], 2))
        if g == 0:
            total = total + jnp.concatenate(
                [product(front_taps[...], 0), product(taps_ref[1, 0:group - 1], 0)], axis=0)
        else:
            total = total + product(taps_ref[1, first - 1:first + group - 1], 0)
        total = total.reshape(group, half_y, half_z, wide)
        out_ref[first:first + group, 1:] = total[:, 1:].astype(jnp.bfloat16)
        out_ref[first:first + group, 0] = (
            total[:, 0] + change[first:first + group]).astype(jnp.bfloat16)


def lower(taps, front, side, corner, w_down):
    span_x = side.shape[0]
    _, span_y, span_z, channels = front.shape
    wide = w_down.shape[-1]
    vm = pl.BlockSpec(memory_space=pltpu.VMEM)
    flops = 2 * span_x * span_y * span_z // 8 * 27 * channels * wide
    return pl.pallas_call(
        lower_kernel,
        out_shape=jax.ShapeDtypeStruct((span_x // 2, span_y // 2, span_z // 2, wide),
                                       jnp.bfloat16),
        in_specs=[vm] * 5,
        out_specs=vm,
        scratch_shapes=[
            pltpu.VMEM((max(span_y + 1, span_x) * span_z + 16, channels), jnp.float32),
            pltpu.VMEM((span_y * span_z // 4, 9 * channels), jnp.bfloat16),
            pltpu.VMEM((3, span_x * span_z // 4, 3 * channels), jnp.bfloat16),
        ],
        compiler_params=pltpu.CompilerParams(vmem_limit_bytes=28 * 2**20),
        name="lower",
        cost_estimate=pl.CostEstimate(flops=flops, bytes_accessed=5 * 10**6, transcendentals=0),
    )(taps, front, side, corner, w_down.reshape(-1, wide))


def shifted(array, by_pts, by_nbr):
    count_pts = lax.axis_size("pts")
    count_nbr = lax.axis_size("nbr")
    pairs = [
        (i * count_nbr + j, (i + by_pts) * count_nbr + j + by_nbr)
        for i in range(count_pts)
        for j in range(count_nbr)
        if 0 <= i + by_pts < count_pts and 0 <= j + by_nbr < count_nbr
    ]
    return lax.ppermute(array, ("pts", "nbr"), pairs)


def exchanged(array, devices):
    got = lax.all_to_all(
        array.reshape(devices, -1, array.shape[-1]),
        ("pts", "nbr"),
        split_axis=0,
        concat_axis=0,
        tiled=True,
    )
    return got.reshape(array.shape)


def body(points, dest_owner, dest_cell, level_input, w_res, w_down):
    devices = lax.axis_size("pts") * lax.axis_size("nbr")
    channels = points.shape[-1]
    rows = points.reshape(-1, channels)
    capacity = 2 * rows.shape[0] // devices
    outgoing = pack(dest_owner.reshape(-1), dest_cell.reshape(-1), rows, devices, capacity)
    outgoing, level = lax.optimization_barrier((outgoing, level_input))
    got = exchanged(outgoing, devices)
    x_first, x_last = level[:1], level[-1:]
    y_first, y_last = level[:, :1], level[:, -1:]
    faces = [
        shifted(x_last, 0, 1),
        shifted(x_first, 0, -1),
        shifted(y_last, 1, 0),
        shifted(y_first, -1, 0),
        shifted(level[-1:, -1:], 1, 1),
        shifted(level[-1:, :1], -1, 1),
        shifted(level[:1, -1:], 1, -1),
        shifted(level[:1, :1], -1, -1),
    ]
    base, ends, edges = residual_base(level, w_res)
    ends, edges = border(ends, edges, (x_first, x_last, y_first, y_last), faces, w_res)
    joined, front, side, corner = add_rows(
        got, base.reshape(-1, channels), ends, edges, level.shape, capacity)
    front = shifted(front, 0, 1)
    side = shifted(side, 1, 0)
    corner = shifted(corner, 1, 1)
    return lower(local_taps(joined), front, side, corner, w_down)


def solution(mesh):
    return jax.shard_map(
        body,
        mesh=mesh,
        in_specs=(
            P("pts", "nbr", None, None),
            P("pts", "nbr", None, None),
            P("pts", "nbr", None),
            P("nbr", "pts", None, None),
            P(),
            P(),
        ),
        out_specs=P("nbr", "pts", None, None),
        check_vma=False,
    )
```

```python
import functools
import jax
import jax.numpy as jnp
from jax import lax
from jax.experimental import pallas as pl
from jax.experimental.pallas import tpu as pltpu
from jax.sharding import PartitionSpec as P


LANES = 128
EXTRA = 8
PIECES = 4
LINES = 4
MOVED = 8


def pack_kernel(devices, cap, owner_ref, cell_ref, rows_hbm, out_hbm,
                rows_ref, wide, spread, staged, slot_vmem, slot_smem, sems):
    p_local, _ = rows_ref.shape
    fetch = pltpu.make_async_copy(rows_hbm, rows_ref, sems.at[PIECES + 1])
    fetch.start()
    blocks = p_local // LANES
    stride = cap + EXTRA
    upper = (lax.broadcasted_iota(jnp.int32, (LANES, LANES), 0)
             <= lax.broadcasted_iota(jnp.int32, (LANES, LANES), 1)).astype(jnp.bfloat16)
    ids = lax.broadcasted_iota(jnp.int32, (devices, LANES), 0)
    spots = lax.broadcasted_iota(jnp.int32, (cap, LANES), 0)
    base = jnp.zeros((devices, 1), jnp.float32)
    table = jnp.zeros((2 * devices, cap), jnp.float32)
    for b in range(blocks):
        own = owner_ref[b:b + 1, :]
        cell = cell_ref[b:b + 1, :]
        hit = ids == own
        hot = hit.astype(jnp.float32)
        run = jnp.dot(hot.astype(jnp.bfloat16), upper, preferred_element_type=jnp.float32)
        place = jnp.sum(hot * (run + base), axis=0, keepdims=True).astype(jnp.int32) - 1
        base = base + run[:, LANES - 1:LANES]
        slot_vmem[b:b + 1, :] = own * stride + place
        high = jnp.where(hit, (cell // LANES + 1).astype(jnp.float32), 0.0)
        low = jnp.where(hit, (cell % LANES).astype(jnp.float32), 0.0)
        left = jnp.concatenate([high, low], axis=0).astype(jnp.bfloat16)
        right = (spots == place).astype(jnp.float32).astype(jnp.bfloat16)
        if b % 2 == 0:
            left_even, right_even = left, right
        else:
            table = table + lax.dot_general(
                jnp.concatenate([left_even, left], axis=1),
                jnp.concatenate([right_even, right], axis=1),
                (((1,), (1,)), ((), ())), preferred_element_type=jnp.float32)
    copy = pltpu.make_async_copy(slot_vmem, slot_smem, sems.at[PIECES])
    copy.start()
    fetch.wait()

    def widen(i, carry):
        at = pl.ds(pl.multiple_of(i * 2 * LANES, 16), 2 * LANES)
        wide[at, :] = rows_ref[at, :].astype(jnp.float32)
        return carry

    lax.fori_loop(0, p_local // (2 * LANES), widen, 0)
    per = -(-cap // LANES)
    for part in range(2):
        for j in range(per):
            width = min(LANES, cap - j * LANES)
            piece = table[part * devices:(part + 1) * devices, j * LANES:j * LANES + width]
            if width < LANES:
                piece = jnp.concatenate(
                    [piece, jnp.zeros((devices, LANES - width), jnp.float32)], axis=1)
            spread[pl.ds(cap + part * per + j, devices, stride=stride), :] = piece
    copy.wait()

    def step(b, carry):
        lines = [slot_smem.at[b * MOVED + i] for i in range(MOVED)]
        for u in range(LANES):
            for i in range(MOVED):
                spread[pl.ds(lines[i][u], 1), :] = wide[
                    pl.ds((b * MOVED + i) * LANES + u, 1), :]
        return carry

    lax.fori_loop(0, blocks // MOVED, step, 0)
    piece = staged.shape[0] // PIECES
    sends = []
    for i in range(PIECES):
        part = pl.ds(i * piece, piece)
        staged[part, :] = spread[part, :].astype(jnp.bfloat16)
        sends.append(pltpu.make_async_copy(staged.at[part], out_hbm.at[part], sems.at[i]))
        sends[-1].start()
    for send in sends:
        send.wait()


def pack(owner, cell, rows, devices, cap):
    p_local, channels = rows.shape
    blocks = p_local // LANES
    total = devices * (cap + EXTRA)
    vm = pl.BlockSpec(memory_space=pltpu.VMEM)
    hbm = pl.BlockSpec(memory_space=pl.ANY)
    return pl.pallas_call(
        functools.partial(pack_kernel, devices, cap),
        out_shape=jax.ShapeDtypeStruct((total, channels), jnp.bfloat16),
        in_specs=[vm, vm, hbm],
        out_specs=hbm,
        scratch_shapes=[
            pltpu.VMEM((p_local, channels), jnp.bfloat16),
            pltpu.VMEM((p_local, channels), jnp.float32),
            pltpu.VMEM((total, channels), jnp.float32),
            pltpu.VMEM((total, channels), jnp.bfloat16),
            pltpu.VMEM((blocks, LANES), jnp.int32),
            pltpu.SMEM((blocks, LANES), jnp.int32),
            pltpu.SemaphoreType.DMA((PIECES + 2,)),
        ],
        name="pack",
        cost_estimate=pl.CostEstimate(flops=10**8, bytes_accessed=4 * 10**6, transcendentals=0),
    )(owner.reshape(blocks, LANES), cell.reshape(blocks, LANES), rows)


WAYS = 8


def add_kernel(capacity, got_ref, base_hbm, ends_ref, edges_ref, out_ref, front_ref, side_ref,
               corner_ref, wide, slot_vmem, slot_smem, sems, *sums):
    span_x, span_y, span_z, channels = out_ref.shape
    cells = span_x * span_y * span_z
    total, _ = got_ref.shape
    stride = capacity + EXTRA
    devices = total // stride
    per = -(-capacity // LANES)
    width = min(LANES, capacity)
    area = span_y * span_z
    first = pltpu.make_async_copy(base_hbm, sums[0].at[pl.ds(0, cells)], sems.at[0])
    first.start()
    wide[...] = got_ref[...].astype(jnp.float32)
    for j in range(per):
        high = wide[pl.ds(capacity + j, devices, stride=stride), :].astype(jnp.int32)
        low = wide[pl.ds(capacity + per + j, devices, stride=stride), :].astype(jnp.int32)
        slot_vmem[j * devices:(j + 1) * devices, :] = jnp.where(
            high > 0, (high - 1) * LANES + low, cells)
    copy = pltpu.make_async_copy(slot_vmem, slot_smem, sems.at[1])
    copy.start()

    def clear(x, carry):
        at = pl.ds(pl.multiple_of(x * area, 8), area)
        for s in sums[1:]:
            s[at, :] = jnp.zeros((area, channels), jnp.float32)
        return carry

    lax.fori_loop(0, span_x, clear, 0)
    for s in sums[1:]:
        s[cells:cells + 8, :] = jnp.zeros((8, channels), jnp.float32)
    first.wait()
    for x in range(span_x):
        sums[0][x * area:x * area + span_z, :] = edges_ref[0, x]
        sums[0][(x + 1) * area - span_z:(x + 1) * area, :] = edges_ref[1, x]
    for k, x in ((0, 0), (1, span_x - 1)):
        sums[0][x * area:(x + 1) * area, :] = ends_ref[k].reshape(area, channels)
    copy.wait()
    for j in range(per):
        def step(o, carry):
            lines = [slot_smem.at[j * devices + o * LINES + i] for i in range(LINES)]
            starts = [pl.multiple_of((o * LINES + i) * stride + j * LANES, 8)
                      for i in range(LINES)]
            for u in range(width):
                for i in range(LINES):
                    s = sums[(u * LINES + i) % len(sums)]
                    s[pl.ds(lines[i][u], 1), :] += wide[pl.ds(starts[i] + u, 1), :]
            return carry

        lax.fori_loop(0, devices // LINES, step, 0)

    def finish(x, carry):
        at = pl.ds(pl.multiple_of(x * area, 8), area)
        value = sums[0][at, :]
        for s in sums[1:]:
            value = value + s[at, :]
        value = value.astype(jnp.bfloat16).reshape(span_y, span_z, channels)
        out_ref[x] = value
        side_ref[x] = value[span_y - 1:]
        return carry

    lax.fori_loop(0, span_x, finish, 0)
    front_ref[...] = out_ref[span_x - 1:]
    corner_ref[...] = out_ref[span_x - 1:, span_y - 1:]


def add_rows(got, base, ends, edges, shape, capacity):
    span_x, span_y, span_z, channels = shape
    cells = span_x * span_y * span_z
    total = got.shape[0]
    devices = total // (capacity + EXTRA)
    per = -(-capacity // LANES)
    vm = pl.BlockSpec(memory_space=pltpu.VMEM)
    return pl.pallas_call(
        functools.partial(add_kernel, capacity),
        out_shape=[
            jax.ShapeDtypeStruct(shape, jnp.bfloat16),
            jax.ShapeDtypeStruct((1, span_y, span_z, channels), jnp.bfloat16),
            jax.ShapeDtypeStruct((span_x, 1, span_z, channels), jnp.bfloat16),
            jax.ShapeDtypeStruct((1, 1, span_z, channels), jnp.bfloat16),
        ],
        in_specs=[vm, pl.BlockSpec(memory_space=pl.ANY), vm, vm],
        out_specs=[vm] * 4,
        scratch_shapes=[
            pltpu.VMEM((total, channels), jnp.float32),
            pltpu.VMEM((devices * per, LANES), jnp.int32),
            pltpu.SMEM((devices * per, LANES), jnp.int32),
            pltpu.SemaphoreType.DMA((2,)),
        ] + [pltpu.VMEM((cells + 8, channels), jnp.float32)] * WAYS,
        compiler_params=pltpu.CompilerParams(vmem_limit_bytes=LIMIT),
        name="add_rows",
        cost_estimate=pl.CostEstimate(flops=10**8, bytes_accessed=8 * 10**6, transcendentals=0),
    )(got, base, ends, edges)


LIMIT = 48 * 2**20


def join_taps(w_ref, wide, rows):
    channels = w_ref.shape[-1]
    for r, a in enumerate(rows):
        for d in range(2):
            for par in range(2):
                for c in range(3):
                    at = (((r * 2 + d) * 2 + par) * 3 + c) * channels
                    for s in range(2):
                        b = 2 * d + par - s
                        if 0 <= b <= 2:
                            tile = w_ref[9 * a + 3 * b + c]
                        else:
                            tile = jnp.zeros((channels, channels), jnp.bfloat16)
                        wide[at:at + channels, s * channels:(s + 1) * channels] = tile


def shifts(plane, count, span_z):
    spot = lax.broadcasted_iota(jnp.int32, (count, plane.shape[-1]), 0) % span_z
    middle = plane[8:8 + count, :]
    low = jnp.where(spot == 0, 0.0, plane[7:7 + count, :])
    high = jnp.where(spot == span_z - 1, 0.0, plane[9:9 + count, :])
    return [value.astype(jnp.bfloat16) for value in (low, middle, high)]


def spread_plane(plane, taps, start, half, span_z):
    channels = plane.shape[-1]
    lines = half * span_z
    for c, value in enumerate(shifts(plane, 2 * lines, span_z)):
        value = value.reshape(half, 2, span_z, channels)
        for par in range(2):
            at = (par * 3 + c) * channels
            taps[pl.ds(start, lines), at:at + channels] = value[:, par].reshape(lines, channels)


def residual_kernel(group, level_ref, w_ref, out_ref, ends_ref, edges_ref,
                    plane, taps, wide, result):
    span_x, span_y, span_z, channels = level_ref.shape
    half = (span_y + 2) // 2
    lines = half * span_z
    depth = 6 * channels
    count = (span_y + 2) * span_z
    join_taps(w_ref, wide, (0, 1, 2))
    plane[0:8 + span_z, :] = jnp.zeros((8 + span_z, channels), jnp.float32)
    plane[8 + count - span_z:16 + count, :] = jnp.zeros((8 + span_z, channels), jnp.float32)
    for x in (0, span_x + 1):
        taps[x * lines:(x + 1) * lines, :] = jnp.zeros((lines, depth), jnp.bfloat16)

    def fill(x, carry):
        plane[8 + span_z:8 + count - span_z, :] = level_ref[x].reshape(
            span_y * span_z, channels).astype(jnp.float32)
        spread_plane(plane, taps, pl.multiple_of((x + 1) * lines, 16), half, span_z)
        return carry

    lax.fori_loop(0, span_x, fill, 0)
    height = group * lines - span_z

    def multiply(g, carry):
        total = None
        for a in range(3):
            for d in range(2):
                start = pl.multiple_of((g * group + a) * lines + d * span_z, 16)
                at = (a * 2 + d) * depth
                part = jnp.dot(taps[pl.ds(start, height), :], wide[at:at + depth, :],
                               preferred_element_type=jnp.float32)
                total = part if total is None else total + part
        result[0:height, :] = total
        for i in range(group):
            x = g * group + i
            for s in range(2):
                value = result[i * lines:i * lines + span_y // 2 * span_z,
                               s * channels:(s + 1) * channels]
                value = value.reshape(span_y // 2, span_z, channels)
                edges_ref[s, x] = value[s * (span_y // 2 - 1)]
                if i == 0:
                    @pl.when(g == 0)
                    def _():
                        ends_ref[0, :, s] = value

                if i == group - 1:
                    @pl.when(x == span_x - 1)
                    def _():
                        ends_ref[1, :, s] = value

                here = level_ref[x].reshape(span_y // 2, 2, span_z, channels)[:, s]
                out_ref[x, :, s] = jnp.maximum(value, 0.0) + here.astype(jnp.float32)
        return carry

    lax.fori_loop(0, span_x // group, multiply, 0)


def residual_base(level, w_res, group=4):
    span_x, span_y, span_z, channels = level.shape
    lines = (span_y + 2) // 2 * span_z
    vm = pl.BlockSpec(memory_space=pltpu.VMEM)
    flops = 2 * span_x * span_y * span_z * 27 * channels * channels
    pairs = (span_y // 2, 2, span_z, channels)
    return pl.pallas_call(
        functools.partial(residual_kernel, group),
        out_shape=[
            jax.ShapeDtypeStruct((span_x,) + pairs, jnp.float32),
            jax.ShapeDtypeStruct((2,) + pairs, jnp.float32),
            jax.ShapeDtypeStruct((2, span_x, span_z, channels), jnp.float32),
        ],
        in_specs=[vm] * 2,
        out_specs=[vm] * 3,
        scratch_shapes=[
            pltpu.VMEM(((span_y + 2) * span_z + 16, channels), jnp.float32),
            pltpu.VMEM(((span_x + 2) * lines, 6 * channels), jnp.bfloat16),
            pltpu.VMEM((36 * channels, 2 * channels), jnp.bfloat16),
            pltpu.VMEM((group * lines, 2 * channels), jnp.float32),
        ],
        compiler_params=pltpu.CompilerParams(vmem_limit_bytes=26 * 2**20),
        name="residual",
        cost_estimate=pl.CostEstimate(flops=flops, bytes_accessed=8 * 10**6, transcendentals=0),
    )(level, w_res)


def border_kernel(ends_ref, edges_ref, xfirst_ref, xlast_ref, yfirst_ref, ylast_ref,
                  xlow_ref, xhigh_ref, ylow_ref, yhigh_ref, ll_ref, lh_ref, hl_ref, hh_ref,
                  w_ref, new_ends_ref, new_edges_ref, plane, taps, wide):
    _, half_y, _, span_z, channels = ends_ref.shape
    span_x = edges_ref.shape[1]
    span_y = 2 * half_y
    count = (span_y + 2) * span_z
    depth = 6 * channels
    join_taps(w_ref, wide, (0, 2))
    plane[0:8, :] = jnp.zeros((8, channels), jnp.float32)
    plane[8 + count:16 + count, :] = jnp.zeros((8, channels), jnp.float32)
    for k, (low, middle, high) in enumerate(
            ((ll_ref, xlow_ref, lh_ref), (hl_ref, xhigh_ref, hh_ref))):
        plane[8:8 + span_z, :] = low[...].reshape(span_z, channels).astype(jnp.float32)
        plane[8 + span_z:8 + count - span_z, :] = middle[...].reshape(
            span_y * span_z, channels).astype(jnp.float32)
        plane[8 + count - span_z:8 + count, :] = high[...].reshape(
            span_z, channels).astype(jnp.float32)
        spread_plane(plane, taps, 0, half_y + 1, span_z)
        change = None
        for d in range(2):
            at = (k * 2 + d) * depth
            part = jnp.dot(taps[d * span_z:(d + half_y) * span_z, :], wide[at:at + depth, :],
                           preferred_element_type=jnp.float32)
            change = part if change is None else change + part
        for s in range(2):
            value = change[:, s * channels:(s + 1) * channels].reshape(
                half_y, span_z, channels)
            new_ends_ref[k, :, s] = ends_ref[k, :, s] + value
    rows = (span_x + 2) * span_z
    for k, (source, here) in enumerate(((ylow_ref, yfirst_ref), (yhigh_ref, ylast_ref))):
        plane[8:8 + span_z, :] = jnp.zeros((span_z, channels), jnp.float32)
        plane[8 + span_z:8 + rows - span_z, :] = source[...].reshape(
            span_x * span_z, channels).astype(jnp.float32)
        plane[8 + rows - span_z:16 + rows, :] = jnp.zeros((span_z + 8, channels), jnp.float32)
        for c, value in enumerate(shifts(plane, rows, span_z)):
            taps[0:rows, c * channels:(c + 1) * channels] = value
        change = None
        for a in range(3):
            first = 9 * a + 3 * (2 * k)
            part = jnp.dot(taps[a * span_z:(a + span_x) * span_z, 0:3 * channels],
                           w_ref[first:first + 3].reshape(3 * channels, channels),
                           preferred_element_type=jnp.float32)
            change = part if change is None else change + part
        change = change.reshape(span_x, span_z, channels)
        new_edges_ref[k] = jnp.maximum(edges_ref[k] + change, 0.0) + here[...].reshape(
            span_x, span_z, channels).astype(jnp.float32)
        for e, x in ((0, 0), (1, span_x - 1)):
            new_ends_ref[e, k * (half_y - 1), k] = new_ends_ref[e, k * (half_y - 1), k] + change[x]
    for e, here in enumerate((xfirst_ref, xlast_ref)):
        new_ends_ref[e] = jnp.maximum(new_ends_ref[e], 0.0) + here[...].reshape(
            half_y, 2, span_z, channels).astype(jnp.float32)


def border(ends, edges, own, faces, w_res):
    _, half_y, _, span_z, channels = ends.shape
    span_x = edges.shape[1]
    rows = max((half_y + 1), (span_x + 2)) * span_z
    vm = pl.BlockSpec(memory_space=pltpu.VMEM)
    return pl.pallas_call(
        border_kernel,
        out_shape=[jax.ShapeDtypeStruct(ends.shape, jnp.float32),
                   jax.ShapeDtypeStruct(edges.shape, jnp.float32)],
        in_specs=[vm] * 15,
        out_specs=[vm] * 2,
        scratch_shapes=[
            pltpu.VMEM((2 * rows + 16, channels), jnp.float32),
            pltpu.VMEM((rows, 6 * channels), jnp.bfloat16),
            pltpu.VMEM((24 * channels, 2 * channels), jnp.bfloat16),
        ],
        compiler_params=pltpu.CompilerParams(vmem_limit_bytes=8 * 2**20),
        name="border",
        cost_estimate=pl.CostEstimate(flops=10**9, bytes_accessed=3 * 10**6, transcendentals=0),
    )(ends, edges, *own, *faces, w_res)


def fill_taps(plane, store, zero, half_y, half_z):
    channels = plane.shape[-1]
    span_y = 2 * half_y
    rows = (span_y + 1) * half_z
    low = jnp.where(zero, 0.0, plane[pl.ds(7, rows, stride=2), :])
    for c, value in enumerate((low, plane[pl.ds(8, rows, stride=2), :],
                               plane[pl.ds(9, rows, stride=2), :])):
        value = value.reshape(span_y + 1, half_z, channels)
        evens = value[0:span_y].reshape(half_y, 2, half_z, channels)
        odds = value[1:].reshape(half_y, 2, half_z, channels)
        for b, piece in enumerate((evens[:, 0], evens[:, 1], odds[:, 1])):
            at = (b * 3 + c) * channels
            store(at, piece.reshape(half_y * half_z, channels).astype(jnp.bfloat16))


def taps_kernel(joined_ref, taps_ref, planes):
    span_x, span_y, span_z, channels = joined_ref.shape
    half_y, half_z = span_y // 2, span_z // 2
    count = (span_y + 1) * span_z
    rows = (span_y + 1) * half_z
    zero = lax.broadcasted_iota(jnp.int32, (rows, channels), 0) % half_z == 0
    for k in range(2):
        planes[k, 0:8 + span_z, :] = jnp.zeros((8 + span_z, channels), jnp.float32)
    for x in range(span_x):
        plane = planes.at[x % 2]
        plane[8 + span_z:8 + count, :] = joined_ref[x].reshape(
            span_y * span_z, channels).astype(jnp.float32)

        def store(at, value):
            taps_ref[x % 2, x // 2, :, at:at + channels] = value

        fill_taps(plane, store, zero, half_y, half_z)


def local_taps(joined):
    span_x, span_y, span_z, channels = joined.shape
    vm = pl.BlockSpec(memory_space=pltpu.VMEM)
    return pl.pallas_call(
        taps_kernel,
        out_shape=jax.ShapeDtypeStruct(
            (2, span_x // 2, span_y * span_z // 4, 9 * channels), jnp.bfloat16),
        in_specs=[vm],
        out_specs=vm,
        scratch_shapes=[pltpu.VMEM((2, (span_y + 1) * span_z + 16, channels), jnp.float32)],
        compiler_params=pltpu.CompilerParams(vmem_limit_bytes=8 * 2**20),
        name="local_taps",
        cost_estimate=pl.CostEstimate(flops=10**7, bytes_accessed=7 * 10**6, transcendentals=0),
    )(joined)


GROUPS = 2


def lower_kernel(taps_ref, front_ref, side_ref, corner_ref, w_ref, out_ref, plane, front_taps,
                 side_taps):
    _, span_y, span_z, channels = front_ref.shape
    span_x = side_ref.shape[0]
    half_x, half_y, half_z = span_x // 2, span_y // 2, span_z // 2
    count = (span_y + 1) * span_z
    rows = (span_y + 1) * half_z
    depth = 9 * channels
    wide = w_ref.shape[-1]
    zero = lax.broadcasted_iota(jnp.int32, (rows, channels), 0) % half_z == 0
    plane[0:8, :] = jnp.zeros((8, channels), jnp.float32)
    plane[8:8 + span_x * span_z, :] = side_ref[...].reshape(
        span_x * span_z, channels).astype(jnp.float32)
    lines = span_x * half_z
    low = jnp.where(zero[0:lines], 0.0, plane[pl.ds(7, lines, stride=2), :])
    for c, value in enumerate((low, plane[pl.ds(8, lines, stride=2), :],
                               plane[pl.ds(9, lines, stride=2), :])):
        value = value.reshape(half_x, 2, half_z, channels)
        even = value[:, 0].reshape(half_x * half_z, channels)
        odd = value[:, 1].reshape(half_x * half_z, channels)
        before = jnp.concatenate(
            [jnp.zeros((half_z, channels), jnp.float32), odd[:(half_x - 1) * half_z]], axis=0)
        for a, piece in enumerate((before, even, odd)):
            side_taps[a, :, c * channels:(c + 1) * channels] = piece.astype(jnp.bfloat16)
    change = None
    for a in range(3):
        part = jnp.dot(side_taps[a], w_ref[a * depth:a * depth + 3 * channels, :],
                       preferred_element_type=jnp.float32)
        change = part if change is None else change + part
    change = change.reshape(half_x, half_z, wide)
    plane[8:8 + span_z, :] = corner_ref[...].reshape(span_z, channels).astype(jnp.float32)
    plane[8 + span_z:8 + count, :] = front_ref[...].reshape(
        span_y * span_z, channels).astype(jnp.float32)

    def store(at, value):
        front_taps[:, at:at + channels] = value

    fill_taps(plane, store, zero, half_y, half_z)
    lines = half_y * half_z
    group = half_x // GROUPS

    def product(piece, a):
        return jnp.dot(piece.reshape(-1, depth), w_ref[a * depth:(a + 1) * depth, :],
                       preferred_element_type=jnp.float32)

    for g in range(GROUPS):
        first = g * group
        total = (product(taps_ref[0, first:first + group], 1)
                 + product(taps_ref[1, first:first + group], 2))
        if g == 0:
            total = total + jnp.concatenate(
                [product(front_taps[...], 0), product(taps_ref[1, 0:group - 1], 0)], axis=0)
        else:
            total = total + product(taps_ref[1, first - 1:first + group - 1], 0)
        total = total.reshape(group, half_y, half_z, wide)
        out_ref[first:first + group, 1:] = total[:, 1:].astype(jnp.bfloat16)
        out_ref[first:first + group, 0] = (
            total[:, 0] + change[first:first + group]).astype(jnp.bfloat16)


def lower(taps, front, side, corner, w_down):
    span_x = side.shape[0]
    _, span_y, span_z, channels = front.shape
    wide = w_down.shape[-1]
    vm = pl.BlockSpec(memory_space=pltpu.VMEM)
    flops = 2 * span_x * span_y * span_z // 8 * 27 * channels * wide
    return pl.pallas_call(
        lower_kernel,
        out_shape=jax.ShapeDtypeStruct((span_x // 2, span_y // 2, span_z // 2, wide),
                                       jnp.bfloat16),
        in_specs=[vm] * 5,
        out_specs=vm,
        scratch_shapes=[
            pltpu.VMEM((max(span_y + 1, span_x) * span_z + 16, channels), jnp.float32),
            pltpu.VMEM((span_y * span_z // 4, 9 * channels), jnp.bfloat16),
            pltpu.VMEM((3, span_x * span_z // 4, 3 * channels), jnp.bfloat16),
        ],
        compiler_params=pltpu.CompilerParams(vmem_limit_bytes=28 * 2**20),
        name="lower",
        cost_estimate=pl.CostEstimate(flops=flops, bytes_accessed=5 * 10**6, transcendentals=0),
    )(taps, front, side, corner, w_down.reshape(-1, wide))


def shifted(array, by_pts, by_nbr):
    count_pts = lax.axis_size("pts")
    count_nbr = lax.axis_size("nbr")
    pairs = [
        (i * count_nbr + j, (i + by_pts) * count_nbr + j + by_nbr)
        for i in range(count_pts)
        for j in range(count_nbr)
        if 0 <= i + by_pts < count_pts and 0 <= j + by_nbr < count_nbr
    ]
    return lax.ppermute(array, ("pts", "nbr"), pairs)


def exchanged(array, devices):
    got = lax.all_to_all(
        array.reshape(devices, -1, array.shape[-1]),
        ("pts", "nbr"),
        split_axis=0,
        concat_axis=0,
        tiled=True,
    )
    return got.reshape(array.shape)


def body(points, dest_owner, dest_cell, level_input, w_res, w_down):
    devices = lax.axis_size("pts") * lax.axis_size("nbr")
    channels = points.shape[-1]
    rows = points.reshape(-1, channels)
    capacity = 2 * rows.shape[0] // devices
    outgoing = pack(dest_owner.reshape(-1), dest_cell.reshape(-1), rows, devices, capacity)
    outgoing, level = lax.optimization_barrier((outgoing, level_input))
    got = exchanged(outgoing, devices)
    x_first, x_last = level[:1], level[-1:]
    y_first, y_last = level[:, :1], level[:, -1:]
    faces = [
        shifted(x_last, 0, 1),
        shifted(x_first, 0, -1),
        shifted(y_last, 1, 0),
        shifted(y_first, -1, 0),
        shifted(level[-1:, -1:], 1, 1),
        shifted(level[-1:, :1], -1, 1),
        shifted(level[:1, -1:], 1, -1),
        shifted(level[:1, :1], -1, -1),
    ]
    base, ends, edges = residual_base(level, w_res)
    ends, edges = border(ends, edges, (x_first, x_last, y_first, y_last), faces, w_res)
    joined, front, side, corner = add_rows(
        got, base.reshape(-1, channels), ends, edges, level.shape, capacity)
    front = shifted(front, 0, 1)
    side = shifted(side, 1, 0)
    corner = shifted(corner, 1, 1)
    return lower(local_taps(joined), front, side, corner, w_down)


def solution(mesh):
    return jax.shard_map(
        body,
        mesh=mesh,
        in_specs=(
            P("pts", "nbr", None, None),
            P("pts", "nbr", None, None),
            P("pts", "nbr", None),
            P("nbr", "pts", None, None),
            P(),
            P(),
        ),
        out_specs=P("nbr", "pts", None, None),
        check_vma=False,
    )
```

```python
import functools
import jax
import jax.numpy as jnp
from jax import lax
from jax.experimental import pallas as pl
from jax.experimental.pallas import tpu as pltpu
from jax.sharding import PartitionSpec as P


LANES = 128
EXTRA = 8
PIECES = 4
LINES = 4
MOVED = 8


def pack_kernel(devices, cap, owner_ref, cell_ref, rows_hbm, out_hbm,
                rows_ref, wide, spread, staged, slot_vmem, slot_smem, sems):
    p_local, _ = rows_ref.shape
    fetch = pltpu.make_async_copy(rows_hbm, rows_ref, sems.at[PIECES + 1])
    fetch.start()
    blocks = p_local // LANES
    stride = cap + EXTRA
    upper = (lax.broadcasted_iota(jnp.int32, (LANES, LANES), 0)
             <= lax.broadcasted_iota(jnp.int32, (LANES, LANES), 1)).astype(jnp.bfloat16)
    ids = lax.broadcasted_iota(jnp.int32, (devices, LANES), 0)
    spots = lax.broadcasted_iota(jnp.int32, (cap, LANES), 0)
    base = jnp.zeros((devices, 1), jnp.float32)
    table = jnp.zeros((2 * devices, cap), jnp.float32)
    lefts, rights = [], []
    for b in range(blocks):
        own = owner_ref[b:b + 1, :]
        cell = cell_ref[b:b + 1, :]
        hit = ids == own
        hot = hit.astype(jnp.float32)
        run = jnp.dot(hot.astype(jnp.bfloat16), upper, preferred_element_type=jnp.float32)
        place = jnp.sum(hot * (run + base), axis=0, keepdims=True).astype(jnp.int32) - 1
        base = base + run[:, LANES - 1:LANES]
        slot_vmem[b:b + 1, :] = own * stride + place
        high = jnp.where(hit, (cell // LANES + 1).astype(jnp.float32), 0.0)
        low = jnp.where(hit, (cell % LANES).astype(jnp.float32), 0.0)
        left = jnp.concatenate([high, low], axis=0).astype(jnp.bfloat16)
        right = (spots == place).astype(jnp.float32).astype(jnp.bfloat16)
        lefts.append(left)
        rights.append(right)
        if len(lefts) == 4 or b == blocks - 1:
            table = table + lax.dot_general(
                jnp.concatenate(lefts, axis=1), jnp.concatenate(rights, axis=1),
                (((1,), (1,)), ((), ())), preferred_element_type=jnp.float32)
            lefts, rights = [], []
    copy = pltpu.make_async_copy(slot_vmem, slot_smem, sems.at[PIECES])
    copy.start()
    fetch.wait()

    def widen(i, carry):
        at = pl.ds(pl.multiple_of(i * 2 * LANES, 16), 2 * LANES)
        wide[at, :] = rows_ref[at, :].astype(jnp.float32)
        return carry

    lax.fori_loop(0, p_local // (2 * LANES), widen, 0)
    per = -(-cap // LANES)
    for part in range(2):
        for j in range(per):
            width = min(LANES, cap - j * LANES)
            piece = table[part * devices:(part + 1) * devices, j * LANES:j * LANES + width]
            if width < LANES:
                piece = jnp.concatenate(
                    [piece, jnp.zeros((devices, LANES - width), jnp.float32)], axis=1)
            spread[pl.ds(cap + part * per + j, devices, stride=stride), :] = piece
    copy.wait()

    def step(b, carry):
        lines = [slot_smem.at[b * MOVED + i] for i in range(MOVED)]
        for u in range(LANES):
            for i in range(MOVED):
                spread[pl.ds(lines[i][u], 1), :] = wide[
                    pl.ds((b * MOVED + i) * LANES + u, 1), :]
        return carry

    lax.fori_loop(0, blocks // MOVED, step, 0)
    piece = staged.shape[0] // PIECES
    sends = []
    for i in range(PIECES):
        part = pl.ds(i * piece, piece)
        staged[part, :] = spread[part, :].astype(jnp.bfloat16)
        sends.append(pltpu.make_async_copy(staged.at[part], out_hbm.at[part], sems.at[i]))
        sends[-1].start()
    for send in sends:
        send.wait()


def pack(owner, cell, rows, devices, cap):
    p_local, channels = rows.shape
    blocks = p_local // LANES
    total = devices * (cap + EXTRA)
    vm = pl.BlockSpec(memory_space=pltpu.VMEM)
    hbm = pl.BlockSpec(memory_space=pl.ANY)
    return pl.pallas_call(
        functools.partial(pack_kernel, devices, cap),
        out_shape=jax.ShapeDtypeStruct((total, channels), jnp.bfloat16),
        in_specs=[vm, vm, hbm],
        out_specs=hbm,
        scratch_shapes=[
            pltpu.VMEM((p_local, channels), jnp.bfloat16),
            pltpu.VMEM((p_local, channels), jnp.float32),
            pltpu.VMEM((total, channels), jnp.float32),
            pltpu.VMEM((total, channels), jnp.bfloat16),
            pltpu.VMEM((blocks, LANES), jnp.int32),
            pltpu.SMEM((blocks, LANES), jnp.int32),
            pltpu.SemaphoreType.DMA((PIECES + 2,)),
        ],
        name="pack",
        cost_estimate=pl.CostEstimate(flops=10**8, bytes_accessed=4 * 10**6, transcendentals=0),
    )(owner.reshape(blocks, LANES), cell.reshape(blocks, LANES), rows)


WAYS = 8


def add_kernel(capacity, got_ref, base_hbm, ends_ref, edges_ref, out_ref, front_ref, side_ref,
               corner_ref, wide, slot_vmem, slot_smem, sems, *sums):
    span_x, span_y, span_z, channels = out_ref.shape
    cells = span_x * span_y * span_z
    total, _ = got_ref.shape
    stride = capacity + EXTRA
    devices = total // stride
    per = -(-capacity // LANES)
    width = min(LANES, capacity)
    area = span_y * span_z
    first = pltpu.make_async_copy(base_hbm, sums[0].at[pl.ds(0, cells)], sems.at[0])
    first.start()
    wide[...] = got_ref[...].astype(jnp.float32)
    for j in range(per):
        high = wide[pl.ds(capacity + j, devices, stride=stride), :].astype(jnp.int32)
        low = wide[pl.ds(capacity + per + j, devices, stride=stride), :].astype(jnp.int32)
        slot_vmem[j * devices:(j + 1) * devices, :] = jnp.where(
            high > 0, (high - 1) * LANES + low, cells)
    copy = pltpu.make_async_copy(slot_vmem, slot_smem, sems.at[1])
    copy.start()

    def clear(x, carry):
        at = pl.ds(pl.multiple_of(x * area, 8), area)
        for s in sums[1:]:
            s[at, :] = jnp.zeros((area, channels), jnp.float32)
        return carry

    lax.fori_loop(0, span_x, clear, 0)
    for s in sums[1:]:
        s[cells:cells + 8, :] = jnp.zeros((8, channels), jnp.float32)
    first.wait()
    for x in range(span_x):
        sums[0][x * area:x * area + span_z, :] = edges_ref[0, x]
        sums[0][(x + 1) * area - span_z:(x + 1) * area, :] = edges_ref[1, x]
    for k, x in ((0, 0), (1, span_x - 1)):
        sums[0][x * area:(x + 1) * area, :] = ends_ref[k].reshape(area, channels)
    copy.wait()
    for j in range(per):
        def step(o, carry):
            lines = [slot_smem.at[j * devices + o * LINES + i] for i in range(LINES)]
            starts = [pl.multiple_of((o * LINES + i) * stride + j * LANES, 8)
                      for i in range(LINES)]
            for u in range(width):
                for i in range(LINES):
                    s = sums[(u * LINES + i) % len(sums)]
                    s[pl.ds(lines[i][u], 1), :] += wide[pl.ds(starts[i] + u, 1), :]
            return carry

        lax.fori_loop(0, devices // LINES, step, 0)

    def finish(x, carry):
        at = pl.ds(pl.multiple_of(x * area, 8), area)
        value = sums[0][at, :]
        for s in sums[1:]:
            value = value + s[at, :]
        value = value.astype(jnp.bfloat16).reshape(span_y, span_z, channels)
        out_ref[x] = value
        side_ref[x] = value[span_y - 1:]
        return carry

    lax.fori_loop(0, span_x, finish, 0)
    front_ref[...] = out_ref[span_x - 1:]
    corner_ref[...] = out_ref[span_x - 1:, span_y - 1:]


def add_rows(got, base, ends, edges, shape, capacity):
    span_x, span_y, span_z, channels = shape
    cells = span_x * span_y * span_z
    total = got.shape[0]
    devices = total // (capacity + EXTRA)
    per = -(-capacity // LANES)
    vm = pl.BlockSpec(memory_space=pltpu.VMEM)
    return pl.pallas_call(
        functools.partial(add_kernel, capacity),
        out_shape=[
            jax.ShapeDtypeStruct(shape, jnp.bfloat16),
            jax.ShapeDtypeStruct((1, span_y, span_z, channels), jnp.bfloat16),
            jax.ShapeDtypeStruct((span_x, 1, span_z, channels), jnp.bfloat16),
            jax.ShapeDtypeStruct((1, 1, span_z, channels), jnp.bfloat16),
        ],
        in_specs=[vm, pl.BlockSpec(memory_space=pl.ANY), vm, vm],
        out_specs=[vm] * 4,
        scratch_shapes=[
            pltpu.VMEM((total, channels), jnp.float32),
            pltpu.VMEM((devices * per, LANES), jnp.int32),
            pltpu.SMEM((devices * per, LANES), jnp.int32),
            pltpu.SemaphoreType.DMA((2,)),
        ] + [pltpu.VMEM((cells + 8, channels), jnp.float32)] * WAYS,
        compiler_params=pltpu.CompilerParams(vmem_limit_bytes=LIMIT),
        name="add_rows",
        cost_estimate=pl.CostEstimate(flops=10**8, bytes_accessed=8 * 10**6, transcendentals=0),
    )(got, base, ends, edges)


LIMIT = 48 * 2**20


def join_taps(w_ref, wide, rows):
    channels = w_ref.shape[-1]
    for r, a in enumerate(rows):
        for d in range(2):
            for par in range(2):
                for c in range(3):
                    at = (((r * 2 + d) * 2 + par) * 3 + c) * channels
                    for s in range(2):
                        b = 2 * d + par - s
                        if 0 <= b <= 2:
                            tile = w_ref[9 * a + 3 * b + c]
                        else:
                            tile = jnp.zeros((channels, channels), jnp.bfloat16)
                        wide[at:at + channels, s * channels:(s + 1) * channels] = tile


def shifts(plane, count, span_z):
    spot = lax.broadcasted_iota(jnp.int32, (count, plane.shape[-1]), 0) % span_z
    middle = plane[8:8 + count, :]
    low = jnp.where(spot == 0, 0.0, plane[7:7 + count, :])
    high = jnp.where(spot == span_z - 1, 0.0, plane[9:9 + count, :])
    return [value.astype(jnp.bfloat16) for value in (low, middle, high)]


def spread_plane(plane, taps, start, half, span_z):
    channels = plane.shape[-1]
    lines = half * span_z
    for c, value in enumerate(shifts(plane, 2 * lines, span_z)):
        value = value.reshape(half, 2, span_z, channels)
        for par in range(2):
            at = (par * 3 + c) * channels
            taps[pl.ds(start, lines), at:at + channels] = value[:, par].reshape(lines, channels)


def residual_kernel(group, level_ref, w_ref, out_ref, ends_ref, edges_ref,
                    plane, taps, wide, result):
    span_x, span_y, span_z, channels = level_ref.shape
    half = (span_y + 2) // 2
    lines = half * span_z
    depth = 6 * channels
    count = (span_y + 2) * span_z
    join_taps(w_ref, wide, (0, 1, 2))
    plane[0:8 + span_z, :] = jnp.zeros((8 + span_z, channels), jnp.float32)
    plane[8 + count - span_z:16 + count, :] = jnp.zeros((8 + span_z, channels), jnp.float32)
    for x in (0, span_x + 1):
        taps[x * lines:(x + 1) * lines, :] = jnp.zeros((lines, depth), jnp.bfloat16)

    def fill(x, carry):
        plane[8 + span_z:8 + count - span_z, :] = level_ref[x].reshape(
            span_y * span_z, channels).astype(jnp.float32)
        spread_plane(plane, taps, pl.multiple_of((x + 1) * lines, 16), half, span_z)
        return carry

    lax.fori_loop(0, span_x, fill, 0)
    height = group * lines - span_z

    def multiply(g, carry):
        total = None
        for a in range(3):
            for d in range(2):
                start = pl.multiple_of((g * group + a) * lines + d * span_z, 16)
                at = (a * 2 + d) * depth
                part = jnp.dot(taps[pl.ds(start, height), :], wide[at:at + depth, :],
                               preferred_element_type=jnp.float32)
                total = part if total is None else total + part
        result[0:height, :] = total
        for i in range(group):
            x = g * group + i
            for s in range(2):
                value = result[i * lines:i * lines + span_y // 2 * span_z,
                               s * channels:(s + 1) * channels]
                value = value.reshape(span_y // 2, span_z, channels)
                edges_ref[s, x] = value[s * (span_y // 2 - 1)]
                if i == 0:
                    @pl.when(g == 0)
                    def _():
                        ends_ref[0, :, s] = value

                if i == group - 1:
                    @pl.when(x == span_x - 1)
                    def _():
                        ends_ref[1, :, s] = value

                here = level_ref[x].reshape(span_y // 2, 2, span_z, channels)[:, s]
                out_ref[x, :, s] = jnp.maximum(value, 0.0) + here.astype(jnp.float32)
        return carry

    lax.fori_loop(0, span_x // group, multiply, 0)


def residual_base(level, w_res, group=4):
    span_x, span_y, span_z, channels = level.shape
    lines = (span_y + 2) // 2 * span_z
    vm = pl.BlockSpec(memory_space=pltpu.VMEM)
    flops = 2 * span_x * span_y * span_z * 27 * channels * channels
    pairs = (span_y // 2, 2, span_z, channels)
    return pl.pallas_call(
        functools.partial(residual_kernel, group),
        out_shape=[
            jax.ShapeDtypeStruct((span_x,) + pairs, jnp.float32),
            jax.ShapeDtypeStruct((2,) + pairs, jnp.float32),
            jax.ShapeDtypeStruct((2, span_x, span_z, channels), jnp.float32),
        ],
        in_specs=[vm] * 2,
        out_specs=[vm] * 3,
        scratch_shapes=[
            pltpu.VMEM(((span_y + 2) * span_z + 16, channels), jnp.float32),
            pltpu.VMEM(((span_x + 2) * lines, 6 * channels), jnp.bfloat16),
            pltpu.VMEM((36 * channels, 2 * channels), jnp.bfloat16),
            pltpu.VMEM((group * lines, 2 * channels), jnp.float32),
        ],
        compiler_params=pltpu.CompilerParams(vmem_limit_bytes=26 * 2**20),
        name="residual",
        cost_estimate=pl.CostEstimate(flops=flops, bytes_accessed=8 * 10**6, transcendentals=0),
    )(level, w_res)


def border_kernel(ends_ref, edges_ref, xfirst_ref, xlast_ref, yfirst_ref, ylast_ref,
                  xlow_ref, xhigh_ref, ylow_ref, yhigh_ref, ll_ref, lh_ref, hl_ref, hh_ref,
                  w_ref, new_ends_ref, new_edges_ref, plane, taps, wide):
    _, half_y, _, span_z, channels = ends_ref.shape
    span_x = edges_ref.shape[1]
    span_y = 2 * half_y
    count = (span_y + 2) * span_z
    depth = 6 * channels
    join_taps(w_ref, wide, (0, 2))
    plane[0:8, :] = jnp.zeros((8, channels), jnp.float32)
    plane[8 + count:16 + count, :] = jnp.zeros((8, channels), jnp.float32)
    for k, (low, middle, high) in enumerate(
            ((ll_ref, xlow_ref, lh_ref), (hl_ref, xhigh_ref, hh_ref))):
        plane[8:8 + span_z, :] = low[...].reshape(span_z, channels).astype(jnp.float32)
        plane[8 + span_z:8 + count - span_z, :] = middle[...].reshape(
            span_y * span_z, channels).astype(jnp.float32)
        plane[8 + count - span_z:8 + count, :] = high[...].reshape(
            span_z, channels).astype(jnp.float32)
        spread_plane(plane, taps, 0, half_y + 1, span_z)
        change = None
        for d in range(2):
            at = (k * 2 + d) * depth
            part = jnp.dot(taps[d * span_z:(d + half_y) * span_z, :], wide[at:at + depth, :],
                           preferred_element_type=jnp.float32)
            change = part if change is None else change + part
        for s in range(2):
            value = change[:, s * channels:(s + 1) * channels].reshape(
                half_y, span_z, channels)
            new_ends_ref[k, :, s] = ends_ref[k, :, s] + value
    rows = (span_x + 2) * span_z
    for k, (source, here) in enumerate(((ylow_ref, yfirst_ref), (yhigh_ref, ylast_ref))):
        plane[8:8 + span_z, :] = jnp.zeros((span_z, channels), jnp.float32)
        plane[8 + span_z:8 + rows - span_z, :] = source[...].reshape(
            span_x * span_z, channels).astype(jnp.float32)
        plane[8 + rows - span_z:16 + rows, :] = jnp.zeros((span_z + 8, channels), jnp.float32)
        for c, value in enumerate(shifts(plane, rows, span_z)):
            taps[0:rows, c * channels:(c + 1) * channels] = value
        change = None
        for a in range(3):
            first = 9 * a + 3 * (2 * k)
            part = jnp.dot(taps[a * span_z:(a + span_x) * span_z, 0:3 * channels],
                           w_ref[first:first + 3].reshape(3 * channels, channels),
                           preferred_element_type=jnp.float32)
            change = part if change is None else change + part
        change = change.reshape(span_x, span_z, channels)
        new_edges_ref[k] = jnp.maximum(edges_ref[k] + change, 0.0) + here[...].reshape(
            span_x, span_z, channels).astype(jnp.float32)
        for e, x in ((0, 0), (1, span_x - 1)):
            new_ends_ref[e, k * (half_y - 1), k] = new_ends_ref[e, k * (half_y - 1), k] + change[x]
    for e, here in enumerate((xfirst_ref, xlast_ref)):
        new_ends_ref[e] = jnp.maximum(new_ends_ref[e], 0.0) + here[...].reshape(
            half_y, 2, span_z, channels).astype(jnp.float32)


def border(ends, edges, own, faces, w_res):
    _, half_y, _, span_z, channels = ends.shape
    span_x = edges.shape[1]
    rows = max((half_y + 1), (span_x + 2)) * span_z
    vm = pl.BlockSpec(memory_space=pltpu.VMEM)
    return pl.pallas_call(
        border_kernel,
        out_shape=[jax.ShapeDtypeStruct(ends.shape, jnp.float32),
                   jax.ShapeDtypeStruct(edges.shape, jnp.float32)],
        in_specs=[vm] * 15,
        out_specs=[vm] * 2,
        scratch_shapes=[
            pltpu.VMEM((2 * rows + 16, channels), jnp.float32),
            pltpu.VMEM((rows, 6 * channels), jnp.bfloat16),
            pltpu.VMEM((24 * channels, 2 * channels), jnp.bfloat16),
        ],
        compiler_params=pltpu.CompilerParams(vmem_limit_bytes=8 * 2**20),
        name="border",
        cost_estimate=pl.CostEstimate(flops=10**9, bytes_accessed=3 * 10**6, transcendentals=0),
    )(ends, edges, *own, *faces, w_res)


def fill_taps(plane, store, zero, half_y, half_z):
    channels = plane.shape[-1]
    span_y = 2 * half_y
    rows = (span_y + 1) * half_z
    low = jnp.where(zero, 0.0, plane[pl.ds(7, rows, stride=2), :])
    for c, value in enumerate((low, plane[pl.ds(8, rows, stride=2), :],
                               plane[pl.ds(9, rows, stride=2), :])):
        value = value.reshape(span_y + 1, half_z, channels)
        evens = value[0:span_y].reshape(half_y, 2, half_z, channels)
        odds = value[1:].reshape(half_y, 2, half_z, channels)
        for b, piece in enumerate((evens[:, 0], evens[:, 1], odds[:, 1])):
            at = (b * 3 + c) * channels
            store(at, piece.reshape(half_y * half_z, channels).astype(jnp.bfloat16))


def taps_kernel(joined_ref, taps_ref, planes):
    span_x, span_y, span_z, channels = joined_ref.shape
    half_y, half_z = span_y // 2, span_z // 2
    count = (span_y + 1) * span_z
    rows = (span_y + 1) * half_z
    zero = lax.broadcasted_iota(jnp.int32, (rows, channels), 0) % half_z == 0
    for k in range(2):
        planes[k, 0:8 + span_z, :] = jnp.zeros((8 + span_z, channels), jnp.float32)
    for x in range(span_x):
        plane = planes.at[x % 2]
        plane[8 + span_z:8 + count, :] = joined_ref[x].reshape(
            span_y * span_z, channels).astype(jnp.float32)

        def store(at, value):
            taps_ref[x % 2, x // 2, :, at:at + channels] = value

        fill_taps(plane, store, zero, half_y, half_z)


def local_taps(joined):
    span_x, span_y, span_z, channels = joined.shape
    vm = pl.BlockSpec(memory_space=pltpu.VMEM)
    return pl.pallas_call(
        taps_kernel,
        out_shape=jax.ShapeDtypeStruct(
            (2, span_x // 2, span_y * span_z // 4, 9 * channels), jnp.bfloat16),
        in_specs=[vm],
        out_specs=vm,
        scratch_shapes=[pltpu.VMEM((2, (span_y + 1) * span_z + 16, channels), jnp.float32)],
        compiler_params=pltpu.CompilerParams(vmem_limit_bytes=8 * 2**20),
        name="local_taps",
        cost_estimate=pl.CostEstimate(flops=10**7, bytes_accessed=7 * 10**6, transcendentals=0),
    )(joined)


GROUPS = 2


def lower_kernel(taps_ref, front_ref, side_ref, corner_ref, w_ref, out_ref, plane, front_taps,
                 side_taps):
    _, span_y, span_z, channels = front_ref.shape
    span_x = side_ref.shape[0]
    half_x, half_y, half_z = span_x // 2, span_y // 2, span_z // 2
    count = (span_y + 1) * span_z
    rows = (span_y + 1) * half_z
    depth = 9 * channels
    wide = w_ref.shape[-1]
    zero = lax.broadcasted_iota(jnp.int32, (rows, channels), 0) % half_z == 0
    plane[0:8, :] = jnp.zeros((8, channels), jnp.float32)
    plane[8:8 + span_x * span_z, :] = side_ref[...].reshape(
        span_x * span_z, channels).astype(jnp.float32)
    lines = span_x * half_z
    low = jnp.where(zero[0:lines], 0.0, plane[pl.ds(7, lines, stride=2), :])
    for c, value in enumerate((low, plane[pl.ds(8, lines, stride=2), :],
                               plane[pl.ds(9, lines, stride=2), :])):
        value = value.reshape(half_x, 2, half_z, channels)
        even = value[:, 0].reshape(half_x * half_z, channels)
        odd = value[:, 1].reshape(half_x * half_z, channels)
        before = jnp.concatenate(
            [jnp.zeros((half_z, channels), jnp.float32), odd[:(half_x - 1) * half_z]], axis=0)
        for a, piece in enumerate((before, even, odd)):
            side_taps[a, :, c * channels:(c + 1) * channels] = piece.astype(jnp.bfloat16)
    change = None
    for a in range(3):
        part = jnp.dot(side_taps[a], w_ref[a * depth:a * depth + 3 * channels, :],
                       preferred_element_type=jnp.float32)
        change = part if change is None else change + part
    change = change.reshape(half_x, half_z, wide)
    plane[8:8 + span_z, :] = corner_ref[...].reshape(span_z, channels).astype(jnp.float32)
    plane[8 + span_z:8 + count, :] = front_ref[...].reshape(
        span_y * span_z, channels).astype(jnp.float32)

    def store(at, value):
        front_taps[:, at:at + channels] = value

    fill_taps(plane, store, zero, half_y, half_z)
    lines = half_y * half_z
    group = half_x // GROUPS

    def product(piece, a):
        return jnp.dot(piece.reshape(-1, depth), w_ref[a * depth:(a + 1) * depth, :],
                       preferred_element_type=jnp.float32)

    for g in range(GROUPS):
        first = g * group
        total = (product(taps_ref[0, first:first + group], 1)
                 + product(taps_ref[1, first:first + group], 2))
        if g == 0:
            total = total + jnp.concatenate(
                [product(front_taps[...], 0), product(taps_ref[1, 0:group - 1], 0)], axis=0)
        else:
            total = total + product(taps_ref[1, first - 1:first + group - 1], 0)
        total = total.reshape(group, half_y, half_z, wide)
        out_ref[first:first + group, 1:] = total[:, 1:].astype(jnp.bfloat16)
        out_ref[first:first + group, 0] = (
            total[:, 0] + change[first:first + group]).astype(jnp.bfloat16)


def lower(taps, front, side, corner, w_down):
    span_x = side.shape[0]
    _, span_y, span_z, channels = front.shape
    wide = w_down.shape[-1]
    vm = pl.BlockSpec(memory_space=pltpu.VMEM)
    flops = 2 * span_x * span_y * span_z // 8 * 27 * channels * wide
    return pl.pallas_call(
        lower_kernel,
        out_shape=jax.ShapeDtypeStruct((span_x // 2, span_y // 2, span_z // 2, wide),
                                       jnp.bfloat16),
        in_specs=[vm] * 5,
        out_specs=vm,
        scratch_shapes=[
            pltpu.VMEM((max(span_y + 1, span_x) * span_z + 16, channels), jnp.float32),
            pltpu.VMEM((span_y * span_z // 4, 9 * channels), jnp.bfloat16),
            pltpu.VMEM((3, span_x * span_z // 4, 3 * channels), jnp.bfloat16),
        ],
        compiler_params=pltpu.CompilerParams(vmem_limit_bytes=28 * 2**20),
        name="lower",
        cost_estimate=pl.CostEstimate(flops=flops, bytes_accessed=5 * 10**6, transcendentals=0),
    )(taps, front, side, corner, w_down.reshape(-1, wide))


def shifted(array, by_pts, by_nbr):
    count_pts = lax.axis_size("pts")
    count_nbr = lax.axis_size("nbr")
    pairs = [
        (i * count_nbr + j, (i + by_pts) * count_nbr + j + by_nbr)
        for i in range(count_pts)
        for j in range(count_nbr)
        if 0 <= i + by_pts < count_pts and 0 <= j + by_nbr < count_nbr
    ]
    return lax.ppermute(array, ("pts", "nbr"), pairs)


def exchanged(array, devices):
    got = lax.all_to_all(
        array.reshape(devices, -1, array.shape[-1]),
        ("pts", "nbr"),
        split_axis=0,
        concat_axis=0,
        tiled=True,
    )
    return got.reshape(array.shape)


def body(points, dest_owner, dest_cell, level_input, w_res, w_down):
    devices = lax.axis_size("pts") * lax.axis_size("nbr")
    channels = points.shape[-1]
    rows = points.reshape(-1, channels)
    capacity = 2 * rows.shape[0] // devices
    outgoing = pack(dest_owner.reshape(-1), dest_cell.reshape(-1), rows, devices, capacity)
    outgoing, level = lax.optimization_barrier((outgoing, level_input))
    got = exchanged(outgoing, devices)
    x_first, x_last = level[:1], level[-1:]
    y_first, y_last = level[:, :1], level[:, -1:]
    faces = [
        shifted(x_last, 0, 1),
        shifted(x_first, 0, -1),
        shifted(y_last, 1, 0),
        shifted(y_first, -1, 0),
        shifted(level[-1:, -1:], 1, 1),
        shifted(level[-1:, :1], -1, 1),
        shifted(level[:1, -1:], 1, -1),
        shifted(level[:1, :1], -1, -1),
    ]
    base, ends, edges = residual_base(level, w_res)
    ends, edges = border(ends, edges, (x_first, x_last, y_first, y_last), faces, w_res)
    joined, front, side, corner = add_rows(
        got, base.reshape(-1, channels), ends, edges, level.shape, capacity)
    front = shifted(front, 0, 1)
    side = shifted(side, 1, 0)
    corner = shifted(corner, 1, 1)
    return lower(local_taps(joined), front, side, corner, w_down)


def solution(mesh):
    return jax.shard_map(
        body,
        mesh=mesh,
        in_specs=(
            P("pts", "nbr", None, None),
            P("pts", "nbr", None, None),
            P("pts", "nbr", None),
            P("nbr", "pts", None, None),
            P(),
            P(),
        ),
        out_specs=P("nbr", "pts", None, None),
        check_vma=False,
    )
```
